32 devices in a mesh: wide: 8 (over z, x), narrow: 4 (over y, core).
Axes of the slice: x: 2, y: 2, z: 4, core: 2. Of those that a mesh axis runs over, the one named last changes fastest.
Arguments:
- flow_field: bfloat16 [64, 64, 16, 512], P('wide', 'narrow'), may hold values from -48 to 48
- fluid_mask: int32 [64, 64, 16], P('wide', 'narrow'), may hold values 0 or 1
- conv_weight: float32 [27, 512], replicated, may hold values from -1 to 1
- latents: bfloat16 [1024, 512], replicated, may hold values from -6 to 6
- w_query1: bfloat16 [512, 512], replicated, may hold values from -0.25 to 0.25
- w_key1: bfloat16 [512, 512], replicated, may hold values from -0.25 to 0.25
- w_value1: bfloat16 [512, 512], replicated, may hold values from -0.25 to 0.25
- w_out1: bfloat16 [512, 512], replicated, may hold values from -0.25 to 0.25
- w_query2: bfloat16 [512, 512], replicated, may hold values from -0.25 to 0.25
- w_key2: bfloat16 [512, 512], replicated, may hold values from -0.25 to 0.25
- w_value2: bfloat16 [512, 512], replicated, may hold values from -0.25 to 0.25
- w_out2: bfloat16 [512, 512], replicated, may hold values from -0.25 to 0.25
Outputs:
- updated_field: float32 [64, 64, 16, 512], P('wide', 'narrow')
The draws below stay inside these ranges and needn't reach their ends.
All inputs are finite; a program needn't handle non-finite values. No bound on the sum of `fluid_mask` on one device may be relied on, other than what follows from the above.
Results may differ from the reference program's by a relative error of at most 0.035.
The reference program's roundings to bfloat16 on the way count: a program that leaves them out, or rounds other values in their place, can miss the bound.
Values may be sent and summed in bfloat16 or wider, within the bound.
No kernel may reach another device: no remote copies, remote signals or barrier semaphores. Data moves between devices by JAX's collectives and lax.ppermute only.
A program may use at most 192 MiB of HBM per device.

```python
import math
import jax
import jax.numpy as jnp
from jax import lax

D = 512
HEADS = 8
HEAD_DIM = 64
LATENTS = 1024
NX = 64
NY = 64
NZ = 16


def draw_flow_field(key, part):
    base_key = jax.random.fold_in(jax.random.fold_in(key, 11), 0)
    grid_shape = (NX, NY, NZ, D)
    values = jnp.clip(jax.random.normal(base_key, grid_shape, jnp.float32), -6.0, 6.0)
    return values.astype(jnp.bfloat16)


def draw_latents(key, part):
    entry_key = jax.random.fold_in(jax.random.fold_in(key, 23), 0)
    latent_shape = (LATENTS, D)
    values = jnp.clip(jax.random.normal(entry_key, latent_shape, jnp.float32), -6.0, 6.0)
    return values.astype(jnp.bfloat16)


def set_ends(values, stream_key, smallest, high):
    longest = values.shape.index(max(values.shape))
    spots = []
    for shift in (0, 1):
        where = [jax.random.randint(jax.random.fold_in(stream_key, axis), (), 0, length) for axis, length in enumerate(values.shape)]
        where[longest] = (where[longest] + shift) % values.shape[longest]
        spots.append(tuple(where))
    return values.at[spots[0]].set(smallest).at[spots[1]].set(high)


def centred(rng, extent, spread, limit, dtype=jnp.bfloat16):
    return jnp.clip(spread * jax.random.normal(rng, extent, jnp.float32), -limit, limit).astype(dtype)


def setup_inputs(seed: int = 0) -> dict:
    keys = jax.random.split(jax.random.key(seed), 13)
    flow_field = draw_flow_field(jax.random.fold_in(keys[12], 71), 0)
    fluid_mask = set_ends((jax.random.randint(keys[1], (NX, NY, NZ), 0, 8) < 7).astype(jnp.int32), jax.random.fold_in(keys[1], 1), 0, 1)
    conv_weight = centred(keys[2], (27, D), 0.2, 1.0, jnp.float32)
    latents = draw_latents(jax.random.fold_in(keys[12], 71), 0)
    w_query1 = centred(keys[4], (D, D), D ** -0.5, 0.25)
    w_key1 = centred(keys[5], (D, D), D ** -0.5, 0.25)
    w_value1 = centred(keys[6], (D, D), D ** -0.5, 0.25)
    w_out1 = centred(keys[7], (D, D), D ** -0.5, 0.25)
    w_query2 = centred(keys[8], (D, D), D ** -0.5, 0.25)
    w_key2 = centred(keys[9], (D, D), D ** -0.5, 0.25)
    w_value2 = centred(keys[10], (D, D), D ** -0.5, 0.25)
    w_out2 = centred(keys[11], (D, D), D ** -0.5, 0.25)
    return {"flow_field": flow_field, "fluid_mask": fluid_mask, "conv_weight": conv_weight, "latents": latents, "w_query1": w_query1, "w_key1": w_key1, "w_value1": w_value1, "w_out1": w_out1, "w_query2": w_query2, "w_key2": w_key2, "w_value2": w_value2, "w_out2": w_out2}


def project(row_block, weight):
    return jnp.dot(row_block, weight, preferred_element_type=jnp.float32).astype(jnp.bfloat16)

def heads_first(matrix):
    return matrix.reshape(matrix.shape[0], HEADS, HEAD_DIM).transpose(1, 0, 2)

def score_block(head_queries, head_keys):
    factor = 1.8 / math.sqrt(HEAD_DIM)
    return factor * lax.dot_general(head_queries, head_keys, (((1,), (1,)), ((), ())), preferred_element_type=jnp.float32)

def attend_exact(operands):
    head_queries, head_keys, head_values = operands
    scores = score_block(head_queries, head_keys)
    top_score = lax.optimization_barrier(jnp.max(scores, axis=1, keepdims=True))
    weights = jnp.exp(scores - top_score)
    totals = lax.optimization_barrier(jnp.sum(weights, axis=1, keepdims=True))
    summed = jnp.dot(weights, head_values.astype(jnp.float32), precision=lax.Precision.HIGHEST, preferred_element_type=jnp.float32)
    return summed / totals

def attend_rounded(operands):
    head_queries, head_keys, head_values = operands
    scores = score_block(head_queries, head_keys)
    top_score = lax.optimization_barrier(jnp.max(scores, axis=1, keepdims=True))
    weights = jnp.exp(scores - top_score)
    totals = lax.optimization_barrier(jnp.sum(weights, axis=1, keepdims=True))
    summed = jnp.dot(weights.astype(jnp.bfloat16), head_values, preferred_element_type=jnp.float32)
    return summed / totals

def heads_last(stacked):
    return stacked.transpose(1, 0, 2).reshape(stacked.shape[1], D).astype(jnp.bfloat16)

def reference(flow_field, fluid_mask, conv_weight, latents, w_query1, w_key1, w_value1, w_out1, w_query2, w_key2, w_value2, w_out2):
    masked = flow_field * fluid_mask[:, :, :, None].astype(jnp.bfloat16)
    padded = jnp.pad(masked, ((1, 1), (1, 1), (1, 1), (0, 0)))
    stencil = masked.astype(jnp.float32)
    for offset_x in range(3):
        for offset_y in range(3):
            for offset_z in range(3):
                window = padded[offset_x:offset_x + NX, offset_y:offset_y + NY, offset_z:offset_z + NZ]
                stencil = stencil + window.astype(jnp.float32) * conv_weight[9 * offset_x + 3 * offset_y + offset_z]
    mixed_cells = stencil.astype(jnp.bfloat16).reshape(NX * NY * NZ, D)
    keys1 = project(mixed_cells, w_key1)
    values1 = project(mixed_cells, w_value1)
    queries1 = project(latents, w_query1)
    read1 = heads_last(lax.map(attend_exact, (heads_first(queries1), heads_first(keys1), heads_first(values1))))
    latent_state = (latents.astype(jnp.float32) + jnp.dot(read1, w_out1, preferred_element_type=jnp.float32)).astype(jnp.bfloat16)
    keys2 = project(latent_state, w_key2)
    values2 = project(latent_state, w_value2)
    queries2 = project(mixed_cells, w_query2)
    read2 = heads_last(lax.map(attend_rounded, (heads_first(queries2), heads_first(keys2), heads_first(values2))))
    flat_masked = masked.reshape(NX * NY * NZ, D)
    result = flat_masked.astype(jnp.float32) + jnp.dot(read2, w_out2, preferred_element_type=jnp.float32)
    return result.reshape(NX, NY, NZ, D)
```

```python
import functools
import math

import jax
import jax.numpy as jnp
from jax import lax
from jax.experimental import pallas as pl
from jax.experimental.pallas import tpu as pltpu
from jax.sharding import Mesh, PartitionSpec as P

HEADS = 8
LANES = 128
ONES_ROWS = 16
VMEM_BYTES = 60 << 20
F32 = jnp.float32
BF16 = jnp.bfloat16


def dot(left, right, contract=((1,), (0,))):
    return lax.dot_general(left, right, (contract, ((), ())), preferred_element_type=F32)


def fill_padded(padded, masked, x_lo, x_hi, y_lo, y_hi, c_lo, c_hi):
    size_x, size_y = masked.shape[:2]

    def plane(i, carry):
        padded[i + 1, 1 : size_y + 1] = masked[i].astype(F32)
        padded[i + 1, 0] = y_lo[i].astype(F32)
        padded[i + 1, size_y + 1] = y_hi[i].astype(F32)
        return carry

    lax.fori_loop(0, size_x, plane, 0)
    for row, face in ((0, x_lo), (size_x + 1, x_hi)):
        padded[row, 1 : size_y + 1] = face[...].astype(F32)
    for end, row in ((0, 0), (1, size_x + 1)):
        padded[row, 0] = c_lo[end].astype(F32)
        padded[row, size_y + 1] = c_hi[end].astype(F32)


def stencil_plane(i, padded, conv, mixed, size_y, size_z):
    width = padded.shape[-1]
    row_of = lax.broadcasted_iota(jnp.int32, (size_z, LANES), 0)
    for tile in range(width // LANES):
        lanes = slice(tile * LANES, (tile + 1) * LANES)
        taps = [jnp.broadcast_to(conv[n : n + 1, lanes], (size_z, LANES)) for n in range(27)]
        for j in range(size_y):
            sums = [None] * 3
            for a in range(3):
                for b in range(3):
                    window = padded[i + a, j + b, :, lanes]
                    for c in range(3):
                        term = window * taps[9 * a + 3 * b + c]
                        sums[c] = term if sums[c] is None else sums[c] + term
            below = jnp.where(row_of == 0, 0.0, pltpu.roll(sums[0], 1, 0))
            above = jnp.where(row_of == size_z - 1, 0.0, pltpu.roll(sums[2], size_z - 1, 0))
            total = padded[i + 1, j + 1, :, lanes] + sums[1] + below + above
            start = pl.multiple_of((i * size_y + j) * size_z, size_z)
            mixed[pl.ds(start, size_z), lanes] = total.astype(BF16)


def score_weights(query_t, head_in_pair, head_size):
    factor = 1.8 / math.sqrt(head_size) * math.log2(math.e)
    scaled = query_t.astype(F32) * factor
    high = scaled.astype(BF16)
    low = (scaled - high.astype(F32)).astype(BF16)
    blank = jnp.zeros_like(high)
    if head_in_pair == 0:
        return jnp.concatenate([high, blank, low, blank], axis=0)
    return jnp.concatenate([blank, high, blank, low], axis=0)


def attention_scores(pair, head_in_pair, block, width, chunk, keys, query_t, scores):
    head_size = LANES // 2
    start = pl.multiple_of(pair * LANES, LANES) + head_in_pair * head_size
    columns = pl.ds(pl.multiple_of(block * width, width), width)
    right = score_weights(query_t[pl.ds(start, head_size), columns], head_in_pair, head_size)
    top = None
    for part in range(keys.shape[0] // chunk):
        rows = pl.ds(part * chunk, chunk)
        left = keys[rows, pl.ds(pl.multiple_of(pair * LANES, LANES), LANES)]
        piece = dot(jnp.concatenate([left, left], axis=1), right)
        scores[head_in_pair, rows, :] = piece
        largest = jnp.max(piece.reshape(chunk // 8, 8, width), axis=0)
        top = largest if top is None else jnp.maximum(top, largest)
    return jnp.max(top, axis=0, keepdims=True)


def attention_sums(head, head_in_pair, chunk, values_t, scores, top):
    total = None
    for part in range(scores.shape[1] // chunk):
        rows = pl.ds(part * chunk, chunk)
        weights = jnp.exp2(scores[head_in_pair, rows, :] - top).astype(BF16)
        piece = dot(values_t[head, :, rows], weights)
        total = piece if total is None else total + piece
    return total


def attention_loop(keys, query_t, values_t, scores, chunk, finish):
    width = scores.shape[2]
    blocks = query_t.shape[1] // width
    pairs = query_t.shape[0] // LANES
    steps = pairs * blocks

    def first(t):
        return attention_scores(t % pairs, 0, t // pairs, width, chunk, keys, query_t, scores)

    def step(t, top_even):
        pair, block = t % pairs, t // pairs
        top_odd = attention_scores(pair, 1, block, width, chunk, keys, query_t, scores)
        even = attention_sums(2 * pair, 0, chunk, values_t, scores, top_even)
        following = first(jnp.minimum(t + 1, steps - 1))
        odd = attention_sums(2 * pair + 1, 1, chunk, values_t, scores, top_odd)
        finish(pair, block, (even, odd), (top_even, top_odd))
        return following

    lax.fori_loop(0, steps, step, first(0))


def split3(value):
    high = value.astype(BF16).astype(F32)
    rest = value - high
    middle = rest.astype(BF16).astype(F32)
    return high, middle, rest - middle


def read_kernel(
    masked,
    x_lo,
    x_hi,
    y_lo,
    y_hi,
    c_lo,
    c_hi,
    conv,
    latents,
    w_query1,
    w_key1,
    w_value1,
    w_query2,
    query2_t,
    packed,
    padded,
    mixed,
    keys,
    values_t,
    query1_t,
    scores,
    stats,
):
    size_x, size_y, size_z, width = masked.shape
    head_size = width // HEADS
    fill_padded(padded, masked, x_lo, x_hi, y_lo, y_hi, c_lo, c_hi)

    def plane(i, carry):
        stencil_plane(i, padded, conv, mixed, size_y, size_z)
        return carry

    lax.fori_loop(0, size_x, plane, 0)

    cells = size_y * size_z
    lower = ((0,), (1,))
    values_t[:, head_size:, :] = jnp.ones_like(values_t[:, head_size:, :])

    def projections(i, carry):
        rows = pl.ds(pl.multiple_of(i * cells, cells), cells)
        block = mixed[rows, :]
        keys[rows, :] = dot(block, w_key1[...]).astype(BF16)
        value_t = dot(w_value1[...], block, lower).astype(BF16)
        values_t[:, :head_size, rows] = value_t.reshape(HEADS, head_size, cells)
        query2_t[:, rows] = dot(w_query2[...], block, lower).astype(BF16)
        return carry

    lax.fori_loop(0, size_x, projections, 0)
    query1_t[...] = dot(w_query1[...], latents[...], lower).astype(BF16)
    stats[...] = jnp.zeros_like(stats)

    def finish(pair, block, sums, tops):
        columns = pl.ds(pl.multiple_of(block * scores.shape[2], LANES), scores.shape[2])
        both = jnp.concatenate([part[:head_size] for part in sums], axis=0)
        lanes = pl.ds(pl.multiple_of(pair * LANES, LANES), LANES)
        packed[columns, lanes] = both.T.astype(BF16)
        for head_in_pair in range(2):
            rows = split3(tops[head_in_pair]) + split3(sums[head_in_pair][head_size : head_size + 1])[:2]
            for slot, row in enumerate(rows):
                stats[pl.ds(slot * HEADS + 2 * pair + head_in_pair, 1), columns] = row

    attention_loop(keys, query1_t, values_t, scores, 256, finish)
    packed[:, width:] = stats[...].T.astype(BF16)


def unpack_stats(tile):
    parts = [tile] + [pltpu.roll(tile, LANES - slot * HEADS, 1) for slot in range(1, 5)]
    return parts[0] + parts[1] + parts[2], parts[3] + parts[4]


def pack_stats(top, total):
    lane = lax.broadcasted_iota(jnp.int32, top.shape, 1)
    tile = jnp.zeros_like(top)
    for slot, value in enumerate(split3(top) + split3(total)[:2]):
        moved = pltpu.roll(value, slot * HEADS, 1) if slot else value
        tile = jnp.where((lane >= slot * HEADS) & (lane < (slot + 1) * HEADS), moved, tile)
    return tile


def spread(per_head, pair):
    rows = per_head.shape[0]
    lane = lax.broadcasted_iota(jnp.int32, (rows, LANES), 1)
    left = jnp.broadcast_to(per_head[:, 2 * pair : 2 * pair + 1], (rows, LANES))
    right = jnp.broadcast_to(per_head[:, 2 * pair + 1 : 2 * pair + 2], (rows, LANES))
    return jnp.where(lane < LANES // 2, left, right)


def merge_parts(loads, width):
    stats = [unpack_stats(load(slice(width, width + LANES))) for load in loads]
    top = functools.reduce(jnp.maximum, [t for t, _ in stats])
    factors = [jnp.exp2(t - top) for t, _ in stats]
    total = sum(f * l for f, (_, l) in zip(factors, stats))
    sums = []
    for pair in range(width // LANES):
        lanes = slice(pair * LANES, (pair + 1) * LANES)
        sums.append(sum(load(lanes) * spread(f, pair) for load, f in zip(loads, factors)))
    return sums, top, total


def merge_two_kernel(left, right, out):
    rows, full = left.shape
    width = full - LANES
    step = min(rows, 64)

    def body(r, carry):
        span = pl.ds(pl.multiple_of(r * step, step), step)
        loads = [lambda lanes, ref=ref: ref[span, lanes].astype(F32) for ref in (left, right)]
        sums, top, total = merge_parts(loads, width)
        for pair, value in enumerate(sums):
            out[span, pair * LANES : (pair + 1) * LANES] = value.astype(BF16)
        out[span, width:] = pack_stats(top, total).astype(BF16)
        return carry

    lax.fori_loop(0, rows // step, body, 0)


def update_kernel(parts, own, w_out1, out):
    count, rows, full = parts.shape
    width = full - LANES
    loads = [lambda lanes, g=g: parts[g, :, lanes].astype(F32) for g in range(count)]
    sums, _, total = merge_parts(loads, width)
    read = [value / spread(total, pair) for pair, value in enumerate(sums)]
    read = jnp.concatenate(read, axis=1).astype(BF16)
    out[...] = (own[...].astype(F32) + dot(read, w_out1[...])).astype(BF16)


def write_kernel(state, query2_t, masked, w_key2, w_value2, w_out2, out, keys, values_t, scores, read_t):
    width = state.shape[1]
    head_size = width // HEADS
    values_t[:, head_size:, :] = jnp.ones_like(values_t[:, head_size:, :])
    keys[...] = dot(state[...], w_key2[...]).astype(BF16)
    value_t = dot(w_value2[...], state[...], ((0,), (1,))).astype(BF16)
    values_t[:, :head_size, :] = value_t.reshape(HEADS, head_size, state.shape[0])
    span = scores.shape[2]

    def finish(pair, block, sums, tops):
        columns = pl.ds(pl.multiple_of(block * span, span), span)
        both = [part[:head_size] / part[head_size : head_size + 1] for part in sums]
        rows = pl.ds(pl.multiple_of(pair * LANES, LANES), LANES)
        read_t[rows, columns] = jnp.concatenate(both, axis=0).astype(BF16)

    attention_loop(keys, query2_t, values_t, scores, 256, finish)

    def emit(r, carry):
        rows = pl.ds(pl.multiple_of(r * span, span), span)
        change = dot(read_t[:, rows], w_out2[...], ((0,), (0,)))
        out[rows, :] = masked[rows, :].astype(F32) + change
        return carry

    lax.fori_loop(0, out.shape[0] // span, emit, 0)


def call(kernel, shapes, scratch, *operands):
    vmem = pl.BlockSpec(memory_space=pltpu.VMEM)
    many = isinstance(shapes, (list, tuple))
    return pl.pallas_call(
        kernel,
        out_shape=shapes,
        in_specs=[vmem] * len(operands),
        out_specs=[vmem] * len(shapes) if many else vmem,
        scratch_shapes=scratch,
        compiler_params=pltpu.CompilerParams(vmem_limit_bytes=VMEM_BYTES),
    )(*operands)


def exchange(low, high, axis):
    count = lax.axis_size(axis)
    up = [(i, i + 1) for i in range(count - 1)]
    down = [(i + 1, i) for i in range(count - 1)]
    return lax.ppermute(high, axis, up), lax.ppermute(low, axis, down)


def flipped(array, axis, distance):
    return lax.ppermute(array, axis, [(i, i ^ distance) for i in range(lax.axis_size(axis))])


def per_device(
    flow_field,
    fluid_mask,
    conv_weight,
    latents,
    w_query1,
    w_key1,
    w_value1,
    w_out1,
    w_query2,
    w_key2,
    w_value2,
    w_out2,
):
    size_x, size_y, size_z, width = flow_field.shape
    head_size = width // HEADS
    cells = size_x * size_y * size_z
    latent_count = latents.shape[0]
    narrow = ("ny", "nc")
    shape = jax.ShapeDtypeStruct
    masked = flow_field * fluid_mask[:, :, :, None].astype(BF16)

    x_lo, x_hi = exchange(masked[0], masked[-1], "wide")
    y_lo, y_hi = exchange(masked[:, 0], masked[:, -1], narrow)
    ends = jnp.stack([x_lo, x_hi])
    c_lo, c_hi = exchange(ends[:, 0], ends[:, -1], narrow)

    query2_t, packed = call(
        read_kernel,
        [shape((width, cells), BF16), shape((latent_count, width + LANES), BF16)],
        [
            pltpu.VMEM((size_x + 2, size_y + 2, size_z, width), F32),
            pltpu.VMEM((cells, width), BF16),
            pltpu.VMEM((cells, width), BF16),
            pltpu.VMEM((HEADS, head_size + ONES_ROWS, cells), BF16),
            pltpu.VMEM((width, latent_count), BF16),
            pltpu.VMEM((2, cells, 256), F32),
            pltpu.VMEM((LANES, latent_count), F32),
        ],
        masked,
        x_lo,
        x_hi,
        y_lo,
        y_hi,
        c_lo,
        c_hi,
        conv_weight,
        latents,
        w_query1,
        w_key1,
        w_value1,
        w_query2,
    )

    half = latent_count // 2
    core = lax.axis_index("nc")
    halves = packed.reshape(2, half, width + LANES)
    kept = lax.dynamic_index_in_dim(halves, core, 0, keepdims=False)
    given = lax.dynamic_index_in_dim(halves, 1 - core, 0, keepdims=False)
    taken = flipped(given, "nc", 1)
    merged = call(merge_two_kernel, shape((half, width + LANES), BF16), [], kept, taken)
    groups = lax.axis_size("wide") * lax.axis_size("ny")
    rows = half // groups
    parts = lax.all_to_all(
        merged.reshape(groups, rows, width + LANES), ("wide", "ny"), split_axis=0, concat_axis=0, tiled=True
    )
    group = lax.axis_index("wide") * lax.axis_size("ny") + lax.axis_index("ny")
    own = lax.dynamic_slice_in_dim(latents, core * half + group * rows, rows, 0)
    state = call(update_kernel, shape((rows, width), BF16), [], parts, own, w_out1)

    distance = lax.axis_size("wide") // 2
    while distance:
        state = jnp.concatenate([state, flipped(state, "wide", distance)], axis=0)
        distance //= 2
    for axis in narrow:
        state = jnp.concatenate([state, flipped(state, axis, 1)], axis=0)

    result = call(
        write_kernel,
        shape((cells, width), F32),
        [
            pltpu.VMEM((latent_count, width), BF16),
            pltpu.VMEM((HEADS, head_size + ONES_ROWS, latent_count), BF16),
            pltpu.VMEM((2, latent_count, 512), F32),
            pltpu.VMEM((width, cells), BF16),
        ],
        state,
        query2_t,
        masked.reshape(cells, width),
        w_key2,
        w_value2,
        w_out2,
    )
    return result.reshape(size_x, size_y, size_z, width)


def solution(mesh):
    wide, narrow = (mesh.shape[name] for name in ("wide", "narrow"))
    grid = Mesh(mesh.devices.reshape(wide, narrow // 2, 2), ("wide", "ny", "nc"))
    split = ("ny", "nc")
    return jax.shard_map(
        per_device,
        mesh=grid,
        in_specs=(P("wide", split, None, None), P("wide", split, None)) + (P(),) * 10,
        out_specs=P("wide", split, None, None),
        check_vma=False,
    )
```

```python
import functools
import math

import jax
import jax.numpy as jnp
from jax import lax
from jax.experimental import pallas as pl
from jax.experimental.pallas import tpu as pltpu
from jax.sharding import Mesh, PartitionSpec as P

HEADS = 8
LANES = 128
ONES_ROWS = 16
STAT_ROWS = 48
MIB = 1 << 20
F32 = jnp.float32
BF16 = jnp.bfloat16


def dot(left, right, contract=((1,), (0,))):
    return lax.dot_general(left, right, (contract, ((), ())), preferred_element_type=F32)


def fill_row(padded, row, plane, left, right):
    size_y = plane.shape[0]
    padded[row, 1 : size_y + 1] = plane.astype(F32)
    padded[row, 0] = left.astype(F32)
    padded[row, size_y + 1] = right.astype(F32)


def stencil_plane(base, padded, conv, mixed, start):
    size_y, size_z, width = padded.shape[1] - 2, padded.shape[2], padded.shape[3]
    row_of = lax.broadcasted_iota(jnp.int32, (size_z, LANES), 0)
    for tile in range(width // LANES):
        lanes = slice(tile * LANES, (tile + 1) * LANES)
        taps = [jnp.broadcast_to(conv[n : n + 1, lanes], (size_z, LANES)) for n in range(27)]
        for j in range(size_y):
            sums = [None] * 3
            for a in range(3):
                for b in range(3):
                    window = padded[base + a, j + b, :, lanes]
                    for c in range(3):
                        term = window * taps[9 * a + 3 * b + c]
                        sums[c] = term if sums[c] is None else sums[c] + term
            below = jnp.where(row_of == 0, 0.0, pltpu.roll(sums[0], 1, 0))
            above = jnp.where(row_of == size_z - 1, 0.0, pltpu.roll(sums[2], size_z - 1, 0))
            total = padded[base + 1, j + 1, :, lanes] + sums[1] + below + above
            mixed[pl.ds(pl.multiple_of(start + j * size_z, size_z), size_z), lanes] = total.astype(BF16)


def project_plane(start, cells, mixed, w_key1, w_value1, keys, values_t):
    head_size = mixed.shape[1] // HEADS
    rows = pl.ds(pl.multiple_of(start, cells), cells)
    block = mixed[rows, :]
    keys[rows, :] = dot(block, w_key1[...]).astype(BF16)
    value_t = dot(w_value1[...], block, ((0,), (1,))).astype(BF16)
    values_t[:, :head_size, rows] = value_t.reshape(HEADS, head_size, cells)


def inner_kernel(
    masked, y_lo, y_hi, conv, latents, w_query1, w_key1, w_value1, mixed, keys, values_t, query1_t, padded
):
    size_x, size_y, size_z, width = masked.shape
    head_size = width // HEADS
    cells = size_y * size_z

    def fill(i, carry):
        fill_row(padded, i, masked[i], y_lo[i], y_hi[i])
        return carry

    lax.fori_loop(0, size_x, fill, 0)
    query1_t[...] = dot(w_query1[...], latents[...], ((0,), (1,))).astype(BF16)
    values_t[:, head_size:, :] = jnp.ones_like(values_t[:, head_size:, :])
    stencil_plane(0, padded, conv, mixed, 0)

    def plane(i, carry):
        project_plane((i - 1) * cells, cells, mixed, w_key1, w_value1, keys, values_t)
        stencil_plane(i, padded, conv, mixed, i * cells)
        return carry

    lax.fori_loop(1, size_x - 2, plane, 0)
    project_plane((size_x - 3) * cells, cells, mixed, w_key1, w_value1, keys, values_t)


def score_weights(query_t, head_in_pair, head_size):
    factor = 1.8 / math.sqrt(head_size) * math.log2(math.e)
    scaled = query_t.astype(F32) * factor
    high = scaled.astype(BF16)
    low = (scaled - high.astype(F32)).astype(BF16)
    blank = jnp.zeros_like(high)
    if head_in_pair == 0:
        return jnp.concatenate([high, blank, low, blank], axis=0)
    return jnp.concatenate([blank, high, blank, low], axis=0)


def attention_scores(pair, head_in_pair, block, width, chunk, keys, query_t, scores):
    head_size = LANES // 2
    start = pl.multiple_of(pair * LANES, LANES) + head_in_pair * head_size
    columns = pl.ds(pl.multiple_of(block * width, width), width)
    right = score_weights(query_t[pl.ds(start, head_size), columns], head_in_pair, head_size)
    top = None
    base = 0
    for piece in keys:
        for part in range(piece.shape[0] // chunk):
            left = piece[pl.ds(part * chunk, chunk), pl.ds(pl.multiple_of(pair * LANES, LANES), LANES)]
            found = dot(jnp.concatenate([left, left], axis=1), right)
            scores[head_in_pair, pl.ds(base, chunk), :] = found
            base += chunk
            largest = jnp.max(found.reshape(chunk // 8, 8, width), axis=0)
            top = largest if top is None else jnp.maximum(top, largest)
    return jnp.max(top, axis=0, keepdims=True)


def attention_sums(head, head_in_pair, chunk, values_t, scores, top):
    total = None
    base = 0
    for piece in values_t:
        for part in range(piece.shape[2] // chunk):
            weights = jnp.exp2(scores[head_in_pair, pl.ds(base, chunk), :] - top).astype(BF16)
            base += chunk
            found = dot(piece[head, :, pl.ds(part * chunk, chunk)], weights)
            total = found if total is None else total + found
    return total


def attention_loop(keys, query_t, values_t, scores, chunk, finish):
    width = scores.shape[2]
    blocks = query_t.shape[1] // width
    pairs = query_t.shape[0] // LANES
    steps = pairs * blocks

    def first(t):
        return attention_scores(t % pairs, 0, t // pairs, width, chunk, keys, query_t, scores)

    def step(t, top_even):
        pair, block = t % pairs, t // pairs
        top_odd = attention_scores(pair, 1, block, width, chunk, keys, query_t, scores)
        even = attention_sums(2 * pair, 0, chunk, values_t, scores, top_even)
        following = first(jnp.minimum(t + 1, steps - 1))
        odd = attention_sums(2 * pair + 1, 1, chunk, values_t, scores, top_odd)
        finish(pair, block, (even, odd), (top_even, top_odd))
        return following

    lax.fori_loop(0, steps, step, first(0))


def split3(value):
    high = value.astype(BF16).astype(F32)
    rest = value - high
    middle = rest.astype(BF16).astype(F32)
    return high, middle, rest - middle


def stat_rows(top, total):
    return split3(top) + split3(total)[:2]


def read_kernel(
    position,
    masked,
    x_lo,
    x_hi,
    y_lo,
    y_hi,
    c_lo,
    c_hi,
    conv,
    w_key1,
    w_value1,
    inner_keys,
    inner_values_t,
    query1_t,
    mixed,
    kept,
    given,
    padded,
    keys,
    values_t,
    scores,
    stats,
):
    size_x, size_y, size_z, width = masked.shape
    head_size = width // HEADS
    cells = size_y * size_z
    last = size_x - 1
    fill_row(padded, 0, x_lo[...], c_lo[0], c_lo[1])
    fill_row(padded, 1, masked[0], y_lo[0], y_hi[0])
    fill_row(padded, 2, masked[1], y_lo[1], y_hi[1])
    fill_row(padded, 3, masked[last - 1], y_lo[last - 1], y_hi[last - 1])
    fill_row(padded, 4, masked[last], y_lo[last], y_hi[last])
    fill_row(padded, 5, x_hi[...], c_hi[0], c_hi[1])
    values_t[:, head_size:, :] = jnp.ones_like(values_t[:, head_size:, :])
    stats[...] = jnp.zeros_like(stats)

    def plane(i, carry):
        stencil_plane(3 * i, padded, conv, mixed, i * cells)
        project_plane(i * cells, cells, mixed, w_key1, w_value1, keys, values_t)
        return carry

    lax.fori_loop(0, 2, plane, 0)

    core = position[0]
    per_half = kept.shape[0]
    span = scores.shape[2]
    ratio = span // LANES

    def finish(pair, block, sums, tops):
        both = jnp.concatenate([part[:head_size] for part in sums], axis=0).astype(BF16)
        rows = pl.ds(pl.multiple_of(pair * LANES, LANES), LANES)
        first = block * ratio
        side = first // per_half

        def write(target):
            for k in range(ratio):
                target[first - side * per_half + k, rows, :] = both[:, k * LANES : (k + 1) * LANES]

        pl.when(side == core)(lambda: write(kept))
        pl.when(side != core)(lambda: write(given))
        columns = pl.ds(pl.multiple_of(block * span, span), span)
        for head_in_pair in range(2):
            values = stat_rows(tops[head_in_pair], sums[head_in_pair][head_size : head_size + 1])
            for slot, row in enumerate(values):
                stats[pl.ds(slot * HEADS + 2 * pair + head_in_pair, 1), columns] = row

    attention_loop([inner_keys, keys], query1_t, [inner_values_t, values_t], scores, 256, finish)
    for target, side in ((kept, core), (given, 1 - core)):
        for k in range(per_half):
            columns = pl.ds(pl.multiple_of((side * per_half + k) * LANES, LANES), LANES)
            target[k, width:, :] = stats[:, columns].astype(BF16)


def merge_blocks(blocks):
    width = blocks[0].shape[0] - STAT_ROWS
    head_size = width // HEADS
    slots = [[block[width + n * HEADS : width + (n + 1) * HEADS] for n in range(5)] for block in blocks]
    tops = [s[0] + s[1] + s[2] for s in slots]
    top = functools.reduce(jnp.maximum, tops)
    factors = [jnp.exp2(t - top) for t in tops]
    total = sum(f * (s[3] + s[4]) for f, s in zip(factors, slots))
    sums = []
    for head in range(HEADS):
        rows = slice(head * head_size, (head + 1) * head_size)
        sums.append(sum(block[rows] * f[head : head + 1] for block, f in zip(blocks, factors)))
    return sums, top, total


def all_stats(top, total, size):
    rows = list(stat_rows(top, total))
    filler = jnp.zeros((size - len(rows) * HEADS,) + top.shape[1:], F32)
    return jnp.concatenate(rows + [filler], axis=0)


def merge_pair_kernel(position, kept, taken, *outs):
    for distance, out in enumerate(outs):
        index = position[1] ^ distance
        sums, top, total = merge_blocks([ref[index].astype(F32) for ref in (kept, taken)])
        sums.append(all_stats(top, total, STAT_ROWS))
        out[...] = jnp.concatenate(sums, axis=0).astype(BF16)


def merge_group_kernel(count, position, *refs):
    blocks, outs, turned = refs[:count], refs[count:-1], refs[-1]
    sums, top, total = merge_blocks([ref[...].astype(F32) for ref in blocks])
    width = turned.shape[1] - LANES
    sums = jnp.concatenate(sums, axis=0)
    for k in range(width // LANES):
        lanes = slice(k * LANES, (k + 1) * LANES)
        turned[:, lanes] = sums[lanes].T
    turned[:, width:] = all_stats(top, total, LANES).T
    rows = outs[0].shape[0]
    for distance, out in enumerate(outs):
        index = position[2] ^ distance
        out[...] = turned[pl.ds(pl.multiple_of(index * rows, rows), rows), :].astype(BF16)


def unpack_stats(tile):
    parts = [tile] + [pltpu.roll(tile, LANES - slot * HEADS, 1) for slot in range(1, 5)]
    return parts[0] + parts[1] + parts[2], parts[3] + parts[4]


def spread(per_head, pair):
    rows = per_head.shape[0]
    lane = lax.broadcasted_iota(jnp.int32, (rows, LANES), 1)
    left = jnp.broadcast_to(per_head[:, 2 * pair : 2 * pair + 1], (rows, LANES))
    right = jnp.broadcast_to(per_head[:, 2 * pair + 1 : 2 * pair + 2], (rows, LANES))
    return jnp.where(lane < LANES // 2, left, right)


def update_kernel(own, w_out1, *refs):
    parts, out = refs[:-1], refs[-1]
    width = own.shape[1]
    stats = [unpack_stats(part[:, width:].astype(F32)) for part in parts]
    top = functools.reduce(jnp.maximum, [t for t, _ in stats])
    factors = [jnp.exp2(t - top) for t, _ in stats]
    total = sum(f * l for f, (_, l) in zip(factors, stats))
    read = []
    for pair in range(width // LANES):
        lanes = slice(pair * LANES, (pair + 1) * LANES)
        value = sum(part[:, lanes].astype(F32) * spread(f, pair) for part, f in zip(parts, factors))
        read.append(value / spread(total, pair))
    read = jnp.concatenate(read, axis=1).astype(BF16)
    out[...] = (own[...].astype(F32) + dot(read, w_out1[...])).astype(BF16)


def join_kernel(*refs):
    parts, out = refs[:-1], refs[-1]
    rows = parts[0].shape[0]
    for k, part in enumerate(parts):
        out[k * rows : (k + 1) * rows, :] = part[...]


def join(parts, name):
    rows, width = parts[0].shape
    out = jax.ShapeDtypeStruct((len(parts) * rows, width), parts[0].dtype)
    return call(join_kernel, out, [], parts, 8, 1e6, name)


def query_kernel(inner, outer, w_query2, query2_t):
    cells = outer.shape[0] // 2
    planes = inner.shape[0] // cells

    def put(block, plane):
        columns = pl.ds(pl.multiple_of(plane * cells, cells), cells)
        query2_t[:, columns] = dot(w_query2[...], block, ((0,), (1,))).astype(BF16)

    put(outer[:cells, :], 0)
    put(outer[cells:, :], planes + 1)

    def plane(i, carry):
        put(inner[pl.ds(pl.multiple_of(i * cells, cells), cells), :], i + 1)
        return carry

    lax.fori_loop(0, planes, plane, 0)


def write_kernel(
    own_state, other_state, query2_t, masked, w_key2, w_value2, w_out2, out, keys, values_t, scores, read_t
):
    half, width = own_state.shape
    head_size = width // HEADS
    values_t[:, head_size:, :] = jnp.ones_like(values_t[:, head_size:, :])
    for side, state in enumerate((own_state, other_state)):
        rows = slice(side * half, (side + 1) * half)
        keys[rows, :] = dot(state[...], w_key2[...]).astype(BF16)
        value_t = dot(w_value2[...], state[...], ((0,), (1,))).astype(BF16)
        values_t[:, :head_size, rows] = value_t.reshape(HEADS, head_size, half)
    span = scores.shape[2]

    def finish(pair, block, sums, tops):
        columns = pl.ds(pl.multiple_of(block * span, span), span)
        both = [part[:head_size] / part[head_size : head_size + 1] for part in sums]
        rows = pl.ds(pl.multiple_of(pair * LANES, LANES), LANES)
        read_t[rows, columns] = jnp.concatenate(both, axis=0).astype(BF16)

    attention_loop([keys], query2_t, [values_t], scores, 256, finish)

    def emit(r, carry):
        rows = pl.ds(pl.multiple_of(r * span, span), span)
        change = dot(read_t[:, rows], w_out2[...], ((0,), (0,)))
        out[rows, :] = masked[rows, :].astype(F32) + change
        return carry

    lax.fori_loop(0, out.shape[0] // span, emit, 0)


def call(kernel, shapes, scratch, operands, limit, flops, name, position=None):
    vmem = pl.BlockSpec(memory_space=pltpu.VMEM)
    many = isinstance(shapes, (list, tuple))
    in_specs = [vmem] * len(operands)
    if position is not None:
        in_specs = [pl.BlockSpec(memory_space=pltpu.SMEM)] + in_specs
        operands = [position] + list(operands)
    moved = sum(x.size * x.dtype.itemsize for x in operands)
    result = pl.pallas_call(
        kernel,
        out_shape=shapes,
        in_specs=in_specs,
        out_specs=[vmem] * len(shapes) if many else vmem,
        scratch_shapes=scratch,
        compiler_params=pltpu.CompilerParams(vmem_limit_bytes=limit * MIB),
        cost_estimate=pl.CostEstimate(flops=int(flops), bytes_accessed=moved, transcendentals=0),
        name=name,
    )(*operands)
    return list(result) if many else result


def exchange(low, high, axis):
    count = lax.axis_size(axis)
    up = [(i, i + 1) for i in range(count - 1)]
    down = [(i + 1, i) for i in range(count - 1)]
    return lax.ppermute(high, axis, up), lax.ppermute(low, axis, down)


def flipped(array, axis, distance):
    return lax.ppermute(array, axis, [(i, i ^ distance) for i in range(lax.axis_size(axis))])


def per_device(
    flow_field,
    fluid_mask,
    conv_weight,
    latents,
    w_query1,
    w_key1,
    w_value1,
    w_out1,
    w_query2,
    w_key2,
    w_value2,
    w_out2,
):
    size_x, size_y, size_z, width = flow_field.shape
    head_size = width // HEADS
    plane_cells = size_y * size_z
    inner_cells, outer_cells = (size_x - 2) * plane_cells, 2 * plane_cells
    cells = inner_cells + outer_cells
    latent_count = latents.shape[0]
    wide, narrow, group = ("wz", "wx"), ("ny", "nc"), ("wx", "ny")
    group_size = lax.axis_size(group)
    far = lax.axis_size("wz")
    core, member, layer = lax.axis_index("nc"), lax.axis_index(group), lax.axis_index("wz")
    position = jnp.stack([core, member, layer]).astype(jnp.int32)
    block_size = latent_count // (2 * group_size)
    rows = block_size // far
    shape = jax.ShapeDtypeStruct
    step = 1e9

    masked = flow_field * fluid_mask[:, :, :, None].astype(BF16)
    y_lo, y_hi = exchange(masked[:, 0], masked[:, -1], narrow)
    x_lo, x_hi = exchange(masked[0], masked[-1], wide)
    sides = jnp.stack([y_lo, y_hi], axis=1)
    c_lo, c_hi = exchange(sides[0], sides[-1], wide)

    inner_mixed, inner_keys, inner_values_t, query1_t = call(
        inner_kernel,
        [
            shape((inner_cells, width), BF16),
            shape((inner_cells, width), BF16),
            shape((HEADS, head_size + ONES_ROWS, inner_cells), BF16),
            shape((width, latent_count), BF16),
        ],
        [pltpu.VMEM((size_x, size_y + 2, size_z, width), F32)],
        [masked, y_lo, y_hi, conv_weight, latents, w_query1, w_key1, w_value1],
        28,
        10 * step,
        "inner",
    )
    outer_mixed, kept, given = call(
        read_kernel,
        [shape((outer_cells, width), BF16)] + [shape((group_size, width + STAT_ROWS, LANES), BF16)] * 2,
        [
            pltpu.VMEM((6, size_y + 2, size_z, width), F32),
            pltpu.VMEM((outer_cells, width), BF16),
            pltpu.VMEM((HEADS, head_size + ONES_ROWS, outer_cells), BF16),
            pltpu.VMEM((2, cells, 256), F32),
            pltpu.VMEM((STAT_ROWS, latent_count), F32),
        ],
        [
            masked,
            x_lo,
            x_hi,
            y_lo,
            y_hi,
            c_lo,
            c_hi,
            conv_weight,
            w_key1,
            w_value1,
            inner_keys,
            inner_values_t,
            query1_t,
        ],
        32,
        20 * step,
        "read",
        position,
    )
    taken = flipped(given, "nc", 1)
    block = shape((width + STAT_ROWS, LANES), BF16)
    blocks = call(merge_pair_kernel, [block] * group_size, [], [kept, taken], 16, step, "merge_pair", position)
    blocks = blocks[:1] + [flipped(blocks[d], group, d) for d in range(1, group_size)]
    parts = call(
        functools.partial(merge_group_kernel, group_size),
        [shape((rows, width + LANES), BF16)] * far,
        [pltpu.VMEM((block_size, width + LANES), F32)],
        blocks,
        16,
        step,
        "merge_group",
        position,
    )
    parts = parts[:1] + [flipped(parts[d], "wz", d) for d in range(1, far)]
    query2_t = call(
        query_kernel,
        shape((width, cells), BF16),
        [],
        [inner_mixed, outer_mixed, w_query2],
        16,
        2 * step,
        "query",
    )
    start = ((core * group_size + member) * far + layer) * rows
    own = lax.dynamic_slice_in_dim(latents, start, rows, 0)
    state = call(update_kernel, shape((rows, width), BF16), [], [own, w_out1] + parts, 16, step, "update")
    state = join([state] + [flipped(state, "wz", d) for d in range(1, far)], "join_far")
    state = join([state] + [flipped(state, group, d) for d in range(1, group_size)], "join_group")
    other = flipped(state, "nc", 1)

    result = call(
        write_kernel,
        shape((cells, width), F32),
        [
            pltpu.VMEM((latent_count, width), BF16),
            pltpu.VMEM((HEADS, head_size + ONES_ROWS, latent_count), BF16),
            pltpu.VMEM((2, latent_count, 512), F32),
            pltpu.VMEM((width, cells), BF16),
        ],
        [state, other, query2_t, masked.reshape(cells, width), w_key2, w_value2, w_out2],
        32,
        20 * step,
        "write",
    )
    return result.reshape(size_x, size_y, size_z, width)


def solution(mesh):
    wide, narrow = (mesh.shape[name] for name in ("wide", "narrow"))
    grid = Mesh(mesh.devices.reshape(wide // 2, 2, narrow // 2, 2), ("wz", "wx", "ny", "nc"))
    split = P(("wz", "wx"), ("ny", "nc"))
    return jax.shard_map(
        per_device,
        mesh=grid,
        in_specs=(split, split) + (P(),) * 10,
        out_specs=split,
        check_vma=False,
    )
```

```python
import functools
import math

import jax
import jax.numpy as jnp
from jax import lax
from jax.experimental import pallas as pl
from jax.experimental.pallas import tpu as pltpu
from jax.sharding import Mesh, PartitionSpec as P

HEADS = 8
LANES = 128
ONES_ROWS = 16
STAT_ROWS = 48
MIB = 1 << 20
F32 = jnp.float32
BF16 = jnp.bfloat16


def dot(left, right, contract=((1,), (0,))):
    return lax.dot_general(left, right, (contract, ((), ())), preferred_element_type=F32)


def prepare_kernel(position, flow, mask, masked, first, second):
    size_x, size_y, size_z, width = flow.shape

    def plane(i, carry):
        turned = mask[i].astype(F32).T
        for j in range(size_y):
            column = jnp.broadcast_to(turned[:, j : j + 1], (size_z, LANES)).astype(BF16)
            for tile in range(width // LANES):
                lanes = slice(tile * LANES, (tile + 1) * LANES)
                masked[i, j, :, lanes] = flow[i, j, :, lanes] * column
        outer = size_y - 1
        first[i] = masked[i, outer * (1 - position[3])]
        second[i] = masked[i, outer * position[3]]
        return carry

    lax.fori_loop(0, size_x, plane, 0)


def edge_kernel(position, masked, y_first, y_second, first, second):
    size_x, size_y = masked.shape[:2]
    outer = size_y + 1
    for face, plane in ((first, (size_x - 1) * (1 - position[4])), (second, (size_x - 1) * position[4])):
        face[1:outer] = masked[plane]
        face[outer * (1 - position[3])] = y_first[plane]
        face[outer * position[3]] = y_second[plane]


def fill_row(position, padded, row, i, masked, y_first, y_second):
    outer = masked.shape[1] + 1
    padded[row, 1:outer] = masked[i].astype(F32)
    padded[row, outer * (1 - position[3])] = y_first[i].astype(F32)
    padded[row, outer * position[3]] = y_second[i].astype(F32)


def stencil_plane(base, padded, conv, mixed, start):
    size_y, size_z, width = padded.shape[1] - 2, padded.shape[2], padded.shape[3]
    row_of = lax.broadcasted_iota(jnp.int32, (size_z, LANES), 0)
    for tile in range(width // LANES):
        lanes = slice(tile * LANES, (tile + 1) * LANES)
        taps = [jnp.broadcast_to(conv[n : n + 1, lanes], (size_z, LANES)) for n in range(27)]
        for j in range(size_y):
            sums = [None] * 3
            for a in range(3):
                for b in range(3):
                    window = padded[base + a, j + b, :, lanes]
                    for c in range(3):
                        term = window * taps[9 * a + 3 * b + c]
                        sums[c] = term if sums[c] is None else sums[c] + term
            below = jnp.where(row_of == 0, 0.0, pltpu.roll(sums[0], 1, 0))
            above = jnp.where(row_of == size_z - 1, 0.0, pltpu.roll(sums[2], size_z - 1, 0))
            total = padded[base + 1, j + 1, :, lanes] + sums[1] + below + above
            mixed[pl.ds(pl.multiple_of(start + j * size_z, size_z), size_z), lanes] = total.astype(BF16)


def project_plane(start, target, cells, mixed, weights, keys, values_t, query2_t):
    w_key1, w_value1, w_query2 = weights
    head_size = mixed.shape[1] // HEADS
    rows = pl.ds(pl.multiple_of(start, cells), cells)
    block = mixed[rows, :]
    keys[rows, :] = dot(block, w_key1[...]).astype(BF16)
    value_t = dot(w_value1[...], block, ((0,), (1,))).astype(BF16)
    values_t[:, :head_size, rows] = value_t.reshape(HEADS, head_size, cells)
    query2_t[:, pl.ds(pl.multiple_of(target, cells), cells)] = dot(w_query2[...], block, ((0,), (1,))).astype(BF16)


def latent_query_kernel(latents, w_query1, query1_t):
    query1_t[...] = dot(w_query1[...], latents[...], ((0,), (1,))).astype(BF16)


def inner_kernel(
    position,
    masked,
    y_first,
    y_second,
    conv,
    far_key1,
    far_value1,
    far_query2,
    keys,
    values_t,
    query2_t,
    padded,
    mixed,
    w_key1,
    w_value1,
    w_query2,
    arrived,
):
    size_x, size_y, size_z, width = masked.shape
    head_size = width // HEADS
    cells = size_y * size_z
    weights = (w_key1, w_value1, w_query2)
    copies = [
        pltpu.make_async_copy(source, target, arrived.at[n])
        for n, (source, target) in enumerate(zip((far_key1, far_value1, far_query2), weights))
    ]
    for copy in copies:
        copy.start()

    def fill(i, carry):
        fill_row(position, padded, i, i, masked, y_first, y_second)
        return carry

    lax.fori_loop(0, size_x, fill, 0)
    values_t[:, head_size:, :] = jnp.ones_like(values_t[:, head_size:, :])
    stencil_plane(0, padded, conv, mixed, 0)
    for copy in copies:
        copy.wait()

    def plane(i, carry):
        project_plane((i - 1) * cells, i * cells, cells, mixed, weights, keys, values_t, query2_t)
        stencil_plane(i, padded, conv, mixed, i * cells)
        return carry

    lax.fori_loop(1, size_x - 2, plane, 0)
    last = size_x - 3
    project_plane(last * cells, (last + 1) * cells, cells, mixed, weights, keys, values_t, query2_t)


def score_weights(query_t, head_in_pair, head_size):
    factor = 1.8 / math.sqrt(head_size) * math.log2(math.e)
    scaled = query_t.astype(F32) * factor
    high = scaled.astype(BF16)
    low = (scaled - high.astype(F32)).astype(BF16)
    blank = jnp.zeros_like(high)
    if head_in_pair == 0:
        return jnp.concatenate([high, blank, low, blank], axis=0)
    return jnp.concatenate([blank, high, blank, low], axis=0)


def attention_scores(pair, head_in_pair, block, width, chunk, keys, query_t, scores):
    head_size = LANES // 2
    start = pl.multiple_of(pair * LANES, LANES) + head_in_pair * head_size
    columns = pl.ds(pl.multiple_of(block * width, width), width)
    right = score_weights(query_t[pl.ds(start, head_size), columns], head_in_pair, head_size)
    top = None
    base = 0
    for piece in keys:
        for part in range(piece.shape[0] // chunk):
            left = piece[pl.ds(part * chunk, chunk), pl.ds(pl.multiple_of(pair * LANES, LANES), LANES)]
            found = dot(jnp.concatenate([left, left], axis=1), right)
            scores[head_in_pair, pl.ds(base, chunk), :] = found
            base += chunk
            largest = jnp.max(found.reshape(chunk // 8, 8, width), axis=0)
            top = largest if top is None else jnp.maximum(top, largest)
    return jnp.max(top, axis=0, keepdims=True)


def attention_sums(head, head_in_pair, chunk, values_t, scores, top):
    total = None
    base = 0
    for piece in values_t:
        for part in range(piece.shape[2] // chunk):
            weights = jnp.exp2(scores[head_in_pair, pl.ds(base, chunk), :] - top).astype(BF16)
            base += chunk
            found = dot(piece[head, :, pl.ds(part * chunk, chunk)], weights)
            total = found if total is None else total + found
    return total


def attention_loop(keys, query_t, values_t, scores, chunk, finish):
    width = scores.shape[2]
    blocks = query_t.shape[1] // width
    pairs = query_t.shape[0] // LANES
    steps = pairs * blocks

    def first(t):
        return attention_scores(t % pairs, 0, t // pairs, width, chunk, keys, query_t, scores)

    def step(t, top_even):
        pair, block = t % pairs, t // pairs
        top_odd = attention_scores(pair, 1, block, width, chunk, keys, query_t, scores)
        even = attention_sums(2 * pair, 0, chunk, values_t, scores, top_even)
        following = first(jnp.minimum(t + 1, steps - 1))
        odd = attention_sums(2 * pair + 1, 1, chunk, values_t, scores, top_odd)
        finish(pair, block, (even, odd), (top_even, top_odd))
        return following

    lax.fori_loop(0, steps, step, first(0))


def split3(value):
    high = value.astype(BF16).astype(F32)
    rest = value - high
    middle = rest.astype(BF16).astype(F32)
    return high, middle, rest - middle


def stat_rows(top, total):
    return split3(top) + split3(total)[:2]


def read_kernel(
    position,
    masked,
    x_first,
    x_second,
    y_first,
    y_second,
    conv,
    w_key1,
    w_value1,
    w_query2,
    inner_keys,
    inner_values_t,
    query1_t,
    inner_query2_t,
    query2_t,
    kept,
    given,
    padded,
    mixed,
    keys,
    values_t,
    scores,
    stats,
):
    size_x, size_y, size_z, width = masked.shape
    head_size = width // HEADS
    cells = size_y * size_z
    last = size_x - 1
    for row, i in ((1, 0), (2, 1), (3, last - 1), (4, last)):
        fill_row(position, padded, row, i, masked, y_first, y_second)
    padded[5 * (1 - position[4])] = x_first[...].astype(F32)
    padded[5 * position[4]] = x_second[...].astype(F32)
    values_t[:, head_size:, :] = jnp.ones_like(values_t[:, head_size:, :])
    stats[...] = jnp.zeros_like(stats)

    def plane(i, carry):
        stencil_plane(3 * i, padded, conv, mixed, i * cells)
        weights = (w_key1, w_value1, w_query2)
        project_plane(i * cells, i * last * cells, cells, mixed, weights, keys, values_t, query2_t)
        return carry

    lax.fori_loop(0, 2, plane, 0)

    core = position[0]
    per_half = kept.shape[0]
    span = scores.shape[2]
    ratio = span // LANES

    def finish(pair, block, sums, tops):
        both = jnp.concatenate([part[:head_size] for part in sums], axis=0).astype(BF16)
        rows = pl.ds(pl.multiple_of(pair * LANES, LANES), LANES)
        first = block * ratio
        side = first // per_half

        def write(target):
            for k in range(ratio):
                target[first - side * per_half + k, rows, :] = both[:, k * LANES : (k + 1) * LANES]

        pl.when(side == core)(lambda: write(kept))
        pl.when(side != core)(lambda: write(given))
        columns = pl.ds(pl.multiple_of(block * span, span), span)
        for head_in_pair in range(2):
            values = stat_rows(tops[head_in_pair], sums[head_in_pair][head_size : head_size + 1])
            for slot, row in enumerate(values):
                stats[pl.ds(slot * HEADS + 2 * pair + head_in_pair, 1), columns] = row

    attention_loop([inner_keys, keys], query1_t, [inner_values_t, values_t], scores, 256, finish)
    for target, side in ((kept, core), (given, 1 - core)):
        for k in range(per_half):
            columns = pl.ds(pl.multiple_of((side * per_half + k) * LANES, LANES), LANES)
            target[k, width:, :] = stats[:, columns].astype(BF16)


def merge_blocks(blocks):
    width = blocks[0].shape[0] - STAT_ROWS
    head_size = width // HEADS
    slots = [[block[width + n * HEADS : width + (n + 1) * HEADS] for n in range(5)] for block in blocks]
    tops = [s[0] + s[1] + s[2] for s in slots]
    top = functools.reduce(jnp.maximum, tops)
    factors = [jnp.exp2(t - top) for t in tops]
    total = sum(f * (s[3] + s[4]) for f, s in zip(factors, slots))
    sums = []
    for head in range(HEADS):
        rows = slice(head * head_size, (head + 1) * head_size)
        sums.append(sum(block[rows] * f[head : head + 1] for block, f in zip(blocks, factors)))
    return sums, top, total


def all_stats(top, total, size):
    rows = list(stat_rows(top, total))
    filler = jnp.zeros((size - len(rows) * HEADS,) + top.shape[1:], F32)
    return jnp.concatenate(rows + [filler], axis=0)


def merge_pair_kernel(position, kept, taken, *outs):
    for distance, out in enumerate(outs):
        index = position[1] ^ distance
        sums, top, total = merge_blocks([ref[index].astype(F32) for ref in (kept, taken)])
        sums.append(all_stats(top, total, STAT_ROWS))
        out[...] = jnp.concatenate(sums, axis=0).astype(BF16)


def merge_group_kernel(count, position, *refs):
    blocks, outs, turned = refs[:count], refs[count:-1], refs[-1]
    sums, top, total = merge_blocks([ref[...].astype(F32) for ref in blocks])
    width = turned.shape[1] - LANES
    sums = jnp.concatenate(sums, axis=0)
    for k in range(width // LANES):
        lanes = slice(k * LANES, (k + 1) * LANES)
        turned[:, lanes] = sums[lanes].T
    turned[:, width:] = all_stats(top, total, LANES).T
    rows = outs[0].shape[0]
    for distance, out in enumerate(outs):
        index = position[2] ^ distance
        out[...] = turned[pl.ds(pl.multiple_of(index * rows, rows), rows), :].astype(BF16)


def unpack_stats(tile):
    parts = [tile] + [pltpu.roll(tile, LANES - slot * HEADS, 1) for slot in range(1, 5)]
    return parts[0] + parts[1] + parts[2], parts[3] + parts[4]


def spread(per_head, pair):
    rows = per_head.shape[0]
    lane = lax.broadcasted_iota(jnp.int32, (rows, LANES), 1)
    left = jnp.broadcast_to(per_head[:, 2 * pair : 2 * pair + 1], (rows, LANES))
    right = jnp.broadcast_to(per_head[:, 2 * pair + 1 : 2 * pair + 2], (rows, LANES))
    return jnp.where(lane < LANES // 2, left, right)


def update_kernel(own, w_out1, *refs):
    parts, out = refs[:-1], refs[-1]
    width = own.shape[1]
    stats = [unpack_stats(part[:, width:].astype(F32)) for part in parts]
    top = functools.reduce(jnp.maximum, [t for t, _ in stats])
    factors = [jnp.exp2(t - top) for t, _ in stats]
    total = sum(f * l for f, (_, l) in zip(factors, stats))
    read = []
    for pair in range(width // LANES):
        lanes = slice(pair * LANES, (pair + 1) * LANES)
        value = sum(part[:, lanes].astype(F32) * spread(f, pair) for part, f in zip(parts, factors))
        read.append(value / spread(total, pair))
    read = jnp.concatenate(read, axis=1).astype(BF16)
    out[...] = (own[...].astype(F32) + dot(read, w_out1[...])).astype(BF16)


def join_kernel(*refs):
    parts, out = refs[:-1], refs[-1]
    rows = parts[0].shape[0]
    for k, part in enumerate(parts):
        out[k * rows : (k + 1) * rows, :] = part[...]


def join(parts, name):
    rows, width = parts[0].shape
    out = jax.ShapeDtypeStruct((len(parts) * rows, width), parts[0].dtype)
    return call(join_kernel, out, [], parts, 8, 1e6, name)


def write_kernel(
    own_state, other_state, query2_t, masked, w_key2, w_value2, w_out2, out, keys, values_t, scores, read_t
):
    half, width = own_state.shape
    head_size = width // HEADS
    values_t[:, head_size:, :] = jnp.ones_like(values_t[:, head_size:, :])
    for side, state in enumerate((own_state, other_state)):
        rows = slice(side * half, (side + 1) * half)
        keys[rows, :] = dot(state[...], w_key2[...]).astype(BF16)
        value_t = dot(w_value2[...], state[...], ((0,), (1,))).astype(BF16)
        values_t[:, :head_size, rows] = value_t.reshape(HEADS, head_size, half)
    span = scores.shape[2]

    def finish(pair, block, sums, tops):
        columns = pl.ds(pl.multiple_of(block * span, span), span)
        both = [part[:head_size] / part[head_size : head_size + 1] for part in sums]
        rows = pl.ds(pl.multiple_of(pair * LANES, LANES), LANES)
        read_t[rows, columns] = jnp.concatenate(both, axis=0).astype(BF16)

    attention_loop([keys], query2_t, [values_t], scores, 256, finish)

    def emit(r, carry):
        rows = pl.ds(pl.multiple_of(r * span, span), span)
        change = dot(read_t[:, rows], w_out2[...], ((0,), (0,)))
        out[rows, :] = masked[rows, :].astype(F32) + change
        return carry

    lax.fori_loop(0, out.shape[0] // span, emit, 0)


def call(kernel, shapes, scratch, operands, limit, flops, name, position=None, far=(), aliases=None):
    vmem = pl.BlockSpec(memory_space=pltpu.VMEM)
    hbm = pl.BlockSpec(memory_space=pltpu.HBM)
    many = isinstance(shapes, (list, tuple))
    in_specs = [hbm if n in far else vmem for n in range(len(operands))]
    if position is not None:
        in_specs = [pl.BlockSpec(memory_space=pltpu.SMEM)] + in_specs
        operands = [position] + list(operands)
    moved = sum(x.size * x.dtype.itemsize for x in operands)
    result = pl.pallas_call(
        kernel,
        out_shape=shapes,
        in_specs=in_specs,
        out_specs=[vmem] * len(shapes) if many else vmem,
        scratch_shapes=scratch,
        compiler_params=pltpu.CompilerParams(vmem_limit_bytes=limit * MIB),
        cost_estimate=pl.CostEstimate(flops=int(flops), bytes_accessed=moved, transcendentals=0),
        input_output_aliases=aliases or {},
        name=name,
    )(*operands)
    return list(result) if many else result


def pair_exchange(first, second, axis):
    count = lax.axis_size(axis)
    swaps = [[], []]
    for i in range(count - 1):
        swaps[i % 2] += [(i, i + 1), (i + 1, i)]
    return lax.ppermute(first, axis, swaps[0]), lax.ppermute(second, axis, swaps[1])


def flipped(array, axis, distance):
    return lax.ppermute(array, axis, [(i, i ^ distance) for i in range(lax.axis_size(axis))])


def per_device(
    flow_field,
    fluid_mask,
    conv_weight,
    latents,
    w_query1,
    w_key1,
    w_value1,
    w_out1,
    w_query2,
    w_key2,
    w_value2,
    w_out2,
):
    size_x, size_y, size_z, width = flow_field.shape
    head_size = width // HEADS
    plane_cells = size_y * size_z
    inner_cells, outer_cells = (size_x - 2) * plane_cells, 2 * plane_cells
    cells = inner_cells + outer_cells
    latent_count = latents.shape[0]
    wide, narrow, group = ("wz", "wx"), ("ny", "nc"), ("wx", "ny")
    group_size = lax.axis_size(group)
    far = lax.axis_size("wz")
    core, member, layer = lax.axis_index("nc"), lax.axis_index(group), lax.axis_index("wz")
    column = lax.axis_index("wx")
    position = jnp.stack([core, member, layer, core, column]).astype(jnp.int32)
    block_size = latent_count // (2 * group_size)
    rows = block_size // far
    shape = jax.ShapeDtypeStruct
    step = 1e9

    side = shape((size_x, size_z, width), BF16)
    masked, y_first, y_second = call(
        prepare_kernel,
        [shape(flow_field.shape, BF16), side, side],
        [],
        [flow_field, fluid_mask],
        12,
        step,
        "prepare",
        position,
    )
    y_first, y_second = pair_exchange(y_first, y_second, narrow)
    query1_t = call(
        latent_query_kernel,
        shape((width, latent_count), BF16),
        [],
        [latents, w_query1],
        12,
        2 * step,
        "latent_query",
    )
    side = shape((size_y + 2, size_z, width), BF16)
    x_first, x_second = call(
        edge_kernel, [side, side], [], [masked, y_first, y_second], 12, step, "edge", position
    )
    x_first, x_second = pair_exchange(x_first, x_second, wide)
    weight = pltpu.VMEM((width, width), BF16)
    inner_keys, inner_values_t, query2_t = call(
        inner_kernel,
        [
            shape((inner_cells, width), BF16),
            shape((HEADS, head_size + ONES_ROWS, inner_cells), BF16),
            shape((width, cells), BF16),
        ],
        [
            pltpu.VMEM((size_x, size_y + 2, size_z, width), F32),
            pltpu.VMEM((inner_cells, width), BF16),
            weight,
            weight,
            weight,
            pltpu.SemaphoreType.DMA((3,)),
        ],
        [masked, y_first, y_second, conv_weight, w_key1, w_value1, w_query2],
        28,
        10 * step,
        "inner",
        position,
        (4, 5, 6),
    )
    query2_t, kept, given = call(
        read_kernel,
        [shape((width, cells), BF16)] + [shape((group_size, width + STAT_ROWS, LANES), BF16)] * 2,
        [
            pltpu.VMEM((6, size_y + 2, size_z, width), F32),
            pltpu.VMEM((outer_cells, width), BF16),
            pltpu.VMEM((outer_cells, width), BF16),
            pltpu.VMEM((HEADS, head_size + ONES_ROWS, outer_cells), BF16),
            pltpu.VMEM((2, cells, 256), F32),
            pltpu.VMEM((STAT_ROWS, latent_count), F32),
        ],
        [
            masked,
            x_first,
            x_second,
            y_first,
            y_second,
            conv_weight,
            w_key1,
            w_value1,
            w_query2,
            inner_keys,
            inner_values_t,
            query1_t,
            query2_t,
        ],
        32,
        20 * step,
        "read",
        position,
        (),
        {13: 0},
    )
    taken = flipped(given, "nc", 1)
    block = shape((width + STAT_ROWS, LANES), BF16)
    blocks = call(merge_pair_kernel, [block] * group_size, [], [kept, taken], 16, step, "merge_pair", position)
    blocks = blocks[:1] + [flipped(blocks[d], group, d) for d in range(1, group_size)]
    parts = call(
        functools.partial(merge_group_kernel, group_size),
        [shape((rows, width + LANES), BF16)] * far,
        [pltpu.VMEM((block_size, width + LANES), F32)],
        blocks,
        16,
        step,
        "merge_group",
        position,
    )
    parts = parts[:1] + [flipped(parts[d], "wz", d) for d in range(1, far)]
    start = ((core * group_size + member) * far + layer) * rows
    own = lax.dynamic_slice_in_dim(latents, start, rows, 0)
    state = call(update_kernel, shape((rows, width), BF16), [], [own, w_out1] + parts, 16, step, "update")
    state = join([state] + [flipped(state, "wz", d) for d in range(1, far)], "join_far")
    state = join([state] + [flipped(state, group, d) for d in range(1, group_size)], "join_group")
    other = flipped(state, "nc", 1)

    result = call(
        write_kernel,
        shape((cells, width), F32),
        [
            pltpu.VMEM((latent_count, width), BF16),
            pltpu.VMEM((HEADS, head_size + ONES_ROWS, latent_count), BF16),
            pltpu.VMEM((2, latent_count, 512), F32),
            pltpu.VMEM((width, cells), BF16),
        ],
        [state, other, query2_t, masked.reshape(cells, width), w_key2, w_value2, w_out2],
        32,
        20 * step,
        "write",
    )
    return result.reshape(size_x, size_y, size_z, width)


def solution(mesh):
    wide, narrow = (mesh.shape[name] for name in ("wide", "narrow"))
    grid = Mesh(mesh.devices.reshape(wide // 2, 2, narrow // 2, 2), ("wz", "wx", "ny", "nc"))
    split = P(("wz", "wx"), ("ny", "nc"))
    return jax.shard_map(
        per_device,
        mesh=grid,
        in_specs=(split, split) + (P(),) * 10,
        out_specs=split,
        check_vma=False,
    )
```

```python
import functools
import math

import jax
import jax.numpy as jnp
from jax import lax
from jax.experimental import pallas as pl
from jax.experimental.pallas import tpu as pltpu
from jax.sharding import Mesh, PartitionSpec as P

HEADS = 8
LANES = 128
ONES_ROWS = 16
STAT_ROWS = 48
MIB = 1 << 20
F32 = jnp.float32
BF16 = jnp.bfloat16


def dot(left, right, contract=((1,), (0,))):
    return lax.dot_general(left, right, (contract, ((), ())), preferred_element_type=F32)


def masked_column(flow, mask_plane, i, j):
    size_z, width = flow.shape[2:]
    column = jnp.broadcast_to(mask_plane[:, j : j + 1], (size_z, LANES)).astype(BF16)
    tiles = [flow[i, j, :, k * LANES : (k + 1) * LANES] * column for k in range(width // LANES)]
    return jnp.concatenate(tiles, axis=1)


def face_kernel(position, flow, far_mask, first, second, low, high, mask, arrived):
    size_x, size_y = flow.shape[:2]
    copies = []
    for n, (j, target) in enumerate(((0, low), (size_y - 1, high))):
        copies.append(pltpu.make_async_copy(flow.at[:, pl.ds(j, 1)], target, arrived.at[n]))
        copies[-1].start()
    copies.append(pltpu.make_async_copy(far_mask, mask, arrived.at[2]))
    copies[-1].start()
    for copy in copies:
        copy.wait()
    odd = position[3] == 1
    for i in range(size_x):
        turned = mask[i].astype(F32).T
        bottom = masked_column(low, turned, i, 0)
        top = masked_column(high, turned[:, size_y - 1 :], i, 0)
        first[i] = jnp.where(odd, bottom, top)
        second[i] = jnp.where(odd, top, bottom)


def prepare_kernel(flow, mask, masked):
    size_x, size_y = flow.shape[:2]

    def plane(i, carry):
        turned = mask[i].astype(F32).T
        for j in range(size_y):
            masked[i, j] = masked_column(flow, turned, i, j)
        return carry

    lax.fori_loop(0, size_x, plane, 0)


def edge_kernel(position, masked, y_first, y_second, first, second):
    size_x, size_y = masked.shape[:2]
    outer = size_y + 1
    for face, plane in ((first, (size_x - 1) * (1 - position[4])), (second, (size_x - 1) * position[4])):
        face[1:outer] = masked[plane]
        face[outer * (1 - position[3])] = y_first[plane]
        face[outer * position[3]] = y_second[plane]


def fill_row(position, padded, row, i, masked, y_first, y_second):
    outer = masked.shape[1] + 1
    padded[row, 1:outer] = masked[i].astype(F32)
    padded[row, outer * (1 - position[3])] = y_first[i].astype(F32)
    padded[row, outer * position[3]] = y_second[i].astype(F32)


def stencil_plane(base, padded, conv, mixed, start):
    size_y, size_z, width = padded.shape[1] - 2, padded.shape[2], padded.shape[3]
    row_of = lax.broadcasted_iota(jnp.int32, (size_z, LANES), 0)
    for tile in range(width // LANES):
        lanes = slice(tile * LANES, (tile + 1) * LANES)
        taps = [jnp.broadcast_to(conv[n : n + 1, lanes], (size_z, LANES)) for n in range(27)]
        for j in range(size_y):
            sums = [None] * 3
            for a in range(3):
                for b in range(3):
                    window = padded[base + a, j + b, :, lanes]
                    for c in range(3):
                        term = window * taps[9 * a + 3 * b + c]
                        sums[c] = term if sums[c] is None else sums[c] + term
            below = jnp.where(row_of == 0, 0.0, pltpu.roll(sums[0], 1, 0))
            above = jnp.where(row_of == size_z - 1, 0.0, pltpu.roll(sums[2], size_z - 1, 0))
            total = padded[base + 1, j + 1, :, lanes] + sums[1] + below + above
            mixed[pl.ds(pl.multiple_of(start + j * size_z, size_z), size_z), lanes] = total.astype(BF16)


def project_plane(start, target, cells, mixed, weights, keys, values_t, query2_t):
    w_key1, w_value1, w_query2 = weights
    head_size = mixed.shape[1] // HEADS
    rows = pl.ds(pl.multiple_of(start, cells), cells)
    block = mixed[rows, :]
    keys[rows, :] = dot(block, w_key1[...]).astype(BF16)
    value_t = dot(w_value1[...], block, ((0,), (1,))).astype(BF16)
    values_t[:, :head_size, rows] = value_t.reshape(HEADS, head_size, cells)
    query2_t[:, pl.ds(pl.multiple_of(target, cells), cells)] = dot(w_query2[...], block, ((0,), (1,))).astype(BF16)


def latent_query_kernel(latents, w_query1, query1_t):
    query1_t[...] = dot(w_query1[...], latents[...], ((0,), (1,))).astype(BF16)


def inner_kernel(
    position,
    masked,
    y_first,
    y_second,
    conv,
    far_key1,
    far_value1,
    far_query2,
    keys,
    values_t,
    query2_t,
    padded,
    mixed,
    w_key1,
    w_value1,
    w_query2,
    arrived,
):
    size_x, size_y, size_z, width = masked.shape
    head_size = width // HEADS
    cells = size_y * size_z
    weights = (w_key1, w_value1, w_query2)
    copies = [
        pltpu.make_async_copy(source, target, arrived.at[n])
        for n, (source, target) in enumerate(zip((far_key1, far_value1, far_query2), weights))
    ]
    for copy in copies:
        copy.start()

    def fill(i, carry):
        fill_row(position, padded, i, i, masked, y_first, y_second)
        return carry

    lax.fori_loop(0, size_x, fill, 0)
    values_t[:, head_size:, :] = jnp.ones_like(values_t[:, head_size:, :])
    stencil_plane(0, padded, conv, mixed, 0)
    for copy in copies:
        copy.wait()

    def plane(i, carry):
        project_plane((i - 1) * cells, i * cells, cells, mixed, weights, keys, values_t, query2_t)
        stencil_plane(i, padded, conv, mixed, i * cells)
        return carry

    lax.fori_loop(1, size_x - 2, plane, 0)
    last = size_x - 3
    project_plane(last * cells, (last + 1) * cells, cells, mixed, weights, keys, values_t, query2_t)


def score_weights(query_t, head_in_pair, head_size):
    factor = 1.8 / math.sqrt(head_size) * math.log2(math.e)
    scaled = query_t.astype(F32) * factor
    high = scaled.astype(BF16)
    low = (scaled - high.astype(F32)).astype(BF16)
    blank = jnp.zeros_like(high)
    if head_in_pair == 0:
        return jnp.concatenate([high, blank, low, blank], axis=0)
    return jnp.concatenate([blank, high, blank, low], axis=0)


def attention_scores(pair, head_in_pair, block, width, chunk, keys, query_t, scores):
    head_size = LANES // 2
    start = pl.multiple_of(pair * LANES, LANES) + head_in_pair * head_size
    columns = pl.ds(pl.multiple_of(block * width, width), width)
    right = score_weights(query_t[pl.ds(start, head_size), columns], head_in_pair, head_size)
    top = None
    base = 0
    for piece in keys:
        for part in range(piece.shape[0] // chunk):
            left = piece[pl.ds(part * chunk, chunk), pl.ds(pl.multiple_of(pair * LANES, LANES), LANES)]
            found = dot(jnp.concatenate([left, left], axis=1), right)
            scores[head_in_pair, pl.ds(base, chunk), :] = found
            base += chunk
            largest = jnp.max(found.reshape(chunk // 8, 8, width), axis=0)
            top = largest if top is None else jnp.maximum(top, largest)
    return jnp.max(top, axis=0, keepdims=True)


def attention_sums(head, head_in_pair, chunk, values_t, scores, top):
    total = None
    base = 0
    for piece in values_t:
        for part in range(piece.shape[2] // chunk):
            weights = jnp.exp2(scores[head_in_pair, pl.ds(base, chunk), :] - top).astype(BF16)
            base += chunk
            found = dot(piece[head, :, pl.ds(part * chunk, chunk)], weights)
            total = found if total is None else total + found
    return total


def attention_loop(keys, query_t, values_t, scores, chunk, finish):
    width = scores.shape[2]
    blocks = query_t.shape[1] // width
    pairs = query_t.shape[0] // LANES
    steps = pairs * blocks

    def first(t):
        return attention_scores(t % pairs, 0, t // pairs, width, chunk, keys, query_t, scores)

    def step(t, top_even):
        pair, block = t % pairs, t // pairs
        top_odd = attention_scores(pair, 1, block, width, chunk, keys, query_t, scores)
        even = attention_sums(2 * pair, 0, chunk, values_t, scores, top_even)
        following = first(jnp.minimum(t + 1, steps - 1))
        odd = attention_sums(2 * pair + 1, 1, chunk, values_t, scores, top_odd)
        finish(pair, block, (even, odd), (top_even, top_odd))
        return following

    lax.fori_loop(0, steps, step, first(0))


def split3(value):
    high = value.astype(BF16).astype(F32)
    rest = value - high
    middle = rest.astype(BF16).astype(F32)
    return high, middle, rest - middle


def stat_rows(top, total):
    return split3(top) + split3(total)[:2]


def read_kernel(
    position,
    masked,
    x_first,
    x_second,
    y_first,
    y_second,
    conv,
    w_key1,
    w_value1,
    w_query2,
    inner_keys,
    inner_values_t,
    query1_t,
    inner_query2_t,
    query2_t,
    kept,
    given,
    padded,
    mixed,
    keys,
    values_t,
    scores,
    stats,
):
    size_x, size_y, size_z, width = masked.shape
    head_size = width // HEADS
    cells = size_y * size_z
    last = size_x - 1
    for row, i in ((1, 0), (2, 1), (3, last - 1), (4, last)):
        fill_row(position, padded, row, i, masked, y_first, y_second)
    padded[5 * (1 - position[4])] = x_first[...].astype(F32)
    padded[5 * position[4]] = x_second[...].astype(F32)
    values_t[:, head_size:, :] = jnp.ones_like(values_t[:, head_size:, :])
    stats[...] = jnp.zeros_like(stats)

    def plane(i, carry):
        stencil_plane(3 * i, padded, conv, mixed, i * cells)
        weights = (w_key1, w_value1, w_query2)
        project_plane(i * cells, i * last * cells, cells, mixed, weights, keys, values_t, query2_t)
        return carry

    lax.fori_loop(0, 2, plane, 0)

    core = position[0]
    per_half = kept.shape[0]
    span = scores.shape[2]
    ratio = span // LANES

    def finish(pair, block, sums, tops):
        both = jnp.concatenate([part[:head_size] for part in sums], axis=0).astype(BF16)
        rows = pl.ds(pl.multiple_of(pair * LANES, LANES), LANES)
        first = block * ratio
        side = first // per_half

        def write(target):
            for k in range(ratio):
                target[first - side * per_half + k, rows, :] = both[:, k * LANES : (k + 1) * LANES]

        pl.when(side == core)(lambda: write(kept))
        pl.when(side != core)(lambda: write(given))
        columns = pl.ds(pl.multiple_of(block * span, span), span)
        for head_in_pair in range(2):
            values = stat_rows(tops[head_in_pair], sums[head_in_pair][head_size : head_size + 1])
            for slot, row in enumerate(values):
                stats[pl.ds(slot * HEADS + 2 * pair + head_in_pair, 1), columns] = row

    attention_loop([inner_keys, keys], query1_t, [inner_values_t, values_t], scores, 256, finish)
    for target, side in ((kept, core), (given, 1 - core)):
        for k in range(per_half):
            columns = pl.ds(pl.multiple_of((side * per_half + k) * LANES, LANES), LANES)
            target[k, width:, :] = stats[:, columns].astype(BF16)


def merge_blocks(blocks):
    width = blocks[0].shape[0] - STAT_ROWS
    head_size = width // HEADS
    slots = [[block[width + n * HEADS : width + (n + 1) * HEADS] for n in range(5)] for block in blocks]
    tops = [s[0] + s[1] + s[2] for s in slots]
    top = functools.reduce(jnp.maximum, tops)
    factors = [jnp.exp2(t - top) for t in tops]
    total = sum(f * (s[3] + s[4]) for f, s in zip(factors, slots))
    sums = []
    for head in range(HEADS):
        rows = slice(head * head_size, (head + 1) * head_size)
        sums.append(sum(block[rows] * f[head : head + 1] for block, f in zip(blocks, factors)))
    return sums, top, total


def all_stats(top, total, size):
    rows = list(stat_rows(top, total))
    filler = jnp.zeros((size - len(rows) * HEADS,) + top.shape[1:], F32)
    return jnp.concatenate(rows + [filler], axis=0)


def merge_pair_kernel(position, kept, taken, *outs):
    for distance, out in enumerate(outs):
        index = position[1] ^ distance
        sums, top, total = merge_blocks([ref[index].astype(F32) for ref in (kept, taken)])
        sums.append(all_stats(top, total, STAT_ROWS))
        out[...] = jnp.concatenate(sums, axis=0).astype(BF16)


def merge_group_kernel(count, position, *refs):
    blocks, outs, turned = refs[:count], refs[count:-1], refs[-1]
    sums, top, total = merge_blocks([ref[...].astype(F32) for ref in blocks])
    width = turned.shape[1] - LANES
    sums = jnp.concatenate(sums, axis=0)
    for k in range(width // LANES):
        lanes = slice(k * LANES, (k + 1) * LANES)
        turned[:, lanes] = sums[lanes].T
    turned[:, width:] = all_stats(top, total, LANES).T
    rows = outs[0].shape[0]
    for distance, out in enumerate(outs):
        index = position[2] ^ distance
        out[...] = turned[pl.ds(pl.multiple_of(index * rows, rows), rows), :].astype(BF16)


def unpack_stats(tile):
    parts = [tile] + [pltpu.roll(tile, LANES - slot * HEADS, 1) for slot in range(1, 5)]
    return parts[0] + parts[1] + parts[2], parts[3] + parts[4]


def spread(per_head, pair):
    rows = per_head.shape[0]
    lane = lax.broadcasted_iota(jnp.int32, (rows, LANES), 1)
    left = jnp.broadcast_to(per_head[:, 2 * pair : 2 * pair + 1], (rows, LANES))
    right = jnp.broadcast_to(per_head[:, 2 * pair + 1 : 2 * pair + 2], (rows, LANES))
    return jnp.where(lane < LANES // 2, left, right)


def update_kernel(own, w_out1, *refs):
    parts, out = refs[:-1], refs[-1]
    width = own.shape[1]
    stats = [unpack_stats(part[:, width:].astype(F32)) for part in parts]
    top = functools.reduce(jnp.maximum, [t for t, _ in stats])
    factors = [jnp.exp2(t - top) for t, _ in stats]
    total = sum(f * l for f, (_, l) in zip(factors, stats))
    read = []
    for pair in range(width // LANES):
        lanes = slice(pair * LANES, (pair + 1) * LANES)
        value = sum(part[:, lanes].astype(F32) * spread(f, pair) for part, f in zip(parts, factors))
        read.append(value / spread(total, pair))
    read = jnp.concatenate(read, axis=1).astype(BF16)
    out[...] = (own[...].astype(F32) + dot(read, w_out1[...])).astype(BF16)


def join_kernel(*refs):
    parts, out = refs[:-1], refs[-1]
    rows = parts[0].shape[0]
    for k, part in enumerate(parts):
        out[k * rows : (k + 1) * rows, :] = part[...]


def join(parts, name):
    rows, width = parts[0].shape
    out = jax.ShapeDtypeStruct((len(parts) * rows, width), parts[0].dtype)
    return call(join_kernel, out, [], parts, 8, 1e6, name)


def write_kernel(
    own_state,
    other_state,
    query2_t,
    masked,
    w_key2,
    w_value2,
    w_out2,
    out,
    keys,
    values_t,
    scores,
    read_t,
    buffers,
    sent,
):
    half, width = own_state.shape
    head_size = width // HEADS
    values_t[:, head_size:, :] = jnp.ones_like(values_t[:, head_size:, :])
    for side, state in enumerate((own_state, other_state)):
        rows = slice(side * half, (side + 1) * half)
        keys[rows, :] = dot(state[...], w_key2[...]).astype(BF16)
        value_t = dot(w_value2[...], state[...], ((0,), (1,))).astype(BF16)
        values_t[:, :head_size, rows] = value_t.reshape(HEADS, head_size, half)
    span = scores.shape[2]
    blocks = out.shape[0] // span
    last_pair = width // LANES - 1

    def send(block):
        slot = block % 2
        rows = pl.ds(pl.multiple_of(block * span, span), span)
        return pltpu.make_async_copy(buffers.at[slot], out.at[rows, :], sent.at[slot])

    def finish(pair, block, sums, tops):
        both = [part[:head_size] / part[head_size : head_size + 1] for part in sums]
        rows = pl.ds(pl.multiple_of(pair * LANES, LANES), LANES)
        read_t[rows, :] = jnp.concatenate(both, axis=0).astype(BF16)

        @pl.when(pair == last_pair)
        def _():
            pl.when(block >= 2)(lambda: send(block - 2).wait())
            cells = pl.ds(pl.multiple_of(block * span, span), span)
            change = dot(read_t[...], w_out2[...], ((0,), (0,)))
            buffers[block % 2] = masked[cells, :].astype(F32) + change
            send(block).start()

    attention_loop([keys], query2_t, [values_t], scores, 256, finish)
    for block in range(max(blocks - 2, 0), blocks):
        send(block).wait()


def call(kernel, shapes, scratch, operands, limit, flops, name, position=None, far=(), aliases=None, out_space=pltpu.VMEM):
    vmem = pl.BlockSpec(memory_space=pltpu.VMEM)
    hbm = pl.BlockSpec(memory_space=pltpu.HBM)
    many = isinstance(shapes, (list, tuple))
    in_specs = [hbm if n in far else vmem for n in range(len(operands))]
    if position is not None:
        in_specs = [pl.BlockSpec(memory_space=pltpu.SMEM)] + in_specs
        operands = [position] + list(operands)
    moved = sum(x.size * x.dtype.itemsize for x in operands)
    result = pl.pallas_call(
        kernel,
        out_shape=shapes,
        in_specs=in_specs,
        out_specs=[vmem] * len(shapes) if many else pl.BlockSpec(memory_space=out_space),
        scratch_shapes=scratch,
        compiler_params=pltpu.CompilerParams(vmem_limit_bytes=limit * MIB),
        cost_estimate=pl.CostEstimate(flops=int(flops), bytes_accessed=moved, transcendentals=0),
        input_output_aliases=aliases or {},
        name=name,
    )(*operands)
    return list(result) if many else result


def pair_exchange(first, second, axis):
    count = lax.axis_size(axis)
    swaps = [[], []]
    for i in range(count - 1):
        swaps[i % 2] += [(i, i + 1), (i + 1, i)]
    other = lax.ppermute(second, axis, swaps[1])
    return lax.ppermute(first, axis, swaps[0]), other


def flipped(array, axis, distance):
    return lax.ppermute(array, axis, [(i, i ^ distance) for i in range(lax.axis_size(axis))])


def per_device(
    flow_field,
    fluid_mask,
    conv_weight,
    latents,
    w_query1,
    w_key1,
    w_value1,
    w_out1,
    w_query2,
    w_key2,
    w_value2,
    w_out2,
):
    size_x, size_y, size_z, width = flow_field.shape
    head_size = width // HEADS
    plane_cells = size_y * size_z
    inner_cells, outer_cells = (size_x - 2) * plane_cells, 2 * plane_cells
    cells = inner_cells + outer_cells
    latent_count = latents.shape[0]
    wide, narrow, group = ("wz", "wx"), ("ny", "nc"), ("wx", "ny")
    group_size = lax.axis_size(group)
    far = lax.axis_size("wz")
    core, member, layer = lax.axis_index("nc"), lax.axis_index(group), lax.axis_index("wz")
    column = lax.axis_index("wx")
    position = jnp.stack([core, member, layer, core, column]).astype(jnp.int32)
    block_size = latent_count // (2 * group_size)
    rows = block_size // far
    shape = jax.ShapeDtypeStruct
    step = 1e9

    side = shape((size_x, size_z, width), BF16)
    ends = pltpu.VMEM((size_x, 1, size_z, width), BF16)
    y_first, y_second = call(
        face_kernel,
        [side, side],
        [ends, ends, pltpu.VMEM(fluid_mask.shape, jnp.int32), pltpu.SemaphoreType.DMA((3,))],
        [flow_field, fluid_mask],
        56,
        step,
        "face",
        position,
        (0, 1),
    )
    y_first, y_second = pair_exchange(y_first, y_second, narrow)
    masked = call(
        prepare_kernel, shape(flow_field.shape, BF16), [], [flow_field, fluid_mask], 12, 2 * step, "prepare"
    )
    query1_t = call(
        latent_query_kernel,
        shape((width, latent_count), BF16),
        [],
        [latents, w_query1],
        12,
        2 * step,
        "latent_query",
    )
    side = shape((size_y + 2, size_z, width), BF16)
    x_first, x_second = call(
        edge_kernel, [side, side], [], [masked, y_first, y_second], 12, step, "edge", position
    )
    x_first, x_second = pair_exchange(x_first, x_second, wide)
    weight = pltpu.VMEM((width, width), BF16)
    inner_keys, inner_values_t, query2_t = call(
        inner_kernel,
        [
            shape((inner_cells, width), BF16),
            shape((HEADS, head_size + ONES_ROWS, inner_cells), BF16),
            shape((width, cells), BF16),
        ],
        [
            pltpu.VMEM((size_x, size_y + 2, size_z, width), F32),
            pltpu.VMEM((inner_cells, width), BF16),
            weight,
            weight,
            weight,
            pltpu.SemaphoreType.DMA((3,)),
        ],
        [masked, y_first, y_second, conv_weight, w_key1, w_value1, w_query2],
        28,
        10 * step,
        "inner",
        position,
        (4, 5, 6),
    )
    query2_t, kept, given = call(
        read_kernel,
        [shape((width, cells), BF16)] + [shape((group_size, width + STAT_ROWS, LANES), BF16)] * 2,
        [
            pltpu.VMEM((6, size_y + 2, size_z, width), F32),
            pltpu.VMEM((outer_cells, width), BF16),
            pltpu.VMEM((outer_cells, width), BF16),
            pltpu.VMEM((HEADS, head_size + ONES_ROWS, outer_cells), BF16),
            pltpu.VMEM((2, cells, latent_count // 2), F32),
            pltpu.VMEM((STAT_ROWS, latent_count), F32),
        ],
        [
            masked,
            x_first,
            x_second,
            y_first,
            y_second,
            conv_weight,
            w_key1,
            w_value1,
            w_query2,
            inner_keys,
            inner_values_t,
            query1_t,
            query2_t,
        ],
        32,
        20 * step,
        "read",
        position,
        (),
        {13: 0},
    )
    taken = flipped(given, "nc", 1)
    block = shape((width + STAT_ROWS, LANES), BF16)
    blocks = call(merge_pair_kernel, [block] * group_size, [], [kept, taken], 16, step, "merge_pair", position)
    blocks = blocks[:1] + [flipped(blocks[d], group, d) for d in range(1, group_size)]
    parts = call(
        functools.partial(merge_group_kernel, group_size),
        [shape((rows, width + LANES), BF16)] * far,
        [pltpu.VMEM((block_size, width + LANES), F32)],
        blocks,
        16,
        step,
        "merge_group",
        position,
    )
    parts = parts[:1] + [flipped(parts[d], "wz", d) for d in range(1, far)]
    start = ((core * group_size + member) * far + layer) * rows
    own = lax.dynamic_slice_in_dim(latents, start, rows, 0)
    state = call(update_kernel, shape((rows, width), BF16), [], [own, w_out1] + parts, 16, step, "update")
    state = join([state] + [flipped(state, "wz", d) for d in range(1, far)], "join_far")
    state = join([state] + [flipped(state, group, d) for d in range(1, group_size)], "join_group")
    other = flipped(state, "nc", 1)
    span = 2 * plane_cells

    result = call(
        write_kernel,
        shape((cells, width), F32),
        [
            pltpu.VMEM((latent_count, width), BF16),
            pltpu.VMEM((HEADS, head_size + ONES_ROWS, latent_count), BF16),
            pltpu.VMEM((2, latent_count, span), F32),
            pltpu.VMEM((width, span), BF16),
            pltpu.VMEM((2, span, width), F32),
            pltpu.SemaphoreType.DMA((2,)),
        ],
        [state, other, query2_t, masked.reshape(cells, width), w_key2, w_value2, w_out2],
        32,
        20 * step,
        "write",
        out_space=pltpu.HBM,
    )
    return result.reshape(size_x, size_y, size_z, width)


def solution(mesh):
    wide, narrow = (mesh.shape[name] for name in ("wide", "narrow"))
    grid = Mesh(mesh.devices.reshape(wide // 2, 2, narrow // 2, 2), ("wz", "wx", "ny", "nc"))
    split = P(("wz", "wx"), ("ny", "nc"))
    return jax.shard_map(
        per_device,
        mesh=grid,
        in_specs=(split, split) + (P(),) * 10,
        out_specs=split,
        check_vma=False,
    )
```

```python
import functools
import math

import jax
import jax.numpy as jnp
from jax import lax
from jax.experimental import pallas as pl
from jax.experimental.pallas import tpu as pltpu
from jax.sharding import Mesh, PartitionSpec as P

HEADS = 8
LANES = 128
ONES_ROWS = 16
STAT_ROWS = 48
MIB = 1 << 20
F32 = jnp.float32
BF16 = jnp.bfloat16


def dot(left, right, contract=((1,), (0,))):
    return lax.dot_general(left, right, (contract, ((), ())), preferred_element_type=F32)


def masked_column(flow, mask_plane, i, j):
    size_z, width = flow.shape[2:]
    column = jnp.broadcast_to(mask_plane[:, j : j + 1], (size_z, LANES)).astype(BF16)
    tiles = [flow[i, j, :, k * LANES : (k + 1) * LANES] * column for k in range(width // LANES)]
    return jnp.concatenate(tiles, axis=1)


def face_kernel(flow, far_mask, first, second, low, high, mask, arrived):
    size_x, size_y = flow.shape[:2]
    copies = []
    for n, (j, target) in enumerate(((0, low), (size_y - 1, high))):
        copies.append(pltpu.make_async_copy(flow.at[:, pl.ds(j, 1)], target, arrived.at[n]))
        copies[-1].start()
    copies.append(pltpu.make_async_copy(far_mask, mask, arrived.at[2]))
    copies[-1].start()
    for copy in copies:
        copy.wait()
    odd = lax.axis_index("nc") == 1
    turned = jnp.concatenate([mask[:, 0, :], mask[:, size_y - 1, :]], axis=0).astype(F32).T
    for i in range(size_x):
        bottom = masked_column(low, turned[:, i:], i, 0)
        top = masked_column(high, turned[:, size_x + i :], i, 0)
        first[i] = jnp.where(odd, bottom, top)
        second[i] = jnp.where(odd, top, bottom)


def prepare_kernel(flow, mask, masked):
    size_x, size_y = flow.shape[:2]

    def plane(i, carry):
        turned = mask[i].astype(F32).T
        for j in range(size_y):
            masked[i, j] = masked_column(flow, turned, i, j)
        return carry

    lax.fori_loop(0, size_x, plane, 0)


def edge_kernel(masked, y_first, y_second, first, second):
    size_x, size_y = masked.shape[:2]
    outer = size_y + 1
    for face, plane in ((first, (size_x - 1) * (1 - lax.axis_index("wx"))), (second, (size_x - 1) * lax.axis_index("wx"))):
        face[1:outer] = masked[plane]
        face[outer * (1 - lax.axis_index("nc"))] = y_first[plane]
        face[outer * lax.axis_index("nc")] = y_second[plane]


def fill_row(padded, row, i, masked, y_first, y_second):
    outer = masked.shape[1] + 1
    padded[row, 1:outer] = masked[i].astype(F32)
    padded[row, outer * (1 - lax.axis_index("nc"))] = y_first[i].astype(F32)
    padded[row, outer * lax.axis_index("nc")] = y_second[i].astype(F32)


def stencil_plane(base, padded, conv, mixed, start):
    size_y, size_z, width = padded.shape[1] - 2, padded.shape[2], padded.shape[3]
    row_of = lax.broadcasted_iota(jnp.int32, (size_z, LANES), 0)
    for tile in range(width // LANES):
        lanes = slice(tile * LANES, (tile + 1) * LANES)
        taps = [jnp.broadcast_to(conv[n : n + 1, lanes], (size_z, LANES)) for n in range(27)]
        for j in range(size_y):
            sums = [None] * 3
            for a in range(3):
                for b in range(3):
                    window = padded[base + a, j + b, :, lanes]
                    for c in range(3):
                        term = window * taps[9 * a + 3 * b + c]
                        sums[c] = term if sums[c] is None else sums[c] + term
            below = jnp.where(row_of == 0, 0.0, pltpu.roll(sums[0], 1, 0))
            above = jnp.where(row_of == size_z - 1, 0.0, pltpu.roll(sums[2], size_z - 1, 0))
            total = padded[base + 1, j + 1, :, lanes] + sums[1] + below + above
            mixed[pl.ds(pl.multiple_of(start + j * size_z, size_z), size_z), lanes] = total.astype(BF16)


def project_plane(start, target, cells, mixed, weights, keys, values_t, query2_t):
    w_key1, w_value1, w_query2 = weights
    head_size = mixed.shape[1] // HEADS
    rows = pl.ds(pl.multiple_of(start, cells), cells)
    block = mixed[rows, :]
    keys[rows, :] = dot(block, w_key1[...]).astype(BF16)
    value_t = dot(w_value1[...], block, ((0,), (1,))).astype(BF16)
    values_t[:, :head_size, rows] = value_t.reshape(HEADS, head_size, cells)
    query2_t[:, pl.ds(pl.multiple_of(target, cells), cells)] = dot(w_query2[...], block, ((0,), (1,))).astype(BF16)


def latent_query_kernel(latents, w_query1, query1_t):
    query1_t[...] = dot(w_query1[...], latents[...], ((0,), (1,))).astype(BF16)


def inner_kernel(
    masked,
    y_first,
    y_second,
    conv,
    far_key1,
    far_value1,
    far_query2,
    keys,
    values_t,
    query2_t,
    padded,
    mixed,
    w_key1,
    w_value1,
    w_query2,
    arrived,
):
    size_x, size_y, size_z, width = masked.shape
    head_size = width // HEADS
    cells = size_y * size_z
    weights = (w_key1, w_value1, w_query2)
    copies = [
        pltpu.make_async_copy(source, target, arrived.at[n])
        for n, (source, target) in enumerate(zip((far_key1, far_value1, far_query2), weights))
    ]
    for copy in copies:
        copy.start()

    def fill(i, carry):
        fill_row(padded, i, i, masked, y_first, y_second)
        return carry

    lax.fori_loop(0, size_x, fill, 0)
    values_t[:, head_size:, :] = jnp.ones_like(values_t[:, head_size:, :])
    stencil_plane(0, padded, conv, mixed, 0)
    for copy in copies:
        copy.wait()

    def plane(i, carry):
        project_plane((i - 1) * cells, i * cells, cells, mixed, weights, keys, values_t, query2_t)
        stencil_plane(i, padded, conv, mixed, i * cells)
        return carry

    lax.fori_loop(1, size_x - 2, plane, 0)
    last = size_x - 3
    project_plane(last * cells, (last + 1) * cells, cells, mixed, weights, keys, values_t, query2_t)


def score_weights(query_t, head, columns):
    head_size = LANES // 2
    factor = 1.8 / math.sqrt(head_size) * math.log2(math.e)
    scaled = query_t[head * head_size : (head + 1) * head_size, columns].astype(F32) * factor
    high = scaled.astype(BF16)
    low = (scaled - high.astype(F32)).astype(BF16)
    blank = jnp.zeros_like(high)
    if head % 2 == 0:
        return jnp.concatenate([high, blank, low, blank], axis=0)
    return jnp.concatenate([blank, high, blank, low], axis=0)


def chunks_of(pieces, axis, chunk):
    found = []
    base = 0
    for piece in pieces:
        for part in range(piece.shape[axis] // chunk):
            found.append((piece, part * chunk, base))
            base += chunk
    return found


def score_chunk(place, head, right, chunk, scores, top):
    piece, start, base = place
    pair = head // 2
    left = piece[start : start + chunk, pair * LANES : (pair + 1) * LANES]
    found = dot(jnp.concatenate([left, left], axis=1), right)
    scores[head % 2, base : base + chunk, :] = found
    largest = jnp.max(found.reshape(chunk // 8, 8, found.shape[1]), axis=0)
    return largest if top is None else jnp.maximum(top, largest)


def sum_chunk(place, head, chunk, scores, top, total):
    piece, start, base = place
    weights = jnp.exp2(scores[head % 2, base : base + chunk, :] - top).astype(BF16)
    found = dot(piece[head, :, start : start + chunk], weights)
    return found if total is None else total + found


def attention_loop(keys, query_t, values_t, scores, chunk, columns_of, finish):
    width = scores.shape[2]
    blocks = query_t.shape[1] // width
    key_chunks, value_chunks = chunks_of(keys, 0, chunk), chunks_of(values_t, 2, chunk)

    def overall(top):
        return jnp.max(top, axis=0, keepdims=True)

    def first(block):
        right = score_weights(query_t, 0, columns_of(block))
        top = None
        for place in key_chunks:
            top = score_chunk(place, 0, right, chunk, scores, top)
        return overall(top)

    def step(block, top):
        for head in range(HEADS):
            following = block if head + 1 < HEADS else jnp.minimum(block + 1, blocks - 1)
            ahead = (head + 1) % HEADS
            right = score_weights(query_t, ahead, columns_of(following))
            upcoming = total = None
            for key_place, value_place in zip(key_chunks, value_chunks):
                upcoming = score_chunk(key_place, ahead, right, chunk, scores, upcoming)
                total = sum_chunk(value_place, head, chunk, scores, top, total)
            finish(head, block, total, top)
            top = overall(upcoming)
        return top

    lax.fori_loop(0, blocks, step, first(0))


def split3(value):
    high = value.astype(BF16).astype(F32)
    rest = value - high
    middle = rest.astype(BF16).astype(F32)
    return high, middle, rest - middle


def stat_rows(top, total):
    return split3(top) + split3(total)[:2]


def read_kernel(
    masked,
    x_first,
    x_second,
    y_first,
    y_second,
    conv,
    w_key1,
    w_value1,
    w_query2,
    inner_keys,
    inner_values_t,
    query1_t,
    inner_query2_t,
    query2_t,
    kept,
    given,
    padded,
    mixed,
    keys,
    values_t,
    scores,
    stats,
):
    size_x, size_y, size_z, width = masked.shape
    head_size = width // HEADS
    cells = size_y * size_z
    last = size_x - 1
    for row, i in ((1, 0), (2, 1), (3, last - 1), (4, last)):
        fill_row(padded, row, i, masked, y_first, y_second)
    padded[5 * (1 - lax.axis_index("wx"))] = x_first[...].astype(F32)
    padded[5 * lax.axis_index("wx")] = x_second[...].astype(F32)
    values_t[:, head_size:, :] = jnp.ones_like(values_t[:, head_size:, :])
    stats[...] = jnp.zeros_like(stats)

    weights = (w_key1, w_value1, w_query2)
    stencil_plane(0, padded, conv, mixed, 0)
    project_plane(0, 0, cells, mixed, weights, keys, values_t, query2_t)
    stencil_plane(3, padded, conv, mixed, cells)
    project_plane(cells, last * cells, cells, mixed, weights, keys, values_t, query2_t)

    core = lax.axis_index("nc")
    per_half = kept.shape[0]
    span = scores.shape[2]

    def columns_of(block):
        return pl.ds(pl.multiple_of((block ^ (1 - core)) * span, span), span)

    def finish(head, block, total, top):
        rows = slice(head * head_size, (head + 1) * head_size)

        def write(target):
            for k in range(per_half):
                target[k, rows, :] = total[:head_size, k * LANES : (k + 1) * LANES].astype(BF16)

        pl.when(block == 1)(lambda: write(kept))
        pl.when(block == 0)(lambda: write(given))
        for slot, row in enumerate(stat_rows(top, total[head_size : head_size + 1])):
            stats[slot * HEADS + head : slot * HEADS + head + 1, columns_of(block)] = row

    attention_loop(
        [inner_keys, keys], query1_t, [inner_values_t, values_t], scores, 256, columns_of, finish
    )
    for target, side in ((kept, core), (given, 1 - core)):
        for k in range(per_half):
            columns = pl.ds(pl.multiple_of((side * per_half + k) * LANES, LANES), LANES)
            target[k, width:, :] = stats[:, columns].astype(BF16)


def merge_blocks(blocks):
    width = blocks[0].shape[0] - STAT_ROWS
    head_size = width // HEADS
    slots = [[block[width + n * HEADS : width + (n + 1) * HEADS] for n in range(5)] for block in blocks]
    tops = [s[0] + s[1] + s[2] for s in slots]
    top = functools.reduce(jnp.maximum, tops)
    factors = [jnp.exp2(t - top) for t in tops]
    total = sum(f * (s[3] + s[4]) for f, s in zip(factors, slots))
    sums = []
    for head in range(HEADS):
        rows = slice(head * head_size, (head + 1) * head_size)
        sums.append(sum(block[rows] * f[head : head + 1] for block, f in zip(blocks, factors)))
    return sums, top, total


def all_stats(top, total, size):
    rows = list(stat_rows(top, total))
    filler = jnp.zeros((size - len(rows) * HEADS,) + top.shape[1:], F32)
    return jnp.concatenate(rows + [filler], axis=0)


def merge_pair_kernel(kept, taken, *outs):
    for distance, out in enumerate(outs):
        index = lax.axis_index(("wx", "ny")) ^ distance
        sums, top, total = merge_blocks([ref[index].astype(F32) for ref in (kept, taken)])
        sums.append(all_stats(top, total, STAT_ROWS))
        out[...] = jnp.concatenate(sums, axis=0).astype(BF16)


def merge_group_kernel(count, *refs):
    blocks, outs, turned = refs[:count], refs[count:-1], refs[-1]
    sums, top, total = merge_blocks([ref[...].astype(F32) for ref in blocks])
    width = turned.shape[1] - LANES
    sums = jnp.concatenate(sums, axis=0)
    for k in range(width // LANES):
        lanes = slice(k * LANES, (k + 1) * LANES)
        turned[:, lanes] = sums[lanes].T
    turned[:, width:] = all_stats(top, total, LANES).T
    rows = outs[0].shape[0]
    for distance, out in enumerate(outs):
        index = lax.axis_index("wz") ^ distance
        out[...] = turned[pl.ds(pl.multiple_of(index * rows, rows), rows), :].astype(BF16)


def unpack_stats(tile):
    parts = [tile] + [pltpu.roll(tile, LANES - slot * HEADS, 1) for slot in range(1, 5)]
    return parts[0] + parts[1] + parts[2], parts[3] + parts[4]


def spread(per_head, pair):
    rows = per_head.shape[0]
    lane = lax.broadcasted_iota(jnp.int32, (rows, LANES), 1)
    left = jnp.broadcast_to(per_head[:, 2 * pair : 2 * pair + 1], (rows, LANES))
    right = jnp.broadcast_to(per_head[:, 2 * pair + 1 : 2 * pair + 2], (rows, LANES))
    return jnp.where(lane < LANES // 2, left, right)


def update_kernel(own, w_out1, *refs):
    parts, out = refs[:-1], refs[-1]
    width = own.shape[1]
    stats = [unpack_stats(part[:, width:].astype(F32)) for part in parts]
    top = functools.reduce(jnp.maximum, [t for t, _ in stats])
    factors = [jnp.exp2(t - top) for t, _ in stats]
    total = sum(f * l for f, (_, l) in zip(factors, stats))
    read = []
    for pair in range(width // LANES):
        lanes = slice(pair * LANES, (pair + 1) * LANES)
        value = sum(part[:, lanes].astype(F32) * spread(f, pair) for part, f in zip(parts, factors))
        read.append(value / spread(total, pair))
    read = jnp.concatenate(read, axis=1).astype(BF16)
    out[...] = (own[...].astype(F32) + dot(read, w_out1[...])).astype(BF16)


def join_kernel(*refs):
    parts, out = refs[:-1], refs[-1]
    rows = parts[0].shape[0]
    for k, part in enumerate(parts):
        out[k * rows : (k + 1) * rows, :] = part[...]


def join(parts, name):
    rows, width = parts[0].shape
    out = jax.ShapeDtypeStruct((len(parts) * rows, width), parts[0].dtype)
    return call(join_kernel, out, [], parts, 8, 1e6, name)


def write_kernel(
    own_state,
    other_state,
    query2_t,
    masked,
    w_key2,
    w_value2,
    w_out2,
    out,
    keys,
    values_t,
    scores,
    read_t,
    buffers,
    sent,
):
    half, width = own_state.shape
    head_size = width // HEADS
    values_t[:, head_size:, :] = jnp.ones_like(values_t[:, head_size:, :])
    for side, state in enumerate((own_state, other_state)):
        rows = slice(side * half, (side + 1) * half)
        keys[rows, :] = dot(state[...], w_key2[...]).astype(BF16)
        value_t = dot(w_value2[...], state[...], ((0,), (1,))).astype(BF16)
        values_t[:, :head_size, rows] = value_t.reshape(HEADS, head_size, half)
    span = scores.shape[2]
    blocks = out.shape[0] // span

    def send(block):
        slot = block % 2
        rows = pl.ds(pl.multiple_of(block * span, span), span)
        return pltpu.make_async_copy(buffers.at[slot], out.at[rows, :], sent.at[slot])

    def columns_of(block):
        return pl.ds(pl.multiple_of(block * span, span), span)

    def finish(head, block, total, top):
        rows = slice(head * head_size, (head + 1) * head_size)
        read_t[rows, :] = (total[:head_size] / total[head_size : head_size + 1]).astype(BF16)
        if head == HEADS - 1:
            pl.when(block >= 2)(lambda: send(block - 2).wait())
            change = dot(read_t[...], w_out2[...], ((0,), (0,)))
            buffers[block % 2] = masked[columns_of(block), :].astype(F32) + change
            send(block).start()

    attention_loop([keys], query2_t, [values_t], scores, 256, columns_of, finish)
    for block in range(max(blocks - 2, 0), blocks):
        send(block).wait()


def call(kernel, shapes, scratch, operands, limit, flops, name, far=(), aliases=None, out_space=pltpu.VMEM):
    vmem = pl.BlockSpec(memory_space=pltpu.VMEM)
    hbm = pl.BlockSpec(memory_space=pltpu.HBM)
    many = isinstance(shapes, (list, tuple))
    in_specs = [hbm if n in far else vmem for n in range(len(operands))]
    moved = sum(x.size * x.dtype.itemsize for x in operands)
    result = pl.pallas_call(
        kernel,
        out_shape=shapes,
        in_specs=in_specs,
        out_specs=[vmem] * len(shapes) if many else pl.BlockSpec(memory_space=out_space),
        scratch_shapes=scratch,
        compiler_params=pltpu.CompilerParams(vmem_limit_bytes=limit * MIB),
        cost_estimate=pl.CostEstimate(flops=int(flops), bytes_accessed=moved, transcendentals=0),
        input_output_aliases=aliases or {},
        name=name,
    )(*operands)
    return list(result) if many else result


def pair_exchange(first, second, axis):
    count = lax.axis_size(axis)
    swaps = [[], []]
    for i in range(count - 1):
        swaps[i % 2] += [(i, i + 1), (i + 1, i)]
    other = lax.ppermute(second, axis, swaps[1])
    return lax.ppermute(first, axis, swaps[0]), other


def flipped(array, axis, distance):
    return lax.ppermute(array, axis, [(i, i ^ distance) for i in range(lax.axis_size(axis))])


def per_device(
    flow_field,
    fluid_mask,
    conv_weight,
    latents,
    w_query1,
    w_key1,
    w_value1,
    w_out1,
    w_query2,
    w_key2,
    w_value2,
    w_out2,
):
    size_x, size_y, size_z, width = flow_field.shape
    head_size = width // HEADS
    plane_cells = size_y * size_z
    inner_cells, outer_cells = (size_x - 2) * plane_cells, 2 * plane_cells
    cells = inner_cells + outer_cells
    latent_count = latents.shape[0]
    wide, narrow, group = ("wz", "wx"), ("ny", "nc"), ("wx", "ny")
    group_size = lax.axis_size(group)
    far = lax.axis_size("wz")
    core, member, layer = lax.axis_index("nc"), lax.axis_index(group), lax.axis_index("wz")
    block_size = latent_count // (2 * group_size)
    rows = block_size // far
    shape = jax.ShapeDtypeStruct
    step = 1e9

    side = shape((size_x, size_z, width), BF16)
    ends = pltpu.VMEM((size_x, 1, size_z, width), BF16)
    y_first, y_second = call(
        face_kernel,
        [side, side],
        [ends, ends, pltpu.VMEM(fluid_mask.shape, jnp.int32), pltpu.SemaphoreType.DMA((3,))],
        [flow_field, fluid_mask],
        56,
        step,
        "face",
        (0, 1),
    )
    y_first, y_second = pair_exchange(y_first, y_second, narrow)
    masked = call(
        prepare_kernel, shape(flow_field.shape, BF16), [], [flow_field, fluid_mask], 12, 2 * step, "prepare"
    )
    query1_t = call(
        latent_query_kernel,
        shape((width, latent_count), BF16),
        [],
        [latents, w_query1],
        12,
        2 * step,
        "latent_query",
    )
    side = shape((size_y + 2, size_z, width), BF16)
    x_first, x_second = call(
        edge_kernel, [side, side], [], [masked, y_first, y_second], 12, step, "edge"
    )
    x_first, x_second = pair_exchange(x_first, x_second, wide)
    weight = pltpu.VMEM((width, width), BF16)
    inner_keys, inner_values_t, query2_t = call(
        inner_kernel,
        [
            shape((inner_cells, width), BF16),
            shape((HEADS, head_size + ONES_ROWS, inner_cells), BF16),
            shape((width, cells), BF16),
        ],
        [
            pltpu.VMEM((size_x, size_y + 2, size_z, width), F32),
            pltpu.VMEM((inner_cells, width), BF16),
            weight,
            weight,
            weight,
            pltpu.SemaphoreType.DMA((3,)),
        ],
        [masked, y_first, y_second, conv_weight, w_key1, w_value1, w_query2],
        28,
        10 * step,
        "inner",
        (4, 5, 6),
    )
    query2_t, kept, given = call(
        read_kernel,
        [shape((width, cells), BF16)] + [shape((group_size, width + STAT_ROWS, LANES), BF16)] * 2,
        [
            pltpu.VMEM((6, size_y + 2, size_z, width), F32),
            pltpu.VMEM((outer_cells, width), BF16),
            pltpu.VMEM((outer_cells, width), BF16),
            pltpu.VMEM((HEADS, head_size + ONES_ROWS, outer_cells), BF16),
            pltpu.VMEM((2, cells, latent_count // 2), F32),
            pltpu.VMEM((STAT_ROWS, latent_count), F32),
        ],
        [
            masked,
            x_first,
            x_second,
            y_first,
            y_second,
            conv_weight,
            w_key1,
            w_value1,
            w_query2,
            inner_keys,
            inner_values_t,
            query1_t,
            query2_t,
        ],
        32,
        20 * step,
        "read",
        (),
        {12: 0},
    )
    taken = flipped(given, "nc", 1)
    block = shape((width + STAT_ROWS, LANES), BF16)
    blocks = call(merge_pair_kernel, [block] * group_size, [], [kept, taken], 16, step, "merge_pair")
    blocks = blocks[:1] + [flipped(blocks[d], group, d) for d in range(1, group_size)]
    parts = call(
        functools.partial(merge_group_kernel, group_size),
        [shape((rows, width + LANES), BF16)] * far,
        [pltpu.VMEM((block_size, width + LANES), F32)],
        blocks,
        16,
        step,
        "merge_group",
    )
    parts = parts[:1] + [flipped(parts[d], "wz", d) for d in range(1, far)]
    start = ((core * group_size + member) * far + layer) * rows
    own = lax.dynamic_slice_in_dim(latents, start, rows, 0)
    state = call(update_kernel, shape((rows, width), BF16), [], [own, w_out1] + parts, 16, step, "update")
    state = join([state] + [flipped(state, "wz", d) for d in range(1, far)], "join_far")
    state = join([state] + [flipped(state, group, d) for d in range(1, group_size)], "join_group")
    other = flipped(state, "nc", 1)
    span = 2 * plane_cells

    result = call(
        write_kernel,
        shape((cells, width), F32),
        [
            pltpu.VMEM((latent_count, width), BF16),
            pltpu.VMEM((HEADS, head_size + ONES_ROWS, latent_count), BF16),
            pltpu.VMEM((2, latent_count, span), F32),
            pltpu.VMEM((width, span), BF16),
            pltpu.VMEM((2, span, width), F32),
            pltpu.SemaphoreType.DMA((2,)),
        ],
        [state, other, query2_t, masked.reshape(cells, width), w_key2, w_value2, w_out2],
        32,
        20 * step,
        "write",
        out_space=pltpu.HBM,
    )
    return result.reshape(size_x, size_y, size_z, width)


def solution(mesh):
    wide, narrow = (mesh.shape[name] for name in ("wide", "narrow"))
    grid = Mesh(mesh.devices.reshape(wide // 2, 2, narrow // 2, 2), ("wz", "wx", "ny", "nc"))
    split = P(("wz", "wx"), ("ny", "nc"))
    return jax.shard_map(
        per_device,
        mesh=grid,
        in_specs=(split, split) + (P(),) * 10,
        out_specs=split,
        check_vma=False,
    )
```

```python
import functools
import math

import jax
import jax.numpy as jnp
from jax import lax
from jax.experimental import pallas as pl
from jax.experimental.pallas import tpu as pltpu
from jax.sharding import Mesh, PartitionSpec as P

HEADS = 8
LANES = 128
ONES_ROWS = 16
STAT_ROWS = 48
MIB = 1 << 20
F32 = jnp.float32
BF16 = jnp.bfloat16


def dot(left, right, contract=((1,), (0,))):
    return lax.dot_general(left, right, (contract, ((), ())), preferred_element_type=F32)


def masked_column(flow, mask_plane, i, j):
    size_z, width = flow.shape[2:]
    column = jnp.broadcast_to(mask_plane[:, j : j + 1], (size_z, LANES)).astype(BF16)
    tiles = [flow[i, j, :, k * LANES : (k + 1) * LANES] * column for k in range(width // LANES)]
    return jnp.concatenate(tiles, axis=1)


def face_kernel(flow, far_mask, first, second, low, high, mask, arrived):
    size_x, size_y = flow.shape[:2]
    copies = []
    for n, (j, target) in enumerate(((0, low), (size_y - 1, high))):
        copies.append(pltpu.make_async_copy(flow.at[:, pl.ds(j, 1)], target, arrived.at[n]))
        copies[-1].start()
    copies.append(pltpu.make_async_copy(far_mask, mask, arrived.at[2]))
    copies[-1].start()
    for copy in copies:
        copy.wait()
    odd = lax.axis_index("nc") == 1
    turned = jnp.concatenate([mask[:, 0, :], mask[:, size_y - 1, :]], axis=0).astype(F32).T
    for i in range(size_x):
        bottom = masked_column(low, turned[:, i:], i, 0)
        top = masked_column(high, turned[:, size_x + i :], i, 0)
        first[i] = jnp.where(odd, bottom, top)
        second[i] = jnp.where(odd, top, bottom)


def prepare_kernel(flow, mask, masked):
    size_x, size_y = flow.shape[:2]

    def plane(i, carry):
        turned = mask[i].astype(F32).T
        for j in range(size_y):
            masked[i, j] = masked_column(flow, turned, i, j)
        return carry

    lax.fori_loop(0, size_x, plane, 0)


def edge_kernel(masked, y_first, y_second, first, second):
    size_x, size_y = masked.shape[:2]
    outer = size_y + 1
    for face, plane in ((first, (size_x - 1) * (1 - lax.axis_index("wx"))), (second, (size_x - 1) * lax.axis_index("wx"))):
        face[1:outer] = masked[plane]
        face[outer * (1 - lax.axis_index("nc"))] = y_first[plane]
        face[outer * lax.axis_index("nc")] = y_second[plane]


def fill_row(padded, row, i, masked, y_first, y_second):
    outer = masked.shape[1] + 1
    padded[row, 1:outer] = masked[i].astype(F32)
    padded[row, outer * (1 - lax.axis_index("nc"))] = y_first[i].astype(F32)
    padded[row, outer * lax.axis_index("nc")] = y_second[i].astype(F32)


def stencil_plane(base, padded, conv, mixed, start):
    size_y, size_z, width = padded.shape[1] - 2, padded.shape[2], padded.shape[3]
    row_of = lax.broadcasted_iota(jnp.int32, (size_z, LANES), 0)
    for tile in range(width // LANES):
        lanes = slice(tile * LANES, (tile + 1) * LANES)
        taps = [jnp.broadcast_to(conv[n : n + 1, lanes], (size_z, LANES)) for n in range(27)]
        for j in range(size_y):
            sums = [None] * 3
            for a in range(3):
                for b in range(3):
                    window = padded[base + a, j + b, :, lanes]
                    for c in range(3):
                        term = window * taps[9 * a + 3 * b + c]
                        sums[c] = term if sums[c] is None else sums[c] + term
            below = jnp.where(row_of == 0, 0.0, pltpu.roll(sums[0], 1, 0))
            above = jnp.where(row_of == size_z - 1, 0.0, pltpu.roll(sums[2], size_z - 1, 0))
            total = padded[base + 1, j + 1, :, lanes] + sums[1] + below + above
            mixed[pl.ds(pl.multiple_of(start + j * size_z, size_z), size_z), lanes] = total.astype(BF16)


def project_plane(start, target, cells, mixed, weights, keys, values_t, query2_t):
    w_key1, w_value1, w_query2 = weights
    head_size = mixed.shape[1] // HEADS
    rows = pl.ds(pl.multiple_of(start, cells), cells)
    block = mixed[rows, :]
    keys[rows, :] = dot(block, w_key1[...]).astype(BF16)
    value_t = dot(w_value1[...], block, ((0,), (1,))).astype(BF16)
    values_t[:, :head_size, rows] = value_t.reshape(HEADS, head_size, cells)
    query2_t[:, pl.ds(pl.multiple_of(target, cells), cells)] = dot(w_query2[...], block, ((0,), (1,))).astype(BF16)


def latent_query_kernel(latents, w_query1, query1_t):
    query1_t[...] = dot(w_query1[...], latents[...], ((0,), (1,))).astype(BF16)


def inner_kernel(
    masked,
    y_first,
    y_second,
    conv,
    far_key1,
    far_value1,
    far_query2,
    keys,
    values_t,
    query2_t,
    padded,
    mixed,
    w_key1,
    w_value1,
    w_query2,
    arrived,
):
    size_x, size_y, size_z, width = masked.shape
    head_size = width // HEADS
    cells = size_y * size_z
    weights = (w_key1, w_value1, w_query2)
    copies = [
        pltpu.make_async_copy(source, target, arrived.at[n])
        for n, (source, target) in enumerate(zip((far_key1, far_value1, far_query2), weights))
    ]
    for copy in copies:
        copy.start()

    def fill(i, carry):
        fill_row(padded, i, i, masked, y_first, y_second)
        return carry

    lax.fori_loop(0, size_x, fill, 0)
    values_t[:, head_size:, :] = jnp.ones_like(values_t[:, head_size:, :])
    stencil_plane(0, padded, conv, mixed, 0)
    for copy in copies:
        copy.wait()

    def plane(i, carry):
        project_plane((i - 1) * cells, i * cells, cells, mixed, weights, keys, values_t, query2_t)
        stencil_plane(i, padded, conv, mixed, i * cells)
        return carry

    lax.fori_loop(1, size_x - 2, plane, 0)
    last = size_x - 3
    project_plane(last * cells, (last + 1) * cells, cells, mixed, weights, keys, values_t, query2_t)


def score_weights(query_t, head, columns):
    head_size = LANES // 2
    factor = 1.8 / math.sqrt(head_size) * math.log2(math.e)
    scaled = query_t[head * head_size : (head + 1) * head_size, columns].astype(F32) * factor
    high = scaled.astype(BF16)
    low = (scaled - high.astype(F32)).astype(BF16)
    blank = jnp.zeros_like(high)
    if head % 2 == 0:
        return jnp.concatenate([high, blank, low, blank], axis=0)
    return jnp.concatenate([blank, high, blank, low], axis=0)


def chunks_of(pieces, axis, chunk):
    found = []
    base = 0
    for piece in pieces:
        for part in range(piece.shape[axis] // chunk):
            found.append((piece, part * chunk, base))
            base += chunk
    return found


def score_chunk(place, head, right, chunk, scores, top):
    piece, start, base = place
    pair = head // 2
    left = piece[start : start + chunk, pair * LANES : (pair + 1) * LANES]
    found = dot(jnp.concatenate([left, left], axis=1), right)
    scores[head % 2, base : base + chunk, :] = found
    largest = jnp.max(found.reshape(chunk // 8, 8, found.shape[1]), axis=0)
    return largest if top is None else jnp.maximum(top, largest)


def sum_chunk(place, head, chunk, scores, top, total):
    piece, start, base = place
    weights = jnp.exp2(scores[head % 2, base : base + chunk, :] - top).astype(BF16)
    found = dot(piece[head, :, start : start + chunk], weights)
    return found if total is None else total + found


def attention_loop(keys, query_t, values_t, scores, chunk, blocks, columns_of, finish):
    key_chunks, value_chunks = chunks_of(keys, 0, chunk), chunks_of(values_t, 2, chunk)

    def overall(top):
        return jnp.max(top, axis=0, keepdims=True)

    def first(block):
        right = score_weights(query_t, 0, columns_of(block))
        top = None
        for place in key_chunks:
            top = score_chunk(place, 0, right, chunk, scores, top)
        return overall(top)

    def step(block, top):
        for head in range(HEADS):
            ahead = (head + 1) % HEADS
            wanted = ahead > 0 or blocks > 1
            following = block if ahead else jnp.minimum(block + 1, blocks - 1)
            right = score_weights(query_t, ahead, columns_of(following)) if wanted else None
            upcoming = total = None
            for key_place, value_place in zip(key_chunks, value_chunks):
                if wanted:
                    upcoming = score_chunk(key_place, ahead, right, chunk, scores, upcoming)
                total = sum_chunk(value_place, head, chunk, scores, top, total)
            finish(head, block, total, top)
            top = overall(upcoming) if wanted else top
        return top

    if blocks == 1:
        step(0, first(0))
    else:
        lax.fori_loop(0, blocks, step, first(0))


def split3(value):
    high = value.astype(BF16).astype(F32)
    rest = value - high
    middle = rest.astype(BF16).astype(F32)
    return high, middle, rest - middle


def stat_rows(top, total):
    return split3(top) + split3(total)[:2]


def half_attention(side, keys, values_t, query1_t, target, scores, stats):
    per_half = target.shape[0]
    span = scores.shape[2]
    head_size = query1_t.shape[0] // HEADS
    width = query1_t.shape[0]
    columns = pl.ds(pl.multiple_of(side * span, span), span)

    def finish(head, block, total, top):
        rows = slice(head * head_size, (head + 1) * head_size)
        for k in range(per_half):
            target[k, rows, :] = total[:head_size, k * LANES : (k + 1) * LANES].astype(BF16)
        for slot, row in enumerate(stat_rows(top, total[head_size : head_size + 1])):
            stats[slot * HEADS + head : slot * HEADS + head + 1, :] = row

    attention_loop(keys, query1_t, values_t, scores, 256, 1, lambda block: columns, finish)
    for k in range(per_half):
        target[k, width:, :] = stats[:, k * LANES : (k + 1) * LANES].astype(BF16)


def read_kernel(
    masked,
    x_first,
    x_second,
    y_first,
    y_second,
    conv,
    w_key1,
    w_value1,
    w_query2,
    inner_keys,
    inner_values_t,
    query1_t,
    inner_query2_t,
    query2_t,
    given,
    keys,
    values_t,
    padded,
    mixed,
    scores,
    stats,
):
    size_x, size_y, size_z, width = masked.shape
    head_size = width // HEADS
    cells = size_y * size_z
    last = size_x - 1
    for row, i in ((1, 0), (2, 1), (3, last - 1), (4, last)):
        fill_row(padded, row, i, masked, y_first, y_second)
    padded[5 * (1 - lax.axis_index("wx"))] = x_first[...].astype(F32)
    padded[5 * lax.axis_index("wx")] = x_second[...].astype(F32)
    values_t[:, head_size:, :] = jnp.ones_like(values_t[:, head_size:, :])
    stats[...] = jnp.zeros_like(stats)

    weights = (w_key1, w_value1, w_query2)
    stencil_plane(0, padded, conv, mixed, 0)
    project_plane(0, 0, cells, mixed, weights, keys, values_t, query2_t)
    stencil_plane(3, padded, conv, mixed, cells)
    project_plane(cells, last * cells, cells, mixed, weights, keys, values_t, query2_t)

    side = 1 - lax.axis_index("nc")
    half_attention(side, [inner_keys, keys], [inner_values_t, values_t], query1_t, given, scores, stats)


def keep_kernel(inner_keys, keys, inner_values_t, values_t, query1_t, kept, scores, stats):
    side = lax.axis_index("nc")
    stats[...] = jnp.zeros_like(stats)
    half_attention(side, [inner_keys, keys], [inner_values_t, values_t], query1_t, kept, scores, stats)


def merge_blocks(blocks):
    width = blocks[0].shape[0] - STAT_ROWS
    head_size = width // HEADS
    slots = [[block[width + n * HEADS : width + (n + 1) * HEADS] for n in range(5)] for block in blocks]
    tops = [s[0] + s[1] + s[2] for s in slots]
    top = functools.reduce(jnp.maximum, tops)
    factors = [jnp.exp2(t - top) for t in tops]
    total = sum(f * (s[3] + s[4]) for f, s in zip(factors, slots))
    sums = []
    for head in range(HEADS):
        rows = slice(head * head_size, (head + 1) * head_size)
        sums.append(sum(block[rows] * f[head : head + 1] for block, f in zip(blocks, factors)))
    return sums, top, total


def all_stats(top, total, size):
    rows = list(stat_rows(top, total))
    filler = jnp.zeros((size - len(rows) * HEADS,) + top.shape[1:], F32)
    return jnp.concatenate(rows + [filler], axis=0)


def merge_pair_kernel(kept, taken, *outs):
    for distance, out in enumerate(outs):
        index = lax.axis_index(("wx", "ny")) ^ distance
        sums, top, total = merge_blocks([ref[index].astype(F32) for ref in (kept, taken)])
        sums.append(all_stats(top, total, STAT_ROWS))
        out[...] = jnp.concatenate(sums, axis=0).astype(BF16)


def merge_group_kernel(count, *refs):
    blocks, outs, turned = refs[:count], refs[count:-1], refs[-1]
    sums, top, total = merge_blocks([ref[...].astype(F32) for ref in blocks])
    width = turned.shape[1] - LANES
    sums = jnp.concatenate(sums, axis=0)
    for k in range(width // LANES):
        lanes = slice(k * LANES, (k + 1) * LANES)
        turned[:, lanes] = sums[lanes].T
    turned[:, width:] = all_stats(top, total, LANES).T
    rows = outs[0].shape[0]
    for distance, out in enumerate(outs):
        index = lax.axis_index("wz") ^ distance
        out[...] = turned[pl.ds(pl.multiple_of(index * rows, rows), rows), :].astype(BF16)


def unpack_stats(tile):
    parts = [tile] + [pltpu.roll(tile, LANES - slot * HEADS, 1) for slot in range(1, 5)]
    return parts[0] + parts[1] + parts[2], parts[3] + parts[4]


def spread(per_head, pair):
    rows = per_head.shape[0]
    lane = lax.broadcasted_iota(jnp.int32, (rows, LANES), 1)
    left = jnp.broadcast_to(per_head[:, 2 * pair : 2 * pair + 1], (rows, LANES))
    right = jnp.broadcast_to(per_head[:, 2 * pair + 1 : 2 * pair + 2], (rows, LANES))
    return jnp.where(lane < LANES // 2, left, right)


def update_kernel(own, w_out1, *refs):
    parts, out = refs[:-1], refs[-1]
    width = own.shape[1]
    stats = [unpack_stats(part[:, width:].astype(F32)) for part in parts]
    top = functools.reduce(jnp.maximum, [t for t, _ in stats])
    factors = [jnp.exp2(t - top) for t, _ in stats]
    total = sum(f * l for f, (_, l) in zip(factors, stats))
    read = []
    for pair in range(width // LANES):
        lanes = slice(pair * LANES, (pair + 1) * LANES)
        value = sum(part[:, lanes].astype(F32) * spread(f, pair) for part, f in zip(parts, factors))
        read.append(value / spread(total, pair))
    read = jnp.concatenate(read, axis=1).astype(BF16)
    out[...] = (own[...].astype(F32) + dot(read, w_out1[...])).astype(BF16)


def join_kernel(*refs):
    parts, out = refs[:-1], refs[-1]
    rows = parts[0].shape[0]
    for k, part in enumerate(parts):
        out[k * rows : (k + 1) * rows, :] = part[...]


def join(parts, name):
    rows, width = parts[0].shape
    out = jax.ShapeDtypeStruct((len(parts) * rows, width), parts[0].dtype)
    return call(join_kernel, out, [], parts, 8, 1e6, name)


def write_kernel(
    own_state,
    other_state,
    query2_t,
    masked,
    w_key2,
    w_value2,
    w_out2,
    out,
    keys,
    values_t,
    scores,
    read_t,
    buffers,
    sent,
):
    half, width = own_state.shape
    head_size = width // HEADS
    values_t[:, head_size:, :] = jnp.ones_like(values_t[:, head_size:, :])
    for side, state in enumerate((own_state, other_state)):
        rows = slice(side * half, (side + 1) * half)
        keys[rows, :] = dot(state[...], w_key2[...]).astype(BF16)
        value_t = dot(w_value2[...], state[...], ((0,), (1,))).astype(BF16)
        values_t[:, :head_size, rows] = value_t.reshape(HEADS, head_size, half)
    span = scores.shape[2]
    blocks = out.shape[0] // span

    def send(block):
        slot = block % 2
        rows = pl.ds(pl.multiple_of(block * span, span), span)
        return pltpu.make_async_copy(buffers.at[slot], out.at[rows, :], sent.at[slot])

    def columns_of(block):
        return pl.ds(pl.multiple_of(block * span, span), span)

    def finish(head, block, total, top):
        rows = slice(head * head_size, (head + 1) * head_size)
        inverse = 1.0 / total[head_size : head_size + 1]
        read_t[rows, :] = (total[:head_size] * inverse).astype(BF16)
        if head == HEADS - 1:
            pl.when(block >= 2)(lambda: send(block - 2).wait())
            change = dot(read_t[...], w_out2[...], ((0,), (0,)))
            buffers[block % 2] = masked[columns_of(block), :].astype(F32) + change
            send(block).start()

    attention_loop([keys], query2_t, [values_t], scores, 256, blocks, columns_of, finish)
    for block in range(max(blocks - 2, 0), blocks):
        send(block).wait()


def call(kernel, shapes, scratch, operands, limit, flops, name, far=(), aliases=None, out_space=pltpu.VMEM):
    vmem = pl.BlockSpec(memory_space=pltpu.VMEM)
    hbm = pl.BlockSpec(memory_space=pltpu.HBM)
    many = isinstance(shapes, (list, tuple))
    in_specs = [hbm if n in far else vmem for n in range(len(operands))]
    moved = sum(x.size * x.dtype.itemsize for x in operands)
    result = pl.pallas_call(
        kernel,
        out_shape=shapes,
        in_specs=in_specs,
        out_specs=[vmem] * len(shapes) if many else pl.BlockSpec(memory_space=out_space),
        scratch_shapes=scratch,
        compiler_params=pltpu.CompilerParams(vmem_limit_bytes=limit * MIB),
        cost_estimate=pl.CostEstimate(flops=int(flops), bytes_accessed=moved, transcendentals=0),
        input_output_aliases=aliases or {},
        name=name,
    )(*operands)
    return list(result) if many else result


def pair_exchange(first, second, axis):
    count = lax.axis_size(axis)
    swaps = [[], []]
    for i in range(count - 1):
        swaps[i % 2] += [(i, i + 1), (i + 1, i)]
    other = lax.ppermute(second, axis, swaps[1])
    return lax.ppermute(first, axis, swaps[0]), other


def flipped(array, axis, distance):
    return lax.ppermute(array, axis, [(i, i ^ distance) for i in range(lax.axis_size(axis))])


def per_device(
    flow_field,
    fluid_mask,
    conv_weight,
    latents,
    w_query1,
    w_key1,
    w_value1,
    w_out1,
    w_query2,
    w_key2,
    w_value2,
    w_out2,
):
    size_x, size_y, size_z, width = flow_field.shape
    head_size = width // HEADS
    plane_cells = size_y * size_z
    inner_cells, outer_cells = (size_x - 2) * plane_cells, 2 * plane_cells
    cells = inner_cells + outer_cells
    latent_count = latents.shape[0]
    wide, narrow, group = ("wz", "wx"), ("ny", "nc"), ("wx", "ny")
    group_size = lax.axis_size(group)
    far = lax.axis_size("wz")
    core, member, layer = lax.axis_index("nc"), lax.axis_index(group), lax.axis_index("wz")
    block_size = latent_count // (2 * group_size)
    rows = block_size // far
    shape = jax.ShapeDtypeStruct
    step = 1e9

    side = shape((size_x, size_z, width), BF16)
    ends = pltpu.VMEM((size_x, 1, size_z, width), BF16)
    y_first, y_second = call(
        face_kernel,
        [side, side],
        [ends, ends, pltpu.VMEM(fluid_mask.shape, jnp.int32), pltpu.SemaphoreType.DMA((3,))],
        [flow_field, fluid_mask],
        56,
        step,
        "face",
        (0, 1),
    )
    y_first, y_second = pair_exchange(y_first, y_second, narrow)
    masked = call(
        prepare_kernel, shape(flow_field.shape, BF16), [], [flow_field, fluid_mask], 12, 2 * step, "prepare"
    )
    query1_t = call(
        latent_query_kernel,
        shape((width, latent_count), BF16),
        [],
        [latents, w_query1],
        12,
        2 * step,
        "latent_query",
    )
    side = shape((size_y + 2, size_z, width), BF16)
    x_first, x_second = call(
        edge_kernel, [side, side], [], [masked, y_first, y_second], 12, step, "edge"
    )
    x_first, x_second = pair_exchange(x_first, x_second, wide)
    weight = pltpu.VMEM((width, width), BF16)
    inner_keys, inner_values_t, query2_t = call(
        inner_kernel,
        [
            shape((inner_cells, width), BF16),
            shape((HEADS, head_size + ONES_ROWS, inner_cells), BF16),
            shape((width, cells), BF16),
        ],
        [
            pltpu.VMEM((size_x, size_y + 2, size_z, width), F32),
            pltpu.VMEM((inner_cells, width), BF16),
            weight,
            weight,
            weight,
            pltpu.SemaphoreType.DMA((3,)),
        ],
        [masked, y_first, y_second, conv_weight, w_key1, w_value1, w_query2],
        28,
        10 * step,
        "inner",
        (4, 5, 6),
    )
    part = shape((group_size, width + STAT_ROWS, LANES), BF16)
    partial_scratch = [
        pltpu.VMEM((2, cells, latent_count // 2), F32),
        pltpu.VMEM((STAT_ROWS, latent_count // 2), F32),
    ]
    query2_t, given, outer_keys, outer_values_t = call(
        read_kernel,
        [
            shape((width, cells), BF16),
            part,
            shape((outer_cells, width), BF16),
            shape((HEADS, head_size + ONES_ROWS, outer_cells), BF16),
        ],
        [
            pltpu.VMEM((6, size_y + 2, size_z, width), F32),
            pltpu.VMEM((outer_cells, width), BF16),
        ]
        + partial_scratch,
        [
            masked,
            x_first,
            x_second,
            y_first,
            y_second,
            conv_weight,
            w_key1,
            w_value1,
            w_query2,
            inner_keys,
            inner_values_t,
            query1_t,
            query2_t,
        ],
        32,
        20 * step,
        "read",
        (),
        {12: 0},
    )
    taken = flipped(given, "nc", 1)
    kept = call(
        keep_kernel,
        part,
        partial_scratch,
        [inner_keys, outer_keys, inner_values_t, outer_values_t, query1_t],
        24,
        10 * step,
        "keep",
    )
    block = shape((width + STAT_ROWS, LANES), BF16)
    blocks = call(merge_pair_kernel, [block] * group_size, [], [kept, taken], 16, step, "merge_pair")
    blocks = [flipped(blocks[d], group, d) for d in range(group_size - 1, 0, -1)] + blocks[:1]
    parts = call(
        functools.partial(merge_group_kernel, group_size),
        [shape((rows, width + LANES), BF16)] * far,
        [pltpu.VMEM((block_size, width + LANES), F32)],
        blocks,
        16,
        step,
        "merge_group",
    )
    order = list(range(far - 2, 0, -1)) + [far - 1]
    parts = [flipped(parts[d], "wz", d) for d in order] + parts[:1]
    start = ((core * group_size + member) * far + layer) * rows
    own = lax.dynamic_slice_in_dim(latents, start, rows, 0)
    state = call(update_kernel, shape((rows, width), BF16), [], [own, w_out1] + parts, 16, step, "update")
    state = join([flipped(state, "wz", d) for d in range(far - 1, 0, -1)] + [state], "join_far")
    state = join([flipped(state, group, d) for d in range(group_size - 1, 0, -1)] + [state], "join_group")
    other = flipped(state, "nc", 1)
    span = 2 * plane_cells

    result = call(
        write_kernel,
        shape((cells, width), F32),
        [
            pltpu.VMEM((latent_count, width), BF16),
            pltpu.VMEM((HEADS, head_size + ONES_ROWS, latent_count), BF16),
            pltpu.VMEM((2, latent_count, span), F32),
            pltpu.VMEM((width, span), BF16),
            pltpu.VMEM((2, span, width), F32),
            pltpu.SemaphoreType.DMA((2,)),
        ],
        [state, other, query2_t, masked.reshape(cells, width), w_key2, w_value2, w_out2],
        32,
        20 * step,
        "write",
        out_space=pltpu.HBM,
    )
    return result.reshape(size_x, size_y, size_z, width)


def solution(mesh):
    wide, narrow = (mesh.shape[name] for name in ("wide", "narrow"))
    grid = Mesh(mesh.devices.reshape(wide // 2, 2, narrow // 2, 2), ("wz", "wx", "ny", "nc"))
    split = P(("wz", "wx"), ("ny", "nc"))
    return jax.shard_map(
        per_device,
        mesh=grid,
        in_specs=(split, split) + (P(),) * 10,
        out_specs=split,
        check_vma=False,
    )
```

```python
import functools
import math

import jax
import jax.numpy as jnp
from jax import lax
from jax.experimental import pallas as pl
from jax.experimental.pallas import tpu as pltpu
from jax.sharding import Mesh, PartitionSpec as P

HEADS = 8
LANES = 128
ONES_ROWS = 16
STAT_ROWS = 48
MIB = 1 << 20
F32 = jnp.float32
BF16 = jnp.bfloat16


def dot(left, right, contract=((1,), (0,))):
    return lax.dot_general(left, right, (contract, ((), ())), preferred_element_type=F32)


def masked_column(flow, mask_plane, i, j):
    size_z, width = flow.shape[2:]
    column = jnp.broadcast_to(mask_plane[:, j : j + 1], (size_z, LANES)).astype(BF16)
    tiles = [flow[i, j, :, k * LANES : (k + 1) * LANES] * column for k in range(width // LANES)]
    return jnp.concatenate(tiles, axis=1)


def face_kernel(flow, far_mask, first, second, low, high, mask, arrived):
    size_x, size_y = flow.shape[:2]
    copies = []
    for n, (j, target) in enumerate(((0, low), (size_y - 1, high))):
        copies.append(pltpu.make_async_copy(flow.at[:, pl.ds(j, 1)], target, arrived.at[n]))
        copies[-1].start()
    copies.append(pltpu.make_async_copy(far_mask, mask, arrived.at[2]))
    copies[-1].start()
    for copy in copies:
        copy.wait()
    odd = lax.axis_index("nc") == 1
    turned = jnp.concatenate([mask[:, 0, :], mask[:, size_y - 1, :]], axis=0).astype(F32).T
    for i in range(size_x):
        bottom = masked_column(low, turned[:, i:], i, 0)
        top = masked_column(high, turned[:, size_x + i :], i, 0)
        first[i] = jnp.where(odd, bottom, top)
        second[i] = jnp.where(odd, top, bottom)


def prepare_kernel(flow, mask, masked):
    size_x, size_y = flow.shape[:2]

    def plane(i, carry):
        turned = mask[i].astype(F32).T
        for j in range(size_y):
            masked[i, j] = masked_column(flow, turned, i, j)
        return carry

    lax.fori_loop(0, size_x, plane, 0)


def edge_kernel(masked, y_first, y_second, first, second):
    size_x, size_y = masked.shape[:2]
    outer = size_y + 1
    for face, plane in ((first, (size_x - 1) * (1 - lax.axis_index("wx"))), (second, (size_x - 1) * lax.axis_index("wx"))):
        face[1:outer] = masked[plane]
        face[outer * (1 - lax.axis_index("nc"))] = y_first[plane]
        face[outer * lax.axis_index("nc")] = y_second[plane]


def fill_row(padded, row, i, masked, y_first, y_second):
    outer = masked.shape[1] + 1
    padded[row, 1:outer] = masked[i].astype(F32)
    padded[row, outer * (1 - lax.axis_index("nc"))] = y_first[i].astype(F32)
    padded[row, outer * lax.axis_index("nc")] = y_second[i].astype(F32)


def stencil_plane(base, padded, conv, mixed, start):
    size_y, size_z, width = padded.shape[1] - 2, padded.shape[2], padded.shape[3]
    row_of = lax.broadcasted_iota(jnp.int32, (size_z, LANES), 0)
    for tile in range(width // LANES):
        lanes = slice(tile * LANES, (tile + 1) * LANES)
        taps = [jnp.broadcast_to(conv[n : n + 1, lanes], (size_z, LANES)) for n in range(27)]
        for j in range(size_y):
            sums = [None] * 3
            for a in range(3):
                for b in range(3):
                    window = padded[base + a, j + b, :, lanes]
                    for c in range(3):
                        term = window * taps[9 * a + 3 * b + c]
                        sums[c] = term if sums[c] is None else sums[c] + term
            below = jnp.where(row_of == 0, 0.0, pltpu.roll(sums[0], 1, 0))
            above = jnp.where(row_of == size_z - 1, 0.0, pltpu.roll(sums[2], size_z - 1, 0))
            total = padded[base + 1, j + 1, :, lanes] + sums[1] + below + above
            mixed[pl.ds(pl.multiple_of(start + j * size_z, size_z), size_z), lanes] = total.astype(BF16)


def project_plane(start, target, cells, mixed, weights, keys, values_t, query2_t):
    w_key1, w_value1, w_query2 = weights
    head_size = mixed.shape[1] // HEADS
    rows = pl.ds(pl.multiple_of(start, cells), cells)
    block = mixed[rows, :]
    keys[rows, :] = dot(block, w_key1[...]).astype(BF16)
    value_t = dot(w_value1[...], block, ((0,), (1,))).astype(BF16)
    values_t[:, :head_size, rows] = value_t.reshape(HEADS, head_size, cells)
    query2_t[:, pl.ds(pl.multiple_of(target, cells), cells)] = dot(w_query2[...], block, ((0,), (1,))).astype(BF16)


def latent_query_kernel(latents, w_query1, query1_t):
    query1_t[...] = dot(w_query1[...], latents[...], ((0,), (1,))).astype(BF16)


def inner_kernel(
    masked,
    y_first,
    y_second,
    conv,
    far_key1,
    far_value1,
    far_query2,
    keys,
    values_t,
    query2_t,
    padded,
    mixed,
    w_key1,
    w_value1,
    w_query2,
    arrived,
):
    size_x, size_y, size_z, width = masked.shape
    head_size = width // HEADS
    cells = size_y * size_z
    weights = (w_key1, w_value1, w_query2)
    copies = [
        pltpu.make_async_copy(source, target, arrived.at[n])
        for n, (source, target) in enumerate(zip((far_key1, far_value1, far_query2), weights))
    ]
    for copy in copies:
        copy.start()

    def fill(i, carry):
        fill_row(padded, i, i, masked, y_first, y_second)
        return carry

    lax.fori_loop(0, size_x, fill, 0)
    values_t[:, head_size:, :] = jnp.ones_like(values_t[:, head_size:, :])
    for copy in copies:
        copy.wait()

    def plane(i, carry):
        stencil_plane(i, padded, conv, mixed, i * cells)
        project_plane(i * cells, (i + 1) * cells, cells, mixed, weights, keys, values_t, query2_t)
        return carry

    lax.fori_loop(0, size_x - 2, plane, 0)


def score_weights(query_t, head, columns):
    head_size = LANES // 2
    factor = 1.8 / math.sqrt(head_size) * math.log2(math.e)
    scaled = query_t[head * head_size : (head + 1) * head_size, columns].astype(F32) * factor
    high = scaled.astype(BF16)
    low = (scaled - high.astype(F32)).astype(BF16)
    blank = jnp.zeros_like(high)
    if head % 2 == 0:
        return jnp.concatenate([high, blank, low, blank], axis=0)
    return jnp.concatenate([blank, high, blank, low], axis=0)


def chunks_of(pieces, axis, chunk):
    found = []
    base = 0
    for piece in pieces:
        for part in range(piece.shape[axis] // chunk):
            found.append((piece, part * chunk, base))
            base += chunk
    return found


def score_chunk(place, head, right, chunk, scores, top):
    piece, start, base = place
    pair = head // 2
    left = piece[start : start + chunk, pair * LANES : (pair + 1) * LANES]
    found = dot(jnp.concatenate([left, left], axis=1), right)
    scores[head % 2, base : base + chunk, :] = found
    largest = jnp.max(found.reshape(chunk // 8, 8, found.shape[1]), axis=0)
    return largest if top is None else jnp.maximum(top, largest)


def sum_chunk(place, head, chunk, scores, top, total):
    piece, start, base = place
    weights = jnp.exp2(scores[head % 2, base : base + chunk, :] - top).astype(BF16)
    found = dot(piece[head, :, start : start + chunk], weights)
    return found if total is None else total + found


def attention_loop(keys, query_t, values_t, scores, chunk, blocks, columns_of, finish):
    key_chunks, value_chunks = chunks_of(keys, 0, chunk), chunks_of(values_t, 2, chunk)

    def overall(top):
        return jnp.max(top, axis=0, keepdims=True)

    def first(block):
        right = score_weights(query_t, 0, columns_of(block))
        top = None
        for place in key_chunks:
            top = score_chunk(place, 0, right, chunk, scores, top)
        return overall(top)

    def step(block, top):
        for head in range(HEADS):
            ahead = (head + 1) % HEADS
            following = block if ahead else jnp.minimum(block + 1, blocks - 1)
            right = score_weights(query_t, ahead, columns_of(following))
            upcoming = total = None
            for key_place, value_place in zip(key_chunks, value_chunks):
                upcoming = score_chunk(key_place, ahead, right, chunk, scores, upcoming)
                total = sum_chunk(value_place, head, chunk, scores, top, total)
            finish(head, block, total, top)
            top = overall(upcoming)
        return top

    lax.fori_loop(0, blocks, step, first(0))


def split3(value):
    high = value.astype(BF16).astype(F32)
    rest = value - high
    middle = rest.astype(BF16).astype(F32)
    return high, middle, rest - middle


def stat_rows(top, total):
    return split3(top) + split3(total)[:2]


def read_kernel(
    masked,
    x_first,
    x_second,
    y_first,
    y_second,
    conv,
    w_key1,
    w_value1,
    w_query2,
    inner_keys,
    inner_values_t,
    query1_t,
    inner_query2_t,
    query2_t,
    kept,
    given,
    padded,
    mixed,
    keys,
    values_t,
    scores,
    stats,
):
    size_x, size_y, size_z, width = masked.shape
    head_size = width // HEADS
    cells = size_y * size_z
    last = size_x - 1
    for row, i in ((1, 0), (2, 1), (3, last - 1), (4, last)):
        fill_row(padded, row, i, masked, y_first, y_second)
    padded[5 * (1 - lax.axis_index("wx"))] = x_first[...].astype(F32)
    padded[5 * lax.axis_index("wx")] = x_second[...].astype(F32)
    values_t[:, head_size:, :] = jnp.ones_like(values_t[:, head_size:, :])
    stats[...] = jnp.zeros_like(stats)

    weights = (w_key1, w_value1, w_query2)

    def plane(i, carry):
        stencil_plane(3 * i, padded, conv, mixed, i * cells)
        project_plane(i * cells, i * last * cells, cells, mixed, weights, keys, values_t, query2_t)
        return carry

    lax.fori_loop(0, 2, plane, 0)

    core = lax.axis_index("nc")
    per_half = kept.shape[0]
    span = scores.shape[2]

    def columns_of(block):
        return pl.ds(pl.multiple_of((block ^ (1 - core)) * span, span), span)

    def finish(head, block, total, top):
        rows = slice(head * head_size, (head + 1) * head_size)

        def write(target):
            for k in range(per_half):
                target[k, rows, :] = total[:head_size, k * LANES : (k + 1) * LANES].astype(BF16)

        pl.when(block == 1)(lambda: write(kept))
        pl.when(block == 0)(lambda: write(given))
        for slot, row in enumerate(stat_rows(top, total[head_size : head_size + 1])):
            stats[slot * HEADS + head : slot * HEADS + head + 1, columns_of(block)] = row

    attention_loop(
        [inner_keys, keys], query1_t, [inner_values_t, values_t], scores, 256, 2, columns_of, finish
    )
    for target, side in ((kept, core), (given, 1 - core)):
        for k in range(per_half):
            columns = pl.ds(pl.multiple_of((side * per_half + k) * LANES, LANES), LANES)
            target[k, width:, :] = stats[:, columns].astype(BF16)


def merge_blocks(blocks):
    width = blocks[0].shape[0] - STAT_ROWS
    head_size = width // HEADS
    slots = [[block[width + n * HEADS : width + (n + 1) * HEADS] for n in range(5)] for block in blocks]
    tops = [s[0] + s[1] + s[2] for s in slots]
    top = functools.reduce(jnp.maximum, tops)
    factors = [jnp.exp2(t - top) for t in tops]
    total = sum(f * (s[3] + s[4]) for f, s in zip(factors, slots))
    sums = []
    for head in range(HEADS):
        rows = slice(head * head_size, (head + 1) * head_size)
        sums.append(sum(block[rows] * f[head : head + 1] for block, f in zip(blocks, factors)))
    return sums, top, total


def all_stats(top, total, size):
    rows = list(stat_rows(top, total))
    filler = jnp.zeros((size - len(rows) * HEADS,) + top.shape[1:], F32)
    return jnp.concatenate(rows + [filler], axis=0)


def merge_pair_kernel(kept, taken, *outs):
    for distance, out in enumerate(outs):
        index = lax.axis_index(("wx", "ny")) ^ distance
        sums, top, total = merge_blocks([ref[index].astype(F32) for ref in (kept, taken)])
        sums.append(all_stats(top, total, STAT_ROWS))
        out[...] = jnp.concatenate(sums, axis=0).astype(BF16)


def merge_group_kernel(count, *refs):
    blocks, outs, turned = refs[:count], refs[count:-1], refs[-1]
    sums, top, total = merge_blocks([ref[...].astype(F32) for ref in blocks])
    width = turned.shape[1] - LANES
    sums = jnp.concatenate(sums, axis=0)
    for k in range(width // LANES):
        lanes = slice(k * LANES, (k + 1) * LANES)
        turned[:, lanes] = sums[lanes].T
    turned[:, width:] = all_stats(top, total, LANES).T
    rows = outs[0].shape[0]
    for distance, out in enumerate(outs):
        index = lax.axis_index("wz") ^ distance
        out[...] = turned[pl.ds(pl.multiple_of(index * rows, rows), rows), :].astype(BF16)


def unpack_stats(tile):
    parts = [tile] + [pltpu.roll(tile, LANES - slot * HEADS, 1) for slot in range(1, 5)]
    return parts[0] + parts[1] + parts[2], parts[3] + parts[4]


def spread(per_head, pair):
    rows = per_head.shape[0]
    lane = lax.broadcasted_iota(jnp.int32, (rows, LANES), 1)
    left = jnp.broadcast_to(per_head[:, 2 * pair : 2 * pair + 1], (rows, LANES))
    right = jnp.broadcast_to(per_head[:, 2 * pair + 1 : 2 * pair + 2], (rows, LANES))
    return jnp.where(lane < LANES // 2, left, right)


def update_kernel(own, w_out1, *refs):
    parts, out = refs[:-1], refs[-1]
    width = own.shape[1]
    stats = [unpack_stats(part[:, width:].astype(F32)) for part in parts]
    top = functools.reduce(jnp.maximum, [t for t, _ in stats])
    factors = [jnp.exp2(t - top) for t, _ in stats]
    total = sum(f * l for f, (_, l) in zip(factors, stats))
    read = []
    for pair in range(width // LANES):
        lanes = slice(pair * LANES, (pair + 1) * LANES)
        value = sum(part[:, lanes].astype(F32) * spread(f, pair) for part, f in zip(parts, factors))
        read.append(value / spread(total, pair))
    read = jnp.concatenate(read, axis=1).astype(BF16)
    out[...] = (own[...].astype(F32) + dot(read, w_out1[...])).astype(BF16)


def join_kernel(*refs):
    parts, out = refs[:-1], refs[-1]
    rows = parts[0].shape[0]
    for k, part in enumerate(parts):
        out[k * rows : (k + 1) * rows, :] = part[...]


def join(parts, name):
    rows, width = parts[0].shape
    out = jax.ShapeDtypeStruct((len(parts) * rows, width), parts[0].dtype)
    return call(join_kernel, out, [], parts, 8, 1e6, name)


def write_kernel(
    own_state,
    other_state,
    query2_t,
    masked,
    w_key2,
    w_value2,
    w_out2,
    out,
    keys,
    values_t,
    scores,
    read_t,
    buffers,
    sent,
):
    half, width = own_state.shape
    head_size = width // HEADS
    values_t[:, head_size:, :] = jnp.ones_like(values_t[:, head_size:, :])
    for side, state in enumerate((own_state, other_state)):
        rows = slice(side * half, (side + 1) * half)
        keys[rows, :] = dot(state[...], w_key2[...]).astype(BF16)
        value_t = dot(w_value2[...], state[...], ((0,), (1,))).astype(BF16)
        values_t[:, :head_size, rows] = value_t.reshape(HEADS, head_size, half)
    span = scores.shape[2]
    blocks = out.shape[0] // span

    def send(block):
        slot = block % 2
        rows = pl.ds(pl.multiple_of(block * span, span), span)
        return pltpu.make_async_copy(buffers.at[slot], out.at[rows, :], sent.at[slot])

    def columns_of(block):
        return pl.ds(pl.multiple_of(block * span, span), span)

    def finish(head, block, total, top):
        rows = slice(head * head_size, (head + 1) * head_size)
        inverse = 1.0 / total[head_size : head_size + 1]
        read_t[rows, :] = (total[:head_size] * inverse).astype(BF16)
        if head == HEADS - 1:
            pl.when(block >= 2)(lambda: send(block - 2).wait())
            change = dot(read_t[...], w_out2[...], ((0,), (0,)))
            buffers[block % 2] = masked[columns_of(block), :].astype(F32) + change
            send(block).start()

    attention_loop([keys], query2_t, [values_t], scores, 256, blocks, columns_of, finish)
    for block in range(max(blocks - 2, 0), blocks):
        send(block).wait()


def call(kernel, shapes, scratch, operands, limit, flops, name, far=(), aliases=None, out_space=pltpu.VMEM):
    vmem = pl.BlockSpec(memory_space=pltpu.VMEM)
    hbm = pl.BlockSpec(memory_space=pltpu.HBM)
    many = isinstance(shapes, (list, tuple))
    in_specs = [hbm if n in far else vmem for n in range(len(operands))]
    moved = sum(x.size * x.dtype.itemsize for x in operands)
    result = pl.pallas_call(
        kernel,
        out_shape=shapes,
        in_specs=in_specs,
        out_specs=[vmem] * len(shapes) if many else pl.BlockSpec(memory_space=out_space),
        scratch_shapes=scratch,
        compiler_params=pltpu.CompilerParams(vmem_limit_bytes=limit * MIB),
        cost_estimate=pl.CostEstimate(flops=int(flops), bytes_accessed=moved, transcendentals=0),
        input_output_aliases=aliases or {},
        name=name,
    )(*operands)
    return list(result) if many else result


def pair_exchange(first, second, axis):
    count = lax.axis_size(axis)
    swaps = [[], []]
    for i in range(count - 1):
        swaps[i % 2] += [(i, i + 1), (i + 1, i)]
    other = lax.ppermute(second, axis, swaps[1])
    return lax.ppermute(first, axis, swaps[0]), other


def flipped(array, axis, distance):
    return lax.ppermute(array, axis, [(i, i ^ distance) for i in range(lax.axis_size(axis))])


def per_device(
    flow_field,
    fluid_mask,
    conv_weight,
    latents,
    w_query1,
    w_key1,
    w_value1,
    w_out1,
    w_query2,
    w_key2,
    w_value2,
    w_out2,
):
    size_x, size_y, size_z, width = flow_field.shape
    head_size = width // HEADS
    plane_cells = size_y * size_z
    inner_cells, outer_cells = (size_x - 2) * plane_cells, 2 * plane_cells
    cells = inner_cells + outer_cells
    latent_count = latents.shape[0]
    wide, narrow, group = ("wz", "wx"), ("ny", "nc"), ("wx", "ny")
    group_size = lax.axis_size(group)
    far = lax.axis_size("wz")
    core, member, layer = lax.axis_index("nc"), lax.axis_index(group), lax.axis_index("wz")
    block_size = latent_count // (2 * group_size)
    rows = block_size // far
    shape = jax.ShapeDtypeStruct
    step = 1e9

    side = shape((size_x, size_z, width), BF16)
    ends = pltpu.VMEM((size_x, 1, size_z, width), BF16)
    y_first, y_second = call(
        face_kernel,
        [side, side],
        [ends, ends, pltpu.VMEM(fluid_mask.shape, jnp.int32), pltpu.SemaphoreType.DMA((3,))],
        [flow_field, fluid_mask],
        56,
        step,
        "face",
        (0, 1),
    )
    y_first, y_second = pair_exchange(y_first, y_second, narrow)
    masked = call(
        prepare_kernel, shape(flow_field.shape, BF16), [], [flow_field, fluid_mask], 12, 2 * step, "prepare"
    )
    query1_t = call(
        latent_query_kernel,
        shape((width, latent_count), BF16),
        [],
        [latents, w_query1],
        12,
        2 * step,
        "latent_query",
    )
    side = shape((size_y + 2, size_z, width), BF16)
    x_first, x_second = call(
        edge_kernel, [side, side], [], [masked, y_first, y_second], 12, step, "edge"
    )
    x_first, x_second = pair_exchange(x_first, x_second, wide)
    weight = pltpu.VMEM((width, width), BF16)
    inner_keys, inner_values_t, query2_t = call(
        inner_kernel,
        [
            shape((inner_cells, width), BF16),
            shape((HEADS, head_size + ONES_ROWS, inner_cells), BF16),
            shape((width, cells), BF16),
        ],
        [
            pltpu.VMEM((size_x, size_y + 2, size_z, width), F32),
            pltpu.VMEM((inner_cells, width), BF16),
            weight,
            weight,
            weight,
            pltpu.SemaphoreType.DMA((3,)),
        ],
        [masked, y_first, y_second, conv_weight, w_key1, w_value1, w_query2],
        28,
        10 * step,
        "inner",
        (4, 5, 6),
    )
    query2_t, kept, given = call(
        read_kernel,
        [shape((width, cells), BF16)] + [shape((group_size, width + STAT_ROWS, LANES), BF16)] * 2,
        [
            pltpu.VMEM((6, size_y + 2, size_z, width), F32),
            pltpu.VMEM((outer_cells, width), BF16),
            pltpu.VMEM((outer_cells, width), BF16),
            pltpu.VMEM((HEADS, head_size + ONES_ROWS, outer_cells), BF16),
            pltpu.VMEM((2, cells, latent_count // 2), F32),
            pltpu.VMEM((STAT_ROWS, latent_count), F32),
        ],
        [
            masked,
            x_first,
            x_second,
            y_first,
            y_second,
            conv_weight,
            w_key1,
            w_value1,
            w_query2,
            inner_keys,
            inner_values_t,
            query1_t,
            query2_t,
        ],
        32,
        20 * step,
        "read",
        (),
        {12: 0},
    )
    taken = flipped(given, "nc", 1)
    block = shape((width + STAT_ROWS, LANES), BF16)
    blocks = call(merge_pair_kernel, [block] * group_size, [], [kept, taken], 16, step, "merge_pair")
    blocks = [flipped(blocks[d], group, d) for d in range(group_size - 1, 0, -1)] + blocks[:1]
    parts = call(
        functools.partial(merge_group_kernel, group_size),
        [shape((rows, width + LANES), BF16)] * far,
        [pltpu.VMEM((block_size, width + LANES), F32)],
        blocks,
        16,
        step,
        "merge_group",
    )
    order = list(range(far - 2, 0, -1)) + [far - 1]
    parts = [flipped(parts[d], "wz", d) for d in order] + parts[:1]
    start = ((core * group_size + member) * far + layer) * rows
    own = lax.dynamic_slice_in_dim(latents, start, rows, 0)
    state = call(update_kernel, shape((rows, width), BF16), [], [own, w_out1] + parts, 16, step, "update")
    state = join([flipped(state, "wz", d) for d in range(far - 1, 0, -1)] + [state], "join_far")
    state = join([flipped(state, group, d) for d in range(group_size - 1, 0, -1)] + [state], "join_group")
    other = flipped(state, "nc", 1)
    span = 2 * plane_cells

    result = call(
        write_kernel,
        shape((cells, width), F32),
        [
            pltpu.VMEM((latent_count, width), BF16),
            pltpu.VMEM((HEADS, head_size + ONES_ROWS, latent_count), BF16),
            pltpu.VMEM((2, latent_count, span), F32),
            pltpu.VMEM((width, span), BF16),
            pltpu.VMEM((2, span, width), F32),
            pltpu.SemaphoreType.DMA((2,)),
        ],
        [state, other, query2_t, masked.reshape(cells, width), w_key2, w_value2, w_out2],
        32,
        20 * step,
        "write",
        out_space=pltpu.HBM,
    )
    return result.reshape(size_x, size_y, size_z, width)


def solution(mesh):
    wide, narrow = (mesh.shape[name] for name in ("wide", "narrow"))
    grid = Mesh(mesh.devices.reshape(wide // 2, 2, narrow // 2, 2), ("wz", "wx", "ny", "nc"))
    split = P(("wz", "wx"), ("ny", "nc"))
    return jax.shard_map(
        per_device,
        mesh=grid,
        in_specs=(split, split) + (P(),) * 10,
        out_specs=split,
        check_vma=False,
    )
```

```python
import functools
import math

import jax
import jax.numpy as jnp
from jax import lax
from jax.experimental import pallas as pl
from jax.experimental.pallas import tpu as pltpu
from jax.sharding import Mesh, PartitionSpec as P

HEADS = 8
LANES = 128
ONES_ROWS = 16
STAT_ROWS = 48
MIB = 1 << 20
F32 = jnp.float32
BF16 = jnp.bfloat16


def dot(left, right, contract=((1,), (0,))):
    return lax.dot_general(left, right, (contract, ((), ())), preferred_element_type=F32)


def masked_column(flow, mask_plane, i, j):
    size_z, width = flow.shape[2:]
    column = jnp.broadcast_to(mask_plane[:, j : j + 1], (size_z, LANES)).astype(BF16)
    tiles = [flow[i, j, :, k * LANES : (k + 1) * LANES] * column for k in range(width // LANES)]
    return jnp.concatenate(tiles, axis=1)


def face_kernel(flow, far_mask, first, second, low, high, mask, arrived):
    size_x, size_y = flow.shape[:2]
    copies = []
    for n, (j, target) in enumerate(((0, low), (size_y - 1, high))):
        copies.append(pltpu.make_async_copy(flow.at[:, pl.ds(j, 1)], target, arrived.at[n]))
        copies[-1].start()
    copies.append(pltpu.make_async_copy(far_mask, mask, arrived.at[2]))
    copies[-1].start()
    for copy in copies:
        copy.wait()
    odd = lax.axis_index("nc") == 1
    turned = jnp.concatenate([mask[:, 0, :], mask[:, size_y - 1, :]], axis=0).astype(F32).T
    for i in range(size_x):
        bottom = masked_column(low, turned[:, i:], i, 0)
        top = masked_column(high, turned[:, size_x + i :], i, 0)
        first[i] = jnp.where(odd, bottom, top)
        second[i] = jnp.where(odd, top, bottom)


def prepare_kernel(flow, mask, masked):
    size_x, size_y = flow.shape[:2]

    def plane(i, carry):
        turned = mask[i].astype(F32).T
        for j in range(size_y):
            masked[i, j] = masked_column(flow, turned, i, j)
        return carry

    lax.fori_loop(0, size_x, plane, 0)


def edge_kernel(masked, y_first, y_second, first, second):
    size_x, size_y = masked.shape[:2]
    outer = size_y + 1
    for face, plane in ((first, (size_x - 1) * (1 - lax.axis_index("wx"))), (second, (size_x - 1) * lax.axis_index("wx"))):
        face[1:outer] = masked[plane]
        face[outer * (1 - lax.axis_index("nc"))] = y_first[plane]
        face[outer * lax.axis_index("nc")] = y_second[plane]


def fill_row(padded, row, i, masked, y_first, y_second):
    outer = masked.shape[1] + 1
    padded[row, 1:outer] = masked[i].astype(F32)
    padded[row, outer * (1 - lax.axis_index("nc"))] = y_first[i].astype(F32)
    padded[row, outer * lax.axis_index("nc")] = y_second[i].astype(F32)


def stencil_plane(base, padded, conv, mixed, start, others=()):
    size_y, size_z, width = padded.shape[1] - 2, padded.shape[2], padded.shape[3]
    row_of = lax.broadcasted_iota(jnp.int32, (size_z, LANES), 0)
    others = list(others)
    for tile in range(width // LANES):
        lanes = slice(tile * LANES, (tile + 1) * LANES)
        taps = [jnp.broadcast_to(conv[n : n + 1, lanes], (size_z, LANES)) for n in range(27)]
        for j in range(size_y):
            if others and j % (size_y // 2) == 0:
                others.pop(0)()
            sums = [None] * 3
            for a in range(3):
                for b in range(3):
                    window = padded[base + a, j + b, :, lanes]
                    for c in range(3):
                        term = window * taps[9 * a + 3 * b + c]
                        sums[c] = term if sums[c] is None else sums[c] + term
            below = jnp.where(row_of == 0, 0.0, pltpu.roll(sums[0], 1, 0))
            above = jnp.where(row_of == size_z - 1, 0.0, pltpu.roll(sums[2], size_z - 1, 0))
            total = padded[base + 1, j + 1, :, lanes] + sums[1] + below + above
            mixed[pl.ds(pl.multiple_of(start + j * size_z, size_z), size_z), lanes] = total.astype(BF16)
    for other in others:
        other()


def projections(start, target, cells, mixed, weights, keys, values_t, query2_t):
    w_key1, w_value1, w_query2 = weights
    width = mixed.shape[1]
    head_size = width // HEADS
    rows = pl.ds(pl.multiple_of(start, cells), cells)
    columns = pl.ds(pl.multiple_of(target, cells), cells)
    work = []
    for part in range(2):

        def key_part(part=part):
            some = pl.ds(pl.multiple_of(start + part * (cells // 2), cells // 2), cells // 2)
            keys[some, :] = dot(mixed[some, :], w_key1[...]).astype(BF16)

        def value_part(part=part):
            channels = slice(part * (width // 2), (part + 1) * (width // 2))
            value_t = dot(w_value1[channels, :], mixed[rows, :], ((1,), (1,))).astype(BF16)
            heads = slice(part * (HEADS // 2), (part + 1) * (HEADS // 2))
            values_t[heads, :head_size, rows] = value_t.reshape(HEADS // 2, head_size, cells)

        def query_part(part=part):
            channels = slice(part * (width // 2), (part + 1) * (width // 2))
            found = dot(w_query2[channels, :], mixed[rows, :], ((1,), (1,)))
            query2_t[channels, columns] = found.astype(BF16)

        work += [key_part, value_part, query_part]
    return work


def latent_query_kernel(latents, w_query1, query1_t):
    query1_t[...] = dot(w_query1[...], latents[...], ((0,), (1,))).astype(BF16)


def inner_kernel(
    masked,
    y_first,
    y_second,
    conv,
    far_key1,
    far_value1,
    far_query2,
    keys,
    values_t,
    query2_t,
    turned_value1,
    turned_query2,
    padded,
    mixed,
    w_key1,
    w_value1,
    w_query2,
    arrived,
):
    size_x, size_y, size_z, width = masked.shape
    head_size = width // HEADS
    cells = size_y * size_z
    weights = (w_key1, turned_value1, turned_query2)
    copies = [
        pltpu.make_async_copy(source, target, arrived.at[n])
        for n, (source, target) in enumerate(zip((far_key1, far_value1, far_query2), (w_key1, w_value1, w_query2)))
    ]
    for copy in copies:
        copy.start()

    def fill(i, carry):
        fill_row(padded, i, i, masked, y_first, y_second)
        return carry

    lax.fori_loop(0, size_x, fill, 0)
    values_t[:, head_size:, :] = jnp.ones_like(values_t[:, head_size:, :])
    for copy in copies:
        copy.wait()
    turned_value1[...] = w_value1[...].T
    turned_query2[...] = w_query2[...].T

    def work(i):
        return projections(i * cells, (i + 1) * cells, cells, mixed, weights, keys, values_t, query2_t)

    stencil_plane(0, padded, conv, mixed, 0)

    def plane(i, carry):
        stencil_plane(i, padded, conv, mixed, i * cells, work(i - 1))
        return carry

    lax.fori_loop(1, size_x - 2, plane, 0)
    for product in work(size_x - 3):
        product()


def score_weights(query_t, head, columns):
    head_size = LANES // 2
    factor = 1.8 / math.sqrt(head_size) * math.log2(math.e)
    scaled = query_t[head * head_size : (head + 1) * head_size, columns].astype(F32) * factor
    high = scaled.astype(BF16)
    low = (scaled - high.astype(F32)).astype(BF16)
    blank = jnp.zeros_like(high)
    if head % 2 == 0:
        return jnp.concatenate([high, blank, low, blank], axis=0)
    return jnp.concatenate([blank, high, blank, low], axis=0)


def chunks_of(pieces, axis, chunk):
    found = []
    base = 0
    for piece in pieces:
        for part in range(piece.shape[axis] // chunk):
            found.append((piece, part * chunk, base))
            base += chunk
    return found


def score_chunk(place, head, right, chunk, scores, top):
    piece, start, base = place
    pair = head // 2
    left = piece[start : start + chunk, pair * LANES : (pair + 1) * LANES]
    found = dot(jnp.concatenate([left, left], axis=1), right)
    scores[head % 2, base : base + chunk, :] = found
    largest = jnp.max(found.reshape(chunk // 8, 8, found.shape[1]), axis=0)
    return largest if top is None else jnp.maximum(top, largest)


def sum_chunk(place, head, chunk, scores, top, total):
    piece, start, base = place
    weights = jnp.exp2(scores[head % 2, base : base + chunk, :] - top).astype(BF16)
    found = dot(piece[head, :, start : start + chunk], weights)
    return found if total is None else total + found


def attention_loop(keys, query_t, values_t, scores, chunk, blocks, columns_of, finish):
    key_chunks, value_chunks = chunks_of(keys, 0, chunk), chunks_of(values_t, 2, chunk)

    def overall(top):
        return jnp.max(top, axis=0, keepdims=True)

    def first(block):
        right = score_weights(query_t, 0, columns_of(block))
        top = None
        for place in key_chunks:
            top = score_chunk(place, 0, right, chunk, scores, top)
        return overall(top)

    def step(block, top):
        for head in range(HEADS):
            ahead = (head + 1) % HEADS
            following = block if ahead else jnp.minimum(block + 1, blocks - 1)
            right = score_weights(query_t, ahead, columns_of(following))
            upcoming = total = None
            for key_place, value_place in zip(key_chunks, value_chunks):
                upcoming = score_chunk(key_place, ahead, right, chunk, scores, upcoming)
                total = sum_chunk(value_place, head, chunk, scores, top, total)
            finish(head, block, total, top)
            top = overall(upcoming)
        return top

    lax.fori_loop(0, blocks, step, first(0))


def split3(value):
    high = value.astype(BF16).astype(F32)
    rest = value - high
    middle = rest.astype(BF16).astype(F32)
    return high, middle, rest - middle


def stat_rows(top, total):
    return split3(top) + split3(total)[:2]


def read_kernel(
    masked,
    x_first,
    x_second,
    y_first,
    y_second,
    conv,
    w_key1,
    w_value1,
    w_query2,
    inner_keys,
    inner_values_t,
    query1_t,
    inner_query2_t,
    query2_t,
    kept,
    given,
    padded,
    mixed,
    keys,
    values_t,
    scores,
    stats,
):
    size_x, size_y, size_z, width = masked.shape
    head_size = width // HEADS
    cells = size_y * size_z
    last = size_x - 1
    for row, i in ((1, 0), (2, 1), (3, last - 1), (4, last)):
        fill_row(padded, row, i, masked, y_first, y_second)
    padded[5 * (1 - lax.axis_index("wx"))] = x_first[...].astype(F32)
    padded[5 * lax.axis_index("wx")] = x_second[...].astype(F32)
    values_t[:, head_size:, :] = jnp.ones_like(values_t[:, head_size:, :])
    stats[...] = jnp.zeros_like(stats)

    weights = (w_key1, w_value1, w_query2)


    def work(i):
        return projections(i * cells, i * last * cells, cells, mixed, weights, keys, values_t, query2_t)

    stencil_plane(0, padded, conv, mixed, 0)
    stencil_plane(3, padded, conv, mixed, cells, work(0))
    for product in work(1):
        product()

    core = lax.axis_index("nc")
    per_half = kept.shape[0]
    span = scores.shape[2]

    def columns_of(block):
        return pl.ds(pl.multiple_of((block ^ (1 - core)) * span, span), span)

    def finish(head, block, total, top):
        rows = slice(head * head_size, (head + 1) * head_size)

        def write(target):
            for k in range(per_half):
                target[k, rows, :] = total[:head_size, k * LANES : (k + 1) * LANES].astype(BF16)

        pl.when(block == 1)(lambda: write(kept))
        pl.when(block == 0)(lambda: write(given))
        for slot, row in enumerate(stat_rows(top, total[head_size : head_size + 1])):
            stats[slot * HEADS + head : slot * HEADS + head + 1, columns_of(block)] = row

    attention_loop(
        [inner_keys, keys], query1_t, [inner_values_t, values_t], scores, 256, 2, columns_of, finish
    )
    for target, side in ((kept, core), (given, 1 - core)):
        for k in range(per_half):
            columns = pl.ds(pl.multiple_of((side * per_half + k) * LANES, LANES), LANES)
            target[k, width:, :] = stats[:, columns].astype(BF16)


def merge_blocks(blocks):
    width = blocks[0].shape[0] - STAT_ROWS
    head_size = width // HEADS
    slots = [[block[width + n * HEADS : width + (n + 1) * HEADS] for n in range(5)] for block in blocks]
    tops = [s[0] + s[1] + s[2] for s in slots]
    top = functools.reduce(jnp.maximum, tops)
    factors = [jnp.exp2(t - top) for t in tops]
    total = sum(f * (s[3] + s[4]) for f, s in zip(factors, slots))
    sums = []
    for head in range(HEADS):
        rows = slice(head * head_size, (head + 1) * head_size)
        sums.append(sum(block[rows] * f[head : head + 1] for block, f in zip(blocks, factors)))
    return sums, top, total


def all_stats(top, total, size):
    rows = list(stat_rows(top, total))
    filler = jnp.zeros((size - len(rows) * HEADS,) + top.shape[1:], F32)
    return jnp.concatenate(rows + [filler], axis=0)


def merge_pair_kernel(kept, taken, *outs):
    for distance, out in enumerate(outs):
        index = lax.axis_index(("wx", "ny")) ^ distance
        sums, top, total = merge_blocks([ref[index].astype(F32) for ref in (kept, taken)])
        sums.append(all_stats(top, total, STAT_ROWS))
        out[...] = jnp.concatenate(sums, axis=0).astype(BF16)


def merge_group_kernel(count, *refs):
    blocks, outs, turned = refs[:count], refs[count:-1], refs[-1]
    sums, top, total = merge_blocks([ref[...].astype(F32) for ref in blocks])
    width = turned.shape[1] - LANES
    sums = jnp.concatenate(sums, axis=0)
    for k in range(width // LANES):
        lanes = slice(k * LANES, (k + 1) * LANES)
        turned[:, lanes] = sums[lanes].T
    turned[:, width:] = all_stats(top, total, LANES).T
    rows = outs[0].shape[0]
    for distance, out in enumerate(outs):
        index = lax.axis_index("wz") ^ distance
        out[...] = turned[pl.ds(pl.multiple_of(index * rows, rows), rows), :].astype(BF16)


def unpack_stats(tile):
    parts = [tile] + [pltpu.roll(tile, LANES - slot * HEADS, 1) for slot in range(1, 5)]
    return parts[0] + parts[1] + parts[2], parts[3] + parts[4]


def spread(per_head, pair):
    rows = per_head.shape[0]
    lane = lax.broadcasted_iota(jnp.int32, (rows, LANES), 1)
    left = jnp.broadcast_to(per_head[:, 2 * pair : 2 * pair + 1], (rows, LANES))
    right = jnp.broadcast_to(per_head[:, 2 * pair + 1 : 2 * pair + 2], (rows, LANES))
    return jnp.where(lane < LANES // 2, left, right)


def update_kernel(own, w_out1, *refs):
    parts, out = refs[:-1], refs[-1]
    width = own.shape[1]
    stats = [unpack_stats(part[:, width:].astype(F32)) for part in parts]
    top = functools.reduce(jnp.maximum, [t for t, _ in stats])
    factors = [jnp.exp2(t - top) for t, _ in stats]
    total = sum(f * l for f, (_, l) in zip(factors, stats))
    read = []
    for pair in range(width // LANES):
        lanes = slice(pair * LANES, (pair + 1) * LANES)
        value = sum(part[:, lanes].astype(F32) * spread(f, pair) for part, f in zip(parts, factors))
        read.append(value / spread(total, pair))
    read = jnp.concatenate(read, axis=1).astype(BF16)
    out[...] = (own[...].astype(F32) + dot(read, w_out1[...])).astype(BF16)


def join_kernel(*refs):
    parts, out = refs[:-1], refs[-1]
    rows = parts[0].shape[0]
    for k, part in enumerate(parts):
        out[k * rows : (k + 1) * rows, :] = part[...]


def join(parts, name):
    rows, width = parts[0].shape
    out = jax.ShapeDtypeStruct((len(parts) * rows, width), parts[0].dtype)
    return call(join_kernel, out, [], parts, 8, 1e6, name)


def write_kernel(
    own_state,
    other_state,
    query2_t,
    masked,
    w_key2,
    w_value2,
    w_out2,
    out,
    keys,
    values_t,
    scores,
    read_t,
    buffers,
    sent,
):
    half, width = own_state.shape
    head_size = width // HEADS
    values_t[:, head_size:, :] = jnp.ones_like(values_t[:, head_size:, :])
    for side, state in enumerate((own_state, other_state)):
        rows = slice(side * half, (side + 1) * half)
        keys[rows, :] = dot(state[...], w_key2[...]).astype(BF16)
        value_t = dot(w_value2[...], state[...], ((0,), (1,))).astype(BF16)
        values_t[:, :head_size, rows] = value_t.reshape(HEADS, head_size, half)
    span = scores.shape[2]
    blocks = out.shape[0] // span

    def send(block):
        slot = block % 2
        rows = pl.ds(pl.multiple_of(block * span, span), span)
        return pltpu.make_async_copy(buffers.at[slot], out.at[rows, :], sent.at[slot])

    def columns_of(block):
        return pl.ds(pl.multiple_of(block * span, span), span)

    def finish(head, block, total, top):
        rows = slice(head * head_size, (head + 1) * head_size)
        inverse = 1.0 / total[head_size : head_size + 1]
        read_t[rows, :] = (total[:head_size] * inverse).astype(BF16)
        if head == HEADS - 1:
            pl.when(block >= 2)(lambda: send(block - 2).wait())
            change = dot(read_t[...], w_out2[...], ((0,), (0,)))
            buffers[block % 2] = masked[columns_of(block), :].astype(F32) + change
            send(block).start()

    attention_loop([keys], query2_t, [values_t], scores, 256, blocks, columns_of, finish)
    for block in range(max(blocks - 2, 0), blocks):
        send(block).wait()


def call(kernel, shapes, scratch, operands, limit, flops, name, far=(), aliases=None, out_space=pltpu.VMEM):
    vmem = pl.BlockSpec(memory_space=pltpu.VMEM)
    hbm = pl.BlockSpec(memory_space=pltpu.HBM)
    many = isinstance(shapes, (list, tuple))
    in_specs = [hbm if n in far else vmem for n in range(len(operands))]
    moved = sum(x.size * x.dtype.itemsize for x in operands)
    result = pl.pallas_call(
        kernel,
        out_shape=shapes,
        in_specs=in_specs,
        out_specs=[vmem] * len(shapes) if many else pl.BlockSpec(memory_space=out_space),
        scratch_shapes=scratch,
        compiler_params=pltpu.CompilerParams(vmem_limit_bytes=limit * MIB),
        cost_estimate=pl.CostEstimate(flops=int(flops), bytes_accessed=moved, transcendentals=0),
        input_output_aliases=aliases or {},
        name=name,
    )(*operands)
    return list(result) if many else result


def pair_exchange(first, second, axis):
    count = lax.axis_size(axis)
    swaps = [[], []]
    for i in range(count - 1):
        swaps[i % 2] += [(i, i + 1), (i + 1, i)]
    other = lax.ppermute(second, axis, swaps[1])
    return lax.ppermute(first, axis, swaps[0]), other


def flipped(array, axis, distance):
    return lax.ppermute(array, axis, [(i, i ^ distance) for i in range(lax.axis_size(axis))])


def per_device(
    flow_field,
    fluid_mask,
    conv_weight,
    latents,
    w_query1,
    w_key1,
    w_value1,
    w_out1,
    w_query2,
    w_key2,
    w_value2,
    w_out2,
):
    size_x, size_y, size_z, width = flow_field.shape
    head_size = width // HEADS
    plane_cells = size_y * size_z
    inner_cells, outer_cells = (size_x - 2) * plane_cells, 2 * plane_cells
    cells = inner_cells + outer_cells
    latent_count = latents.shape[0]
    wide, narrow, group = ("wz", "wx"), ("ny", "nc"), ("wx", "ny")
    group_size = lax.axis_size(group)
    far = lax.axis_size("wz")
    core, member, layer = lax.axis_index("nc"), lax.axis_index(group), lax.axis_index("wz")
    block_size = latent_count // (2 * group_size)
    rows = block_size // far
    shape = jax.ShapeDtypeStruct
    step = 1e9

    side = shape((size_x, size_z, width), BF16)
    ends = pltpu.VMEM((size_x, 1, size_z, width), BF16)
    y_first, y_second = call(
        face_kernel,
        [side, side],
        [ends, ends, pltpu.VMEM(fluid_mask.shape, jnp.int32), pltpu.SemaphoreType.DMA((3,))],
        [flow_field, fluid_mask],
        56,
        step,
        "face",
        (0, 1),
    )
    y_first, y_second = pair_exchange(y_first, y_second, narrow)
    masked = call(
        prepare_kernel, shape(flow_field.shape, BF16), [], [flow_field, fluid_mask], 12, 2 * step, "prepare"
    )
    query1_t = call(
        latent_query_kernel,
        shape((width, latent_count), BF16),
        [],
        [latents, w_query1],
        12,
        2 * step,
        "latent_query",
    )
    side = shape((size_y + 2, size_z, width), BF16)
    x_first, x_second = call(
        edge_kernel, [side, side], [], [masked, y_first, y_second], 12, step, "edge"
    )
    x_first, x_second = pair_exchange(x_first, x_second, wide)
    weight = pltpu.VMEM((width, width), BF16)
    inner_keys, inner_values_t, query2_t, turned_value1, turned_query2 = call(
        inner_kernel,
        [
            shape((inner_cells, width), BF16),
            shape((HEADS, head_size + ONES_ROWS, inner_cells), BF16),
            shape((width, cells), BF16),
            shape((width, width), BF16),
            shape((width, width), BF16),
        ],
        [
            pltpu.VMEM((size_x, size_y + 2, size_z, width), F32),
            pltpu.VMEM((inner_cells, width), BF16),
            weight,
            weight,
            weight,
            pltpu.SemaphoreType.DMA((3,)),
        ],
        [masked, y_first, y_second, conv_weight, w_key1, w_value1, w_query2],
        28,
        10 * step,
        "inner",
        (4, 5, 6),
    )
    query2_t, kept, given = call(
        read_kernel,
        [shape((width, cells), BF16)] + [shape((group_size, width + STAT_ROWS, LANES), BF16)] * 2,
        [
            pltpu.VMEM((6, size_y + 2, size_z, width), F32),
            pltpu.VMEM((outer_cells, width), BF16),
            pltpu.VMEM((outer_cells, width), BF16),
            pltpu.VMEM((HEADS, head_size + ONES_ROWS, outer_cells), BF16),
            pltpu.VMEM((2, cells, latent_count // 2), F32),
            pltpu.VMEM((STAT_ROWS, latent_count), F32),
        ],
        [
            masked,
            x_first,
            x_second,
            y_first,
            y_second,
            conv_weight,
            w_key1,
            turned_value1,
            turned_query2,
            inner_keys,
            inner_values_t,
            query1_t,
            query2_t,
        ],
        32,
        20 * step,
        "read",
        (),
        {12: 0},
    )
    taken = flipped(given, "nc", 1)
    block = shape((width + STAT_ROWS, LANES), BF16)
    blocks = call(merge_pair_kernel, [block] * group_size, [], [kept, taken], 16, step, "merge_pair")
    blocks = [flipped(blocks[d], group, d) for d in range(group_size - 1, 0, -1)] + blocks[:1]
    parts = call(
        functools.partial(merge_group_kernel, group_size),
        [shape((rows, width + LANES), BF16)] * far,
        [pltpu.VMEM((block_size, width + LANES), F32)],
        blocks,
        16,
        step,
        "merge_group",
    )
    order = list(range(far - 2, 0, -1)) + [far - 1]
    parts = [flipped(parts[d], "wz", d) for d in order] + parts[:1]
    start = ((core * group_size + member) * far + layer) * rows
    own = lax.dynamic_slice_in_dim(latents, start, rows, 0)
    state = call(update_kernel, shape((rows, width), BF16), [], [own, w_out1] + parts, 16, step, "update")
    state = join([flipped(state, "wz", d) for d in range(far - 1, 0, -1)] + [state], "join_far")
    state = join([flipped(state, group, d) for d in range(group_size - 1, 0, -1)] + [state], "join_group")
    other = flipped(state, "nc", 1)
    span = 2 * plane_cells

    result = call(
        write_kernel,
        shape((cells, width), F32),
        [
            pltpu.VMEM((latent_count, width), BF16),
            pltpu.VMEM((HEADS, head_size + ONES_ROWS, latent_count), BF16),
            pltpu.VMEM((2, latent_count, span), F32),
            pltpu.VMEM((width, span), BF16),
            pltpu.VMEM((2, span, width), F32),
            pltpu.SemaphoreType.DMA((2,)),
        ],
        [state, other, query2_t, masked.reshape(cells, width), w_key2, w_value2, w_out2],
        32,
        20 * step,
        "write",
        out_space=pltpu.HBM,
    )
    return result.reshape(size_x, size_y, size_z, width)


def solution(mesh):
    wide, narrow = (mesh.shape[name] for name in ("wide", "narrow"))
    grid = Mesh(mesh.devices.reshape(wide // 2, 2, narrow // 2, 2), ("wz", "wx", "ny", "nc"))
    split = P(("wz", "wx"), ("ny", "nc"))
    return jax.shard_map(
        per_device,
        mesh=grid,
        in_specs=(split, split) + (P(),) * 10,
        out_specs=split,
        check_vma=False,
    )
```

```python
import functools
import math

import jax
import jax.numpy as jnp
from jax import lax
from jax.experimental import pallas as pl
from jax.experimental.pallas import tpu as pltpu
from jax.sharding import Mesh, PartitionSpec as P

HEADS = 8
LANES = 128
ONES_ROWS = 16
STAT_ROWS = 48
MIB = 1 << 20
F32 = jnp.float32
BF16 = jnp.bfloat16


def dot(left, right, contract=((1,), (0,))):
    return lax.dot_general(left, right, (contract, ((), ())), preferred_element_type=F32)


def masked_column(flow, mask_plane, i, j):
    size_z, width = flow.shape[2:]
    column = jnp.broadcast_to(mask_plane[:, j : j + 1], (size_z, LANES)).astype(BF16)
    tiles = [flow[i, j, :, k * LANES : (k + 1) * LANES] * column for k in range(width // LANES)]
    return jnp.concatenate(tiles, axis=1)


def face_kernel(flow, far_mask, first, second, low, high, mask, arrived):
    size_x, size_y = flow.shape[:2]
    copies = []
    for n, (j, target) in enumerate(((0, low), (size_y - 1, high))):
        copies.append(pltpu.make_async_copy(flow.at[:, pl.ds(j, 1)], target, arrived.at[n]))
        copies[-1].start()
    copies.append(pltpu.make_async_copy(far_mask, mask, arrived.at[2]))
    copies[-1].start()
    for copy in copies:
        copy.wait()
    odd = lax.axis_index("nc") == 1
    turned = jnp.concatenate([mask[:, 0, :], mask[:, size_y - 1, :]], axis=0).astype(F32).T
    for i in range(size_x):
        bottom = masked_column(low, turned[:, i:], i, 0)
        top = masked_column(high, turned[:, size_x + i :], i, 0)
        first[i] = jnp.where(odd, bottom, top)
        second[i] = jnp.where(odd, top, bottom)


def prepare_kernel(flow, mask, masked):
    size_x, size_y = flow.shape[:2]

    def plane(i, carry):
        turned = mask[i].astype(F32).T
        for j in range(size_y):
            masked[i, j] = masked_column(flow, turned, i, j)
        return carry

    lax.fori_loop(0, size_x, plane, 0)


def edge_kernel(masked, y_second, y_first, first, second):
    size_x, size_y = masked.shape[:2]
    outer = size_y + 1
    for face, plane in ((first, (size_x - 1) * (1 - lax.axis_index("wx"))), (second, (size_x - 1) * lax.axis_index("wx"))):
        face[1:outer] = masked[plane]
        face[outer * (1 - lax.axis_index("nc"))] = y_first[plane]
        face[outer * lax.axis_index("nc")] = y_second[plane]


def fill_row(padded, row, i, masked, y_first, y_second):
    outer = masked.shape[1] + 1
    padded[row, 1:outer] = masked[i].astype(F32)
    padded[row, outer * (1 - lax.axis_index("nc"))] = y_first[i].astype(F32)
    padded[row, outer * lax.axis_index("nc")] = y_second[i].astype(F32)


def stencil_plane(base, padded, conv, mixed, start):
    size_y, size_z, width = padded.shape[1] - 2, padded.shape[2], padded.shape[3]
    row_of = lax.broadcasted_iota(jnp.int32, (size_z, LANES), 0)
    for tile in range(width // LANES):
        lanes = slice(tile * LANES, (tile + 1) * LANES)
        taps = [jnp.broadcast_to(conv[n : n + 1, lanes], (size_z, LANES)) for n in range(27)]
        for j in range(size_y):
            sums = [None] * 3
            for a in range(3):
                for b in range(3):
                    window = padded[base + a, j + b, :, lanes]
                    for c in range(3):
                        term = window * taps[9 * a + 3 * b + c]
                        sums[c] = term if sums[c] is None else sums[c] + term
            below = jnp.where(row_of == 0, 0.0, pltpu.roll(sums[0], 1, 0))
            above = jnp.where(row_of == size_z - 1, 0.0, pltpu.roll(sums[2], size_z - 1, 0))
            total = padded[base + 1, j + 1, :, lanes] + sums[1] + below + above
            mixed[pl.ds(pl.multiple_of(start + j * size_z, size_z), size_z), lanes] = total.astype(BF16)


def project_plane(start, target, cells, mixed, weights, keys, values_t, query2_t):
    w_key1, w_value1, w_query2 = weights
    head_size = mixed.shape[1] // HEADS
    rows = pl.ds(pl.multiple_of(start, cells), cells)
    block = mixed[rows, :]
    keys[rows, :] = dot(block, w_key1[...]).astype(BF16)
    value_t = dot(w_value1[...], block, ((0,), (1,))).astype(BF16)
    values_t[:, :head_size, rows] = value_t.reshape(HEADS, head_size, cells)
    query2_t[:, pl.ds(pl.multiple_of(target, cells), cells)] = dot(w_query2[...], block, ((0,), (1,))).astype(BF16)


def latent_query_kernel(latents, w_query1, query1_t):
    query1_t[...] = dot(w_query1[...], latents[...], ((0,), (1,))).astype(BF16)


def inner_kernel(
    masked,
    y_first,
    y_second,
    conv,
    far_key1,
    far_value1,
    far_query2,
    keys,
    values_t,
    query2_t,
    padded,
    mixed,
    w_key1,
    w_value1,
    w_query2,
    arrived,
):
    size_x, size_y, size_z, width = masked.shape
    head_size = width // HEADS
    cells = size_y * size_z
    weights = (w_key1, w_value1, w_query2)
    copies = [
        pltpu.make_async_copy(source, target, arrived.at[n])
        for n, (source, target) in enumerate(zip((far_key1, far_value1, far_query2), weights))
    ]
    for copy in copies:
        copy.start()

    def fill(i, carry):
        fill_row(padded, i, i, masked, y_first, y_second)
        return carry

    lax.fori_loop(0, size_x, fill, 0)
    values_t[:, head_size:, :] = jnp.ones_like(values_t[:, head_size:, :])
    stencil_plane(0, padded, conv, mixed, 0)
    for copy in copies:
        copy.wait()

    def plane(i, carry):
        project_plane((i - 1) * cells, i * cells, cells, mixed, weights, keys, values_t, query2_t)
        stencil_plane(i, padded, conv, mixed, i * cells)
        return carry

    lax.fori_loop(1, size_x - 2, plane, 0)
    last = size_x - 3
    project_plane(last * cells, (last + 1) * cells, cells, mixed, weights, keys, values_t, query2_t)


def score_weights(query_t, head, columns):
    head_size = LANES // 2
    factor = 1.8 / math.sqrt(head_size) * math.log2(math.e)
    scaled = query_t[head * head_size : (head + 1) * head_size, columns].astype(F32) * factor
    high = scaled.astype(BF16)
    low = (scaled - high.astype(F32)).astype(BF16)
    blank = jnp.zeros_like(high)
    if head % 2 == 0:
        return jnp.concatenate([high, blank, low, blank], axis=0)
    return jnp.concatenate([blank, high, blank, low], axis=0)


def chunks_of(pieces, axis, chunk):
    found = []
    base = 0
    for piece in pieces:
        for part in range(piece.shape[axis] // chunk):
            found.append((piece, part * chunk, base))
            base += chunk
    return found


def score_chunk(place, head, right, chunk, scores, top):
    piece, start, base = place
    pair = head // 2
    left = piece[start : start + chunk, pair * LANES : (pair + 1) * LANES]
    found = dot(jnp.concatenate([left, left], axis=1), right)
    scores[head % 2, base : base + chunk, :] = found
    largest = jnp.max(found.reshape(chunk // 8, 8, found.shape[1]), axis=0)
    return largest if top is None else jnp.maximum(top, largest)


def sum_chunk(place, head, chunk, scores, top, total):
    piece, start, base = place
    weights = jnp.exp2(scores[head % 2, base : base + chunk, :] - top).astype(BF16)
    found = dot(piece[head, :, start : start + chunk], weights)
    return found if total is None else total + found


def attention_loop(keys, query_t, values_t, scores, chunk, columns_of, finish):
    width = scores.shape[2]
    blocks = query_t.shape[1] // width
    key_chunks, value_chunks = chunks_of(keys, 0, chunk), chunks_of(values_t, 2, chunk)

    def overall(top):
        return jnp.max(top, axis=0, keepdims=True)

    def first(block):
        right = score_weights(query_t, 0, columns_of(block))
        top = None
        for place in key_chunks:
            top = score_chunk(place, 0, right, chunk, scores, top)
        return overall(top)

    def step(block, top):
        for head in range(HEADS):
            following = block if head + 1 < HEADS else jnp.minimum(block + 1, blocks - 1)
            ahead = (head + 1) % HEADS
            right = score_weights(query_t, ahead, columns_of(following))
            upcoming = total = None
            for key_place, value_place in zip(key_chunks, value_chunks):
                upcoming = score_chunk(key_place, ahead, right, chunk, scores, upcoming)
                total = sum_chunk(value_place, head, chunk, scores, top, total)
            finish(head, block, total, top)
            top = overall(upcoming)
        return top

    lax.fori_loop(0, blocks, step, first(0))


def split3(value):
    high = value.astype(BF16).astype(F32)
    rest = value - high
    middle = rest.astype(BF16).astype(F32)
    return high, middle, rest - middle


def stat_rows(top, total):
    return split3(top) + split3(total)[:2]


def read_kernel(
    masked,
    x_first,
    x_second,
    y_first,
    y_second,
    conv,
    w_key1,
    w_value1,
    w_query2,
    inner_keys,
    inner_values_t,
    query1_t,
    inner_query2_t,
    query2_t,
    kept,
    given,
    padded,
    mixed,
    keys,
    values_t,
    scores,
    stats,
):
    size_x, size_y, size_z, width = masked.shape
    head_size = width // HEADS
    cells = size_y * size_z
    last = size_x - 1
    for row, i in ((1, 0), (2, 1), (3, last - 1), (4, last)):
        fill_row(padded, row, i, masked, y_first, y_second)
    padded[5 * (1 - lax.axis_index("wx"))] = x_first[...].astype(F32)
    padded[5 * lax.axis_index("wx")] = x_second[...].astype(F32)
    values_t[:, head_size:, :] = jnp.ones_like(values_t[:, head_size:, :])
    stats[...] = jnp.zeros_like(stats)

    weights = (w_key1, w_value1, w_query2)
    stencil_plane(0, padded, conv, mixed, 0)
    project_plane(0, 0, cells, mixed, weights, keys, values_t, query2_t)
    stencil_plane(3, padded, conv, mixed, cells)
    project_plane(cells, last * cells, cells, mixed, weights, keys, values_t, query2_t)

    core = lax.axis_index("nc")
    per_half = kept.shape[0]
    span = scores.shape[2]

    def columns_of(block):
        return pl.ds(pl.multiple_of((block ^ (1 - core)) * span, span), span)

    def finish(head, block, total, top):
        rows = slice(head * head_size, (head + 1) * head_size)

        def write(target):
            for k in range(per_half):
                target[k, rows, :] = total[:head_size, k * LANES : (k + 1) * LANES].astype(BF16)

        pl.when(block == 1)(lambda: write(kept))
        pl.when(block == 0)(lambda: write(given))
        for slot, row in enumerate(stat_rows(top, total[head_size : head_size + 1])):
            stats[slot * HEADS + head : slot * HEADS + head + 1, columns_of(block)] = row

    attention_loop(
        [inner_keys, keys], query1_t, [inner_values_t, values_t], scores, 256, columns_of, finish
    )
    for target, side in ((kept, core), (given, 1 - core)):
        for k in range(per_half):
            columns = pl.ds(pl.multiple_of((side * per_half + k) * LANES, LANES), LANES)
            target[k, width:, :] = stats[:, columns].astype(BF16)


def merge_blocks(blocks):
    width = blocks[0].shape[0] - STAT_ROWS
    head_size = width // HEADS
    slots = [[block[width + n * HEADS : width + (n + 1) * HEADS] for n in range(5)] for block in blocks]
    tops = [s[0] + s[1] + s[2] for s in slots]
    top = functools.reduce(jnp.maximum, tops)
    factors = [jnp.exp2(t - top) for t in tops]
    total = sum(f * (s[3] + s[4]) for f, s in zip(factors, slots))
    sums = []
    for head in range(HEADS):
        rows = slice(head * head_size, (head + 1) * head_size)
        sums.append(sum(block[rows] * f[head : head + 1] for block, f in zip(blocks, factors)))
    return sums, top, total


def all_stats(top, total, size):
    rows = list(stat_rows(top, total))
    filler = jnp.zeros((size - len(rows) * HEADS,) + top.shape[1:], F32)
    return jnp.concatenate(rows + [filler], axis=0)


def merge_pair_kernel(kept, taken, *outs):
    for distance, out in enumerate(outs):
        index = lax.axis_index(("wx", "ny")) ^ distance
        sums, top, total = merge_blocks([ref[index].astype(F32) for ref in (kept, taken)])
        sums.append(all_stats(top, total, STAT_ROWS))
        out[...] = jnp.concatenate(sums, axis=0).astype(BF16)


def merge_group_kernel(count, *refs):
    blocks, outs, turned = refs[:count], refs[count:-1], refs[-1]
    sums, top, total = merge_blocks([ref[...].astype(F32) for ref in blocks])
    width = turned.shape[1] - LANES
    sums = jnp.concatenate(sums, axis=0)
    for k in range(width // LANES):
        lanes = slice(k * LANES, (k + 1) * LANES)
        turned[:, lanes] = sums[lanes].T
    turned[:, width:] = all_stats(top, total, LANES).T
    rows = outs[0].shape[0]
    for distance, out in enumerate(outs):
        index = lax.axis_index("wz") ^ distance
        out[...] = turned[pl.ds(pl.multiple_of(index * rows, rows), rows), :].astype(BF16)


def unpack_stats(tile):
    parts = [tile] + [pltpu.roll(tile, LANES - slot * HEADS, 1) for slot in range(1, 5)]
    return parts[0] + parts[1] + parts[2], parts[3] + parts[4]


def spread(per_head, pair):
    rows = per_head.shape[0]
    lane = lax.broadcasted_iota(jnp.int32, (rows, LANES), 1)
    left = jnp.broadcast_to(per_head[:, 2 * pair : 2 * pair + 1], (rows, LANES))
    right = jnp.broadcast_to(per_head[:, 2 * pair + 1 : 2 * pair + 2], (rows, LANES))
    return jnp.where(lane < LANES // 2, left, right)


def update_kernel(own, w_out1, *refs):
    parts, out = refs[:-1], refs[-1]
    width = own.shape[1]
    stats = [unpack_stats(part[:, width:].astype(F32)) for part in parts]
    top = functools.reduce(jnp.maximum, [t for t, _ in stats])
    factors = [jnp.exp2(t - top) for t, _ in stats]
    total = sum(f * l for f, (_, l) in zip(factors, stats))
    read = []
    for pair in range(width // LANES):
        lanes = slice(pair * LANES, (pair + 1) * LANES)
        value = sum(part[:, lanes].astype(F32) * spread(f, pair) for part, f in zip(parts, factors))
        read.append(value / spread(total, pair))
    read = jnp.concatenate(read, axis=1).astype(BF16)
    out[...] = (own[...].astype(F32) + dot(read, w_out1[...])).astype(BF16)


def join_kernel(*refs):
    parts, out = refs[:-1], refs[-1]
    rows = parts[0].shape[0]
    for k, part in enumerate(parts):
        out[k * rows : (k + 1) * rows, :] = part[...]


def join(parts, name):
    rows, width = parts[0].shape
    out = jax.ShapeDtypeStruct((len(parts) * rows, width), parts[0].dtype)
    return call(join_kernel, out, [], parts, 8, 1e6, name)


def write_kernel(
    own_state,
    other_state,
    query2_t,
    masked,
    w_key2,
    w_value2,
    w_out2,
    out,
    keys,
    values_t,
    scores,
    read_t,
    buffers,
    sent,
):
    half, width = own_state.shape
    head_size = width // HEADS
    values_t[:, head_size:, :] = jnp.ones_like(values_t[:, head_size:, :])
    for side, state in enumerate((own_state, other_state)):
        rows = slice(side * half, (side + 1) * half)
        keys[rows, :] = dot(state[...], w_key2[...]).astype(BF16)
        value_t = dot(w_value2[...], state[...], ((0,), (1,))).astype(BF16)
        values_t[:, :head_size, rows] = value_t.reshape(HEADS, head_size, half)
    span = scores.shape[2]
    blocks = out.shape[0] // span

    def send(block):
        slot = block % 2
        rows = pl.ds(pl.multiple_of(block * span, span), span)
        return pltpu.make_async_copy(buffers.at[slot], out.at[rows, :], sent.at[slot])

    def columns_of(block):
        return pl.ds(pl.multiple_of(block * span, span), span)

    def finish(head, block, total, top):
        rows = slice(head * head_size, (head + 1) * head_size)
        inverse = 1.0 / total[head_size : head_size + 1]
        read_t[rows, :] = (total[:head_size] * inverse).astype(BF16)
        if head == HEADS - 1:
            pl.when(block >= 2)(lambda: send(block - 2).wait())
            change = dot(read_t[...], w_out2[...], ((0,), (0,)))
            buffers[block % 2] = masked[columns_of(block), :].astype(F32) + change
            send(block).start()

    attention_loop([keys], query2_t, [values_t], scores, 256, columns_of, finish)
    for block in range(max(blocks - 2, 0), blocks):
        send(block).wait()


def call(kernel, shapes, scratch, operands, limit, flops, name, far=(), aliases=None, out_space=pltpu.VMEM):
    vmem = pl.BlockSpec(memory_space=pltpu.VMEM)
    hbm = pl.BlockSpec(memory_space=pltpu.HBM)
    many = isinstance(shapes, (list, tuple))
    in_specs = [hbm if n in far else vmem for n in range(len(operands))]
    moved = sum(x.size * x.dtype.itemsize for x in operands)
    result = pl.pallas_call(
        kernel,
        out_shape=shapes,
        in_specs=in_specs,
        out_specs=[vmem] * len(shapes) if many else pl.BlockSpec(memory_space=out_space),
        scratch_shapes=scratch,
        compiler_params=pltpu.CompilerParams(vmem_limit_bytes=limit * MIB),
        cost_estimate=pl.CostEstimate(flops=int(flops), bytes_accessed=moved, transcendentals=0),
        input_output_aliases=aliases or {},
        name=name,
    )(*operands)
    return list(result) if many else result


def pair_exchange(first, second, axis):
    count = lax.axis_size(axis)
    swaps = [[], []]
    for i in range(count - 1):
        swaps[i % 2] += [(i, i + 1), (i + 1, i)]
    other = lax.ppermute(second, axis, swaps[1])
    return lax.ppermute(first, axis, swaps[0]), other


def flipped(array, axis, distance):
    return lax.ppermute(array, axis, [(i, i ^ distance) for i in range(lax.axis_size(axis))])


def per_device(
    flow_field,
    fluid_mask,
    conv_weight,
    latents,
    w_query1,
    w_key1,
    w_value1,
    w_out1,
    w_query2,
    w_key2,
    w_value2,
    w_out2,
):
    size_x, size_y, size_z, width = flow_field.shape
    head_size = width // HEADS
    plane_cells = size_y * size_z
    inner_cells, outer_cells = (size_x - 2) * plane_cells, 2 * plane_cells
    cells = inner_cells + outer_cells
    latent_count = latents.shape[0]
    wide, narrow, group = ("wz", "wx"), ("ny", "nc"), ("wx", "ny")
    group_size = lax.axis_size(group)
    far = lax.axis_size("wz")
    core, member, layer = lax.axis_index("nc"), lax.axis_index(group), lax.axis_index("wz")
    block_size = latent_count // (2 * group_size)
    rows = block_size // far
    shape = jax.ShapeDtypeStruct
    step = 1e9

    side = shape((size_x, size_z, width), BF16)
    ends = pltpu.VMEM((size_x, 1, size_z, width), BF16)
    y_first, y_second = call(
        face_kernel,
        [side, side],
        [ends, ends, pltpu.VMEM(fluid_mask.shape, jnp.int32), pltpu.SemaphoreType.DMA((3,))],
        [flow_field, fluid_mask],
        56,
        step,
        "face",
        (0, 1),
    )
    y_first, y_second = pair_exchange(y_first, y_second, narrow)
    masked = call(
        prepare_kernel, shape(flow_field.shape, BF16), [], [flow_field, fluid_mask], 12, 2 * step, "prepare"
    )
    query1_t = call(
        latent_query_kernel,
        shape((width, latent_count), BF16),
        [],
        [latents, w_query1],
        12,
        2 * step,
        "latent_query",
    )
    side = shape((size_y + 2, size_z, width), BF16)
    x_first, x_second = call(
        edge_kernel, [side, side], [], [masked, y_second, y_first], 12, step, "edge"
    )
    x_first, x_second = pair_exchange(x_first, x_second, wide)
    weight = pltpu.VMEM((width, width), BF16)
    inner_keys, inner_values_t, query2_t = call(
        inner_kernel,
        [
            shape((inner_cells, width), BF16),
            shape((HEADS, head_size + ONES_ROWS, inner_cells), BF16),
            shape((width, cells), BF16),
        ],
        [
            pltpu.VMEM((size_x, size_y + 2, size_z, width), F32),
            pltpu.VMEM((inner_cells, width), BF16),
            weight,
            weight,
            weight,
            pltpu.SemaphoreType.DMA((3,)),
        ],
        [masked, y_first, y_second, conv_weight, w_key1, w_value1, w_query2],
        28,
        10 * step,
        "inner",
        (4, 5, 6),
    )
    query2_t, kept, given = call(
        read_kernel,
        [shape((width, cells), BF16)] + [shape((group_size, width + STAT_ROWS, LANES), BF16)] * 2,
        [
            pltpu.VMEM((6, size_y + 2, size_z, width), F32),
            pltpu.VMEM((outer_cells, width), BF16),
            pltpu.VMEM((outer_cells, width), BF16),
            pltpu.VMEM((HEADS, head_size + ONES_ROWS, outer_cells), BF16),
            pltpu.VMEM((2, cells, latent_count // 2), F32),
            pltpu.VMEM((STAT_ROWS, latent_count), F32),
        ],
        [
            masked,
            x_first,
            x_second,
            y_first,
            y_second,
            conv_weight,
            w_key1,
            w_value1,
            w_query2,
            inner_keys,
            inner_values_t,
            query1_t,
            query2_t,
        ],
        32,
        20 * step,
        "read",
        (),
        {12: 0},
    )
    taken = flipped(given, "nc", 1)
    block = shape((width + STAT_ROWS, LANES), BF16)
    blocks = call(merge_pair_kernel, [block] * group_size, [], [kept, taken], 16, step, "merge_pair")
    blocks = [flipped(blocks[d], group, d) for d in range(group_size - 1, 0, -1)] + blocks[:1]
    parts = call(
        functools.partial(merge_group_kernel, group_size),
        [shape((rows, width + LANES), BF16)] * far,
        [pltpu.VMEM((block_size, width + LANES), F32)],
        blocks,
        16,
        step,
        "merge_group",
    )
    order = list(range(far - 2, 0, -1)) + [far - 1]
    parts = [flipped(parts[d], "wz", d) for d in order] + parts[:1]
    start = ((core * group_size + member) * far + layer) * rows
    own = lax.dynamic_slice_in_dim(latents, start, rows, 0)
    state = call(update_kernel, shape((rows, width), BF16), [], [own, w_out1] + parts, 16, step, "update")
    state = join([flipped(state, "wz", d) for d in range(far - 1, 0, -1)] + [state], "join_far")
    state = join([flipped(state, group, d) for d in range(group_size - 1, 0, -1)] + [state], "join_group")
    other = flipped(state, "nc", 1)
    span = 2 * plane_cells

    result = call(
        write_kernel,
        shape((cells, width), F32),
        [
            pltpu.VMEM((latent_count, width), BF16),
            pltpu.VMEM((HEADS, head_size + ONES_ROWS, latent_count), BF16),
            pltpu.VMEM((2, latent_count, span), F32),
            pltpu.VMEM((width, span), BF16),
            pltpu.VMEM((2, span, width), F32),
            pltpu.SemaphoreType.DMA((2,)),
        ],
        [state, other, query2_t, masked.reshape(cells, width), w_key2, w_value2, w_out2],
        32,
        20 * step,
        "write",
        out_space=pltpu.HBM,
    )
    return result.reshape(size_x, size_y, size_z, width)


def solution(mesh):
    wide, narrow = (mesh.shape[name] for name in ("wide", "narrow"))
    grid = Mesh(mesh.devices.reshape(wide // 2, 2, narrow // 2, 2), ("wz", "wx", "ny", "nc"))
    split = P(("wz", "wx"), ("ny", "nc"))
    return jax.shard_map(
        per_device,
        mesh=grid,
        in_specs=(split, split) + (P(),) * 10,
        out_specs=split,
        check_vma=False,
    )
```

```python
import functools
import math

import jax
import jax.numpy as jnp
from jax import lax
from jax.experimental import pallas as pl
from jax.experimental.pallas import tpu as pltpu
from jax.sharding import Mesh, PartitionSpec as P

HEADS = 8
LANES = 128
ONES_ROWS = 16
STAT_ROWS = 48
MIB = 1 << 20
F32 = jnp.float32
BF16 = jnp.bfloat16


def dot(left, right, contract=((1,), (0,))):
    return lax.dot_general(left, right, (contract, ((), ())), preferred_element_type=F32)


def masked_column(flow, mask_plane, i, j):
    size_z, width = flow.shape[2:]
    column = jnp.broadcast_to(mask_plane[:, j : j + 1], (size_z, LANES)).astype(BF16)
    tiles = [flow[i, j, :, k * LANES : (k + 1) * LANES] * column for k in range(width // LANES)]
    return jnp.concatenate(tiles, axis=1)


def face_kernel(flow, far_mask, first, second, low, high, mask, arrived):
    size_x, size_y = flow.shape[:2]
    copies = []
    for n, (j, target) in enumerate(((0, low), (size_y - 1, high))):
        copies.append(pltpu.make_async_copy(flow.at[:, pl.ds(j, 1)], target, arrived.at[n]))
        copies[-1].start()
    copies.append(pltpu.make_async_copy(far_mask, mask, arrived.at[2]))
    copies[-1].start()
    for copy in copies:
        copy.wait()
    odd = lax.axis_index("nc") == 1
    turned = jnp.concatenate([mask[:, 0, :], mask[:, size_y - 1, :]], axis=0).astype(F32).T
    for i in range(size_x):
        bottom = masked_column(low, turned[:, i:], i, 0)
        top = masked_column(high, turned[:, size_x + i :], i, 0)
        first[i] = jnp.where(odd, bottom, top)
        second[i] = jnp.where(odd, top, bottom)


def prepare_kernel(flow, mask, masked):
    size_x, size_y = flow.shape[:2]

    def plane(i, carry):
        turned = mask[i].astype(F32).T
        for j in range(size_y):
            masked[i, j] = masked_column(flow, turned, i, j)
        return carry

    lax.fori_loop(0, size_x, plane, 0)


def edge_kernel(masked, y_first, y_second, first, second):
    size_x, size_y = masked.shape[:2]
    outer = size_y + 1
    for face, plane in ((first, (size_x - 1) * (1 - lax.axis_index("wx"))), (second, (size_x - 1) * lax.axis_index("wx"))):
        face[1:outer] = masked[plane]
        face[outer * (1 - lax.axis_index("nc"))] = y_first[plane]
        face[outer * lax.axis_index("nc")] = y_second[plane]


def fill_row(padded, row, i, masked, y_first, y_second):
    outer = masked.shape[1] + 1
    padded[row, 1:outer] = masked[i].astype(F32)
    padded[row, outer * (1 - lax.axis_index("nc"))] = y_first[i].astype(F32)
    padded[row, outer * lax.axis_index("nc")] = y_second[i].astype(F32)


def stencil_plane(base, padded, conv, mixed, start):
    size_y, size_z, width = padded.shape[1] - 2, padded.shape[2], padded.shape[3]
    row_of = lax.broadcasted_iota(jnp.int32, (size_z, LANES), 0)
    for tile in range(width // LANES):
        lanes = slice(tile * LANES, (tile + 1) * LANES)
        taps = [jnp.broadcast_to(conv[n : n + 1, lanes], (size_z, LANES)) for n in range(27)]
        for j in range(size_y):
            sums = [None] * 3
            for a in range(3):
                for b in range(3):
                    window = padded[base + a, j + b, :, lanes]
                    for c in range(3):
                        term = window * taps[9 * a + 3 * b + c]
                        sums[c] = term if sums[c] is None else sums[c] + term
            below = jnp.where(row_of == 0, 0.0, pltpu.roll(sums[0], 1, 0))
            above = jnp.where(row_of == size_z - 1, 0.0, pltpu.roll(sums[2], size_z - 1, 0))
            total = padded[base + 1, j + 1, :, lanes] + sums[1] + below + above
            mixed[pl.ds(pl.multiple_of(start + j * size_z, size_z), size_z), lanes] = total.astype(BF16)


def project_plane(start, target, cells, mixed, weights, keys, values_t, query2_t):
    w_key1, w_value1, w_query2 = weights
    head_size = mixed.shape[1] // HEADS
    rows = pl.ds(pl.multiple_of(start, cells), cells)
    block = mixed[rows, :]
    keys[rows, :] = dot(block, w_key1[...]).astype(BF16)
    value_t = dot(w_value1[...], block, ((0,), (1,))).astype(BF16)
    values_t[:, :head_size, rows] = value_t.reshape(HEADS, head_size, cells)
    query2_t[:, pl.ds(pl.multiple_of(target, cells), cells)] = dot(w_query2[...], block, ((0,), (1,))).astype(BF16)


def latent_query_kernel(latents, w_query1, query1_t):
    query1_t[...] = dot(w_query1[...], latents[...], ((0,), (1,))).astype(BF16)


def inner_kernel(
    masked,
    y_first,
    y_second,
    conv,
    far_key1,
    far_value1,
    far_query2,
    keys,
    values_t,
    query2_t,
    padded,
    mixed,
    w_key1,
    w_value1,
    w_query2,
    arrived,
):
    size_x, size_y, size_z, width = masked.shape
    head_size = width // HEADS
    cells = size_y * size_z
    weights = (w_key1, w_value1, w_query2)
    copies = [
        pltpu.make_async_copy(source, target, arrived.at[n])
        for n, (source, target) in enumerate(zip((far_key1, far_value1, far_query2), weights))
    ]
    for copy in copies:
        copy.start()

    def fill(i, carry):
        fill_row(padded, i, i, masked, y_first, y_second)
        return carry

    lax.fori_loop(0, size_x, fill, 0)
    values_t[:, head_size:, :] = jnp.ones_like(values_t[:, head_size:, :])
    stencil_plane(0, padded, conv, mixed, 0)
    for copy in copies:
        copy.wait()

    def plane(i, carry):
        project_plane((i - 1) * cells, i * cells, cells, mixed, weights, keys, values_t, query2_t)
        stencil_plane(i, padded, conv, mixed, i * cells)
        return carry

    lax.fori_loop(1, size_x - 2, plane, 0)
    last = size_x - 3
    project_plane(last * cells, (last + 1) * cells, cells, mixed, weights, keys, values_t, query2_t)


def score_weights(query_t, head, columns):
    head_size = LANES // 2
    factor = 1.8 / math.sqrt(head_size) * math.log2(math.e)
    scaled = query_t[head * head_size : (head + 1) * head_size, columns].astype(F32) * factor
    high = scaled.astype(BF16)
    low = (scaled - high.astype(F32)).astype(BF16)
    blank = jnp.zeros_like(high)
    if head % 2 == 0:
        return jnp.concatenate([high, blank, low, blank], axis=0)
    return jnp.concatenate([blank, high, blank, low], axis=0)


def chunks_of(pieces, axis, chunk):
    found = []
    base = 0
    for piece in pieces:
        for part in range(piece.shape[axis] // chunk):
            found.append((piece, part * chunk, base))
            base += chunk
    return found


def score_chunk(place, head, right, chunk, scores, top):
    piece, start, base = place
    pair = head // 2
    left = piece[start : start + chunk, pair * LANES : (pair + 1) * LANES]
    found = dot(jnp.concatenate([left, left], axis=1), right)
    scores[head % 2, base : base + chunk, :] = found
    largest = jnp.max(found.reshape(chunk // 8, 8, found.shape[1]), axis=0)
    return largest if top is None else jnp.maximum(top, largest)


def sum_chunk(place, head, chunk, scores, top, total):
    piece, start, base = place
    weights = jnp.exp2(scores[head % 2, base : base + chunk, :] - top).astype(BF16)
    found = dot(piece[head, :, start : start + chunk], weights)
    return found if total is None else total + found


def attention_loop(keys, query_t, values_t, scores, chunk, columns_of, finish):
    width = scores.shape[2]
    blocks = query_t.shape[1] // width
    key_chunks, value_chunks = chunks_of(keys, 0, chunk), chunks_of(values_t, 2, chunk)

    def overall(top):
        return jnp.max(top, axis=0, keepdims=True)

    def first(block):
        right = score_weights(query_t, 0, columns_of(block))
        top = None
        for place in key_chunks:
            top = score_chunk(place, 0, right, chunk, scores, top)
        return overall(top)

    def step(block, top):
        for head in range(HEADS):
            following = block if head + 1 < HEADS else jnp.minimum(block + 1, blocks - 1)
            ahead = (head + 1) % HEADS
            right = score_weights(query_t, ahead, columns_of(following))
            upcoming = total = None
            for key_place, value_place in zip(key_chunks, value_chunks):
                upcoming = score_chunk(key_place, ahead, right, chunk, scores, upcoming)
                total = sum_chunk(value_place, head, chunk, scores, top, total)
            finish(head, block, total, top)
            top = overall(upcoming)
        return top

    lax.fori_loop(0, blocks, step, first(0))


def split3(value):
    high = value.astype(BF16).astype(F32)
    rest = value - high
    middle = rest.astype(BF16).astype(F32)
    return high, middle, rest - middle


def stat_rows(top, total):
    return split3(top) + split3(total)[:2]


def read_kernel(
    masked,
    x_first,
    x_second,
    y_first,
    y_second,
    conv,
    w_key1,
    w_value1,
    w_query2,
    inner_keys,
    inner_values_t,
    query1_t,
    inner_query2_t,
    query2_t,
    kept,
    given,
    padded,
    mixed,
    keys,
    values_t,
    scores,
    stats,
):
    size_x, size_y, size_z, width = masked.shape
    head_size = width // HEADS
    cells = size_y * size_z
    last = size_x - 1
    for row, i in ((1, 0), (2, 1), (3, last - 1), (4, last)):
        fill_row(padded, row, i, masked, y_first, y_second)
    padded[5 * (1 - lax.axis_index("wx"))] = x_first[...].astype(F32)
    padded[5 * lax.axis_index("wx")] = x_second[...].astype(F32)
    values_t[:, head_size:, :] = jnp.ones_like(values_t[:, head_size:, :])
    stats[...] = jnp.zeros_like(stats)

    weights = (w_key1, w_value1, w_query2)
    stencil_plane(0, padded, conv, mixed, 0)
    project_plane(0, 0, cells, mixed, weights, keys, values_t, query2_t)
    stencil_plane(3, padded, conv, mixed, cells)
    project_plane(cells, last * cells, cells, mixed, weights, keys, values_t, query2_t)

    core = lax.axis_index("nc")
    per_half = kept.shape[0]
    span = scores.shape[2]

    def columns_of(block):
        return pl.ds(pl.multiple_of((block ^ (1 - core)) * span, span), span)

    def finish(head, block, total, top):
        rows = slice(head * head_size, (head + 1) * head_size)

        def write(target):
            for k in range(per_half):
                target[k, rows, :] = total[:head_size, k * LANES : (k + 1) * LANES].astype(BF16)

        pl.when(block == 1)(lambda: write(kept))
        pl.when(block == 0)(lambda: write(given))
        for slot, row in enumerate(stat_rows(top, total[head_size : head_size + 1])):
            stats[slot * HEADS + head : slot * HEADS + head + 1, columns_of(block)] = row

    attention_loop(
        [inner_keys, keys], query1_t, [inner_values_t, values_t], scores, 256, columns_of, finish
    )
    for target, side in ((kept, core), (given, 1 - core)):
        for k in range(per_half):
            columns = pl.ds(pl.multiple_of((side * per_half + k) * LANES, LANES), LANES)
            target[k, width:, :] = stats[:, columns].astype(BF16)


def merge_blocks(blocks):
    width = blocks[0].shape[0] - STAT_ROWS
    head_size = width // HEADS
    slots = [[block[width + n * HEADS : width + (n + 1) * HEADS] for n in range(5)] for block in blocks]
    tops = [s[0] + s[1] + s[2] for s in slots]
    top = functools.reduce(jnp.maximum, tops)
    factors = [jnp.exp2(t - top) for t in tops]
    total = sum(f * (s[3] + s[4]) for f, s in zip(factors, slots))
    sums = []
    for head in range(HEADS):
        rows = slice(head * head_size, (head + 1) * head_size)
        sums.append(sum(block[rows] * f[head : head + 1] for block, f in zip(blocks, factors)))
    return sums, top, total


def all_stats(top, total, size):
    rows = list(stat_rows(top, total))
    filler = jnp.zeros((size - len(rows) * HEADS,) + top.shape[1:], F32)
    return jnp.concatenate(rows + [filler], axis=0)


def merge_pair_kernel(kept, taken, *outs):
    for distance, out in enumerate(outs):
        index = lax.axis_index(("wx", "ny")) ^ distance
        sums, top, total = merge_blocks([ref[index].astype(F32) for ref in (kept, taken)])
        sums.append(all_stats(top, total, STAT_ROWS))
        out[...] = jnp.concatenate(sums, axis=0).astype(BF16)


def merge_group_kernel(count, *refs):
    blocks, outs, turned = refs[:count], refs[count:-1], refs[-1]
    sums, top, total = merge_blocks([ref[...].astype(F32) for ref in blocks])
    width = turned.shape[1] - LANES
    sums = jnp.concatenate(sums, axis=0)
    for k in range(width // LANES):
        lanes = slice(k * LANES, (k + 1) * LANES)
        turned[:, lanes] = sums[lanes].T
    turned[:, width:] = all_stats(top, total, LANES).T
    rows = outs[0].shape[0]
    for distance, out in enumerate(outs):
        index = lax.axis_index("wz") ^ distance
        out[...] = turned[pl.ds(pl.multiple_of(index * rows, rows), rows), :].astype(BF16)


def unpack_stats(tile):
    parts = [tile] + [pltpu.roll(tile, LANES - slot * HEADS, 1) for slot in range(1, 5)]
    return parts[0] + parts[1] + parts[2], parts[3] + parts[4]


def spread(per_head, pair):
    rows = per_head.shape[0]
    lane = lax.broadcasted_iota(jnp.int32, (rows, LANES), 1)
    left = jnp.broadcast_to(per_head[:, 2 * pair : 2 * pair + 1], (rows, LANES))
    right = jnp.broadcast_to(per_head[:, 2 * pair + 1 : 2 * pair + 2], (rows, LANES))
    return jnp.where(lane < LANES // 2, left, right)


def update_kernel(own, w_out1, *refs):
    parts, out = refs[:-1], refs[-1]
    width = own.shape[1]
    stats = [unpack_stats(part[:, width:].astype(F32)) for part in parts]
    top = functools.reduce(jnp.maximum, [t for t, _ in stats])
    factors = [jnp.exp2(t - top) for t, _ in stats]
    total = sum(f * l for f, (_, l) in zip(factors, stats))
    read = []
    for pair in range(width // LANES):
        lanes = slice(pair * LANES, (pair + 1) * LANES)
        value = sum(part[:, lanes].astype(F32) * spread(f, pair) for part, f in zip(parts, factors))
        read.append(value / spread(total, pair))
    read = jnp.concatenate(read, axis=1).astype(BF16)
    out[...] = (own[...].astype(F32) + dot(read, w_out1[...])).astype(BF16)


def join_kernel(*refs):
    parts, out = refs[:-1], refs[-1]
    rows = parts[0].shape[0]
    for k, part in enumerate(parts):
        out[k * rows : (k + 1) * rows, :] = part[...]


def join(parts, name):
    rows, width = parts[0].shape
    out = jax.ShapeDtypeStruct((len(parts) * rows, width), parts[0].dtype)
    return call(join_kernel, out, [], parts, 8, 1e6, name)


def write_kernel(
    own_state,
    other_state,
    query2_t,
    masked,
    w_key2,
    w_value2,
    w_out2,
    out,
    keys,
    values_t,
    scores,
    read_t,
    buffers,
    sent,
):
    half, width = own_state.shape
    head_size = width // HEADS
    values_t[:, head_size:, :] = jnp.ones_like(values_t[:, head_size:, :])
    for side, state in enumerate((own_state, other_state)):
        rows = slice(side * half, (side + 1) * half)
        keys[rows, :] = dot(state[...], w_key2[...]).astype(BF16)
        value_t = dot(w_value2[...], state[...], ((0,), (1,))).astype(BF16)
        values_t[:, :head_size, rows] = value_t.reshape(HEADS, head_size, half)
    span = scores.shape[2]
    blocks = out.shape[0] // span

    def send(block):
        slot = block % 2
        rows = pl.ds(pl.multiple_of(block * span, span), span)
        return pltpu.make_async_copy(buffers.at[slot], out.at[rows, :], sent.at[slot])

    def columns_of(block):
        return pl.ds(pl.multiple_of(block * span, span), span)

    def finish(head, block, total, top):
        rows = slice(head * head_size, (head + 1) * head_size)
        inverse = 1.0 / total[head_size : head_size + 1]
        read_t[rows, :] = (total[:head_size] * inverse).astype(BF16)
        if head == HEADS - 1:
            pl.when(block >= 2)(lambda: send(block - 2).wait())
            change = dot(read_t[...], w_out2[...], ((0,), (0,)))
            buffers[block % 2] = masked[columns_of(block), :].astype(F32) + change
            send(block).start()

    attention_loop([keys], query2_t, [values_t], scores, 256, columns_of, finish)
    for block in range(max(blocks - 2, 0), blocks):
        send(block).wait()


def call(kernel, shapes, scratch, operands, limit, flops, name, far=(), aliases=None, out_space=pltpu.VMEM):
    vmem = pl.BlockSpec(memory_space=pltpu.VMEM)
    hbm = pl.BlockSpec(memory_space=pltpu.HBM)
    many = isinstance(shapes, (list, tuple))
    in_specs = [hbm if n in far else vmem for n in range(len(operands))]
    moved = sum(x.size * x.dtype.itemsize for x in operands)
    result = pl.pallas_call(
        kernel,
        out_shape=shapes,
        in_specs=in_specs,
        out_specs=[vmem] * len(shapes) if many else pl.BlockSpec(memory_space=out_space),
        scratch_shapes=scratch,
        compiler_params=pltpu.CompilerParams(vmem_limit_bytes=limit * MIB),
        cost_estimate=pl.CostEstimate(flops=int(flops), bytes_accessed=moved, transcendentals=0),
        input_output_aliases=aliases or {},
        name=name,
    )(*operands)
    return list(result) if many else result


def pair_exchange(first, second, axis):
    count = lax.axis_size(axis)
    swaps = [[], []]
    for i in range(count - 1):
        swaps[i % 2] += [(i, i + 1), (i + 1, i)]
    other = lax.ppermute(second, axis, swaps[1])
    return lax.ppermute(first, axis, swaps[0]), other


def flipped(array, axis, distance):
    return lax.ppermute(array, axis, [(i, i ^ distance) for i in range(lax.axis_size(axis))])


def per_device(
    flow_field,
    fluid_mask,
    conv_weight,
    latents,
    w_query1,
    w_key1,
    w_value1,
    w_out1,
    w_query2,
    w_key2,
    w_value2,
    w_out2,
):
    size_x, size_y, size_z, width = flow_field.shape
    head_size = width // HEADS
    plane_cells = size_y * size_z
    inner_cells, outer_cells = (size_x - 2) * plane_cells, 2 * plane_cells
    cells = inner_cells + outer_cells
    latent_count = latents.shape[0]
    wide, narrow, group = ("wz", "wx"), ("ny", "nc"), ("wx", "ny")
    group_size = lax.axis_size(group)
    far = lax.axis_size("wz")
    core, member, layer = lax.axis_index("nc"), lax.axis_index(group), lax.axis_index("wz")
    block_size = latent_count // (2 * group_size)
    rows = block_size // far
    shape = jax.ShapeDtypeStruct
    step = 1e9

    side = shape((size_x, size_z, width), BF16)
    ends = pltpu.VMEM((size_x, 1, size_z, width), BF16)
    y_first, y_second = call(
        face_kernel,
        [side, side],
        [ends, ends, pltpu.VMEM(fluid_mask.shape, jnp.int32), pltpu.SemaphoreType.DMA((3,))],
        [flow_field, fluid_mask],
        56,
        step,
        "face",
        (0, 1),
    )
    y_first, y_second = pair_exchange(y_first, y_second, narrow)
    masked = call(
        prepare_kernel, shape(flow_field.shape, BF16), [], [flow_field, fluid_mask], 12, 2 * step, "prepare"
    )
    query1_t = call(
        latent_query_kernel,
        shape((width, latent_count), BF16),
        [],
        [latents, w_query1],
        12,
        2 * step,
        "latent_query",
    )
    side = shape((size_y + 2, size_z, width), BF16)
    x_first, x_second = call(
        edge_kernel, [side, side], [], [masked, y_first, y_second], 12, step, "edge"
    )
    x_first, x_second = pair_exchange(x_first, x_second, wide)
    weight = pltpu.VMEM((width, width), BF16)
    inner_keys, inner_values_t, query2_t = call(
        inner_kernel,
        [
            shape((inner_cells, width), BF16),
            shape((HEADS, head_size + ONES_ROWS, inner_cells), BF16),
            shape((width, cells), BF16),
        ],
        [
            pltpu.VMEM((size_x, size_y + 2, size_z, width), F32),
            pltpu.VMEM((inner_cells, width), BF16),
            weight,
            weight,
            weight,
            pltpu.SemaphoreType.DMA((3,)),
        ],
        [masked, y_first, y_second, conv_weight, w_key1, w_value1, w_query2],
        28,
        10 * step,
        "inner",
        (4, 5, 6),
    )
    query2_t, kept, given = call(
        read_kernel,
        [shape((width, cells), BF16)] + [shape((group_size, width + STAT_ROWS, LANES), BF16)] * 2,
        [
            pltpu.VMEM((6, size_y + 2, size_z, width), F32),
            pltpu.VMEM((outer_cells, width), BF16),
            pltpu.VMEM((outer_cells, width), BF16),
            pltpu.VMEM((HEADS, head_size + ONES_ROWS, outer_cells), BF16),
            pltpu.VMEM((2, cells, latent_count // 2), F32),
            pltpu.VMEM((STAT_ROWS, latent_count), F32),
        ],
        [
            masked,
            x_first,
            x_second,
            y_first,
            y_second,
            conv_weight,
            w_key1,
            w_value1,
            w_query2,
            inner_keys,
            inner_values_t,
            query1_t,
            query2_t,
        ],
        32,
        20 * step,
        "read",
        (),
        {12: 0},
    )
    taken = flipped(given, "nc", 1)
    block = shape((width + STAT_ROWS, LANES), BF16)
    blocks = call(merge_pair_kernel, [block] * group_size, [], [kept, taken], 16, step, "merge_pair")
    blocks = [flipped(blocks[d], group, d) for d in range(group_size - 1, 0, -1)] + blocks[:1]
    parts = call(
        functools.partial(merge_group_kernel, group_size),
        [shape((rows, width + LANES), BF16)] * far,
        [pltpu.VMEM((block_size, width + LANES), F32)],
        blocks,
        16,
        step,
        "merge_group",
    )
    order = list(range(far - 2, 0, -1)) + [far - 1]
    parts = [flipped(parts[d], "wz", d) for d in order] + parts[:1]
    start = ((core * group_size + member) * far + layer) * rows
    own = lax.dynamic_slice_in_dim(latents, start, rows, 0)
    state = call(update_kernel, shape((rows, width), BF16), [], [own, w_out1] + parts, 16, step, "update")
    state = join([flipped(state, "wz", d) for d in range(far - 1, 0, -1)] + [state], "join_far")
    state = join([flipped(state, group, d) for d in range(group_size - 1, 0, -1)] + [state], "join_group")
    other = flipped(state, "nc", 1)
    span = 2 * plane_cells

    result = call(
        write_kernel,
        shape((cells, width), F32),
        [
            pltpu.VMEM((latent_count, width), BF16),
            pltpu.VMEM((HEADS, head_size + ONES_ROWS, latent_count), BF16),
            pltpu.VMEM((2, latent_count, span), F32),
            pltpu.VMEM((width, span), BF16),
            pltpu.VMEM((2, span, width), F32),
            pltpu.SemaphoreType.DMA((2,)),
        ],
        [state, other, query2_t, masked.reshape(cells, width), w_key2, w_value2, w_out2],
        32,
        20 * step,
        "write",
        out_space=pltpu.HBM,
    )
    return result.reshape(size_x, size_y, size_z, width)


def solution(mesh):
    wide, narrow = (mesh.shape[name] for name in ("wide", "narrow"))
    grid = Mesh(mesh.devices.reshape(wide // 2, 2, narrow // 2, 2), ("wz", "wx", "ny", "nc"))
    split = P(("wz", "wx"), ("ny", "nc"))
    return jax.shard_map(
        per_device,
        mesh=grid,
        in_specs=(split, split) + (P(),) * 10,
        out_specs=split,
        check_vma=False,
    )
```
